32 devices in a mesh: fsdp: 32 (over z, y, x, core).
Axes of the slice: x: 2, y: 2, z: 4, core: 2. Of those that a mesh axis runs over, the one named last changes fastest.
Arguments:
- tokens: bfloat16 [64, 128, 2048], P(None, 'fsdp'), may hold values from -6 to 6
- lengths: int32 [64], replicated, may hold values from 1 to 128, 6144 in all
- dealing: int32 [64], replicated, may hold values from 0 to 63, each once
- w_query: bfloat16 [2048, 2048], P('fsdp'), may hold values from -0.125 to 0.125
- w_key: bfloat16 [2048, 2048], P('fsdp'), may hold values from -0.125 to 0.125
- w_value: bfloat16 [2048, 2048], P('fsdp'), may hold values from -0.125 to 0.125
- w_output: bfloat16 [2048, 2048], P('fsdp'), may hold values from -0.125 to 0.125
- query_gain: bfloat16 [2048], P('fsdp'), may hold values from 1 to 2.5
- key_gain: bfloat16 [2048], P('fsdp'), may hold values from 1 to 2.5
- attn_gain: bfloat16 [2048], P('fsdp'), may hold values from 0.099609375 to 1.8984375
- w_gate: bfloat16 [2048, 8192], P(None, 'fsdp'), may hold values from -0.125 to 0.125
- w_up: bfloat16 [2048, 8192], P(None, 'fsdp'), may hold values from -0.125 to 0.125
- w_down: bfloat16 [8192, 2048], P('fsdp'), may hold values from -0.0625 to 0.0625
- mlp_gain: bfloat16 [2048], P('fsdp'), may hold values from 0.099609375 to 1.8984375
- cotangent: bfloat16 [64, 128, 2048], P('fsdp'), may hold values from -6 to 6
Outputs:
- block_out: bfloat16 [64, 128, 2048], P('fsdp')
- input_grad: bfloat16 [64, 128, 2048], P(None, 'fsdp')
- w_query_grad: float32 [2048, 2048], P('fsdp')
- w_key_grad: float32 [2048, 2048], P('fsdp')
- w_value_grad: float32 [2048, 2048], P('fsdp')
- w_output_grad: float32 [2048, 2048], P('fsdp')
- query_gain_grad: float32 [2048], P('fsdp')
- key_gain_grad: float32 [2048], P('fsdp')
- attn_gain_grad: float32 [2048], P('fsdp')
- w_gate_grad: float32 [2048, 8192], P(None, 'fsdp')
- w_up_grad: float32 [2048, 8192], P(None, 'fsdp')
- w_down_grad: float32 [8192, 2048], P('fsdp')
- mlp_gain_grad: float32 [2048], P('fsdp')
The draws below stay inside these ranges and needn't reach their ends.
Inputs may be any that keep to these rules, and one draw needn't show every extreme that they name: `lengths`: the longest sequence has exactly 128 used slots. `dealing`: each sequence number appears once.
All inputs are finite; a program needn't handle non-finite values.
Results may differ from the reference program's by a relative error of at most 0.017.
Values may be sent and summed in bfloat16 or wider, within the bound.
No kernel may reach another device: no remote copies, remote signals or barrier semaphores. Data moves between devices by JAX's collectives and lax.ppermute only.
A program may use at most 512 MiB of HBM per device.

```python
import math
import jax
import jax.numpy as jnp
import numpy as np
from jax import lax

D = 2048
HEADS = 16
FF = 8192
SEQ_LEN = 128
NSEQ = 64


def steps_of(own_key, extent, cuts, low, largest):
    factor_of, own = 1.0, jax.random.fold_in(own_key, 6)
    for dim, parts in cuts:
        heights = jnp.exp(jax.random.uniform(jax.random.fold_in(own, dim), (parts,), jnp.float32, low / len(cuts), largest / len(cuts)))
        factor_of = factor_of * jnp.repeat(heights, extent[dim] // parts).reshape([-1 if axis == dim else 1 for axis in range(len(extent))])
    return factor_of


def length_profile(amount, total, limit, slope):
    weights = [(1 << 20) // math.isqrt(rank ** slope) + 1 for rank in range(2, amount + 1)]
    spare, given = total - limit - (amount - 1), [1] * (amount - 1)
    while spare > 0:
        movable = [i for i in range(amount - 1) if given[i] < limit]
        pool, remaining = sum([weights[i] for i in movable]), spare
        for i in movable:
            addition = min(limit - given[i], max(1, remaining * weights[i] // pool), spare)
            given[i] = given[i] + addition
            spare = spare - addition
    return np.array([limit] + given)


def ragged(key, amount, total, reach, lean):
    if amount == 2:
        one = jax.random.randint(key, (), max(1, total - reach), min(reach, total - 1) + 1)
        return jnp.stack([one, total - one])
    sizes = jnp.asarray(length_profile(amount, total, reach, lean), jnp.int32)
    pairs = (amount - 1) // 2
    giver, sink = sizes[1:1 + 2 * pairs:2], sizes[2:2 + 2 * pairs:2]
    slack = jnp.minimum(giver - 1, reach - sink)
    passed = jax.random.randint(jax.random.fold_in(key, 1), (pairs,), 0, 1 << 20) % (slack + 1)
    sizes = sizes.at[1:1 + 2 * pairs:2].set(giver - passed).at[2:2 + 2 * pairs:2].set(sink + passed)
    return sizes[jax.random.permutation(jax.random.fold_in(key, 2), amount)]


def gaussian(key, dims, spread, reach, split=(), kind=jnp.bfloat16):
    drawn = spread * jax.random.normal(key, dims, jnp.float32)
    if split:
        drawn = drawn * steps_of(key, dims, split, -0.22, 0.18)
    return jnp.clip(drawn, -reach, reach).astype(kind)


def setup_inputs(seed: int = 0) -> dict:
    key_of = jax.random.split(jax.random.key(seed), 16)
    tokens = gaussian(key_of[0], (NSEQ, SEQ_LEN, D), 1.0, 6.0, ((1, 32),))
    lengths = ragged(key_of[1], NSEQ, NSEQ * SEQ_LEN * 3 // 4, SEQ_LEN, 0).astype(jnp.int32)
    dealing = jax.random.permutation(key_of[2], NSEQ).astype(jnp.int32)
    w_query = gaussian(key_of[3], (D, D), D ** -0.5, 0.125, ((0, 32),))
    w_key = gaussian(key_of[4], (D, D), D ** -0.5, 0.125, ((0, 32),))
    w_value = gaussian(key_of[5], (D, D), D ** -0.5, 0.125, ((0, 32),))
    w_output = gaussian(key_of[6], (D, D), D ** -0.5, 0.125, ((0, 32),))
    query_gain = jnp.clip(jnp.exp(math.log(2.5) - 0.916290732 * jax.random.uniform(key_of[7], (D,), jnp.float32) ** steps_of(key_of[7], (D,), ((0, 32),), -0.2, 0.2)), 1.0, 2.5).astype(jnp.bfloat16)
    key_gain = jnp.clip(jnp.exp(math.log(2.5) - 0.916290732 * jax.random.uniform(key_of[8], (D,), jnp.float32) ** steps_of(key_of[8], (D,), ((0, 32),), -0.2, 0.2)), 1.0, 2.5).astype(jnp.bfloat16)
    attn_gain = jnp.clip(1.0 + 0.18 * jax.random.normal(key_of[9], (D,), jnp.float32), 0.099609375, 1.8984375).astype(jnp.bfloat16)
    w_gate = gaussian(key_of[10], (D, FF), D ** -0.5, 0.125, ((1, 32),))
    w_up = gaussian(key_of[11], (D, FF), D ** -0.5, 0.125, ((1, 32),))
    w_down = gaussian(key_of[12], (FF, D), FF ** -0.5, 0.0625, ((0, 32),))
    mlp_gain = jnp.clip(1.0 + 0.18 * jax.random.normal(key_of[13], (D,), jnp.float32), 0.099609375, 1.8984375).astype(jnp.bfloat16)
    cotangent = gaussian(key_of[14], (NSEQ, SEQ_LEN, D), 1.0, 6.0, ((0, 32),))
    return dict(tokens=tokens, lengths=lengths, dealing=dealing, w_query=w_query, w_key=w_key, w_value=w_value, w_output=w_output, query_gain=query_gain, key_gain=key_gain, attn_gain=attn_gain, w_gate=w_gate, w_up=w_up, w_down=w_down, mlp_gain=mlp_gain, cotangent=cotangent)


norm_eps = 1e-06
rope_base = 500000.0
highest = lax.Precision.HIGHEST

@jax.custom_vjp
def low(v):
    return lax.optimization_barrier(v.astype(jnp.bfloat16)).astype(jnp.float32)

@jax.custom_vjp
def low_back(v):
    return v

def low_keep(v):
    return (low(v), None)

def low_pass(kept, grad):
    return (grad,)

def back_keep(v):
    return (v, None)

def back_low(kept, grad):
    return (low(grad),)
low.defvjp(low_keep, low_pass)
low_back.defvjp(back_keep, back_low)

def rotary_tables(length, head_dim):
    half_dim = head_dim // 2
    exponents = jnp.arange(half_dim, dtype=jnp.float32) * (2.0 / head_dim)
    frequency = jnp.power(jnp.float32(rope_base), -exponents)
    angles = jnp.arange(length, dtype=jnp.float32)[:, None] * frequency[None, :]
    return (jnp.cos(angles), jnp.sin(angles))

def rotate(values, cosines, sines):
    half_dim = values.shape[-1] // 2
    first_half = values[..., :half_dim]
    second_half = values[..., half_dim:]
    cos_rows = cosines[:, None, :]
    sin_rows = sines[:, None, :]
    return jnp.concatenate([first_half * cos_rows - second_half * sin_rows, second_half * cos_rows + first_half * sin_rows], axis=-1)

def rms_norm(values, gain_vec):
    return values * lax.rsqrt(lax.optimization_barrier(jnp.mean(values * values, axis=-1, keepdims=True)) + norm_eps) * gain_vec

def project(left_side, right_side):
    return jnp.einsum('gtd,de->gte', left_side, right_side, precision=highest)

def layer(x_block, valid_mask, w_query, w_key, w_value, w_output, query_gain, key_gain, attn_gain, w_gate, w_up, w_down, mlp_gain):
    blocks_here, seq_len, model_width = x_block.shape
    head_dim = model_width // HEADS
    cosines, sines = rotary_tables(seq_len, head_dim)
    query_raw = low_back(project(x_block, w_query))
    key_raw = low_back(project(x_block, w_key))
    value_raw = low_back(project(x_block, w_value))
    query_low = low(rotate(rms_norm(query_raw, query_gain).reshape(blocks_here, seq_len, HEADS, head_dim), cosines, sines))
    key_low = low(rotate(rms_norm(key_raw, key_gain).reshape(blocks_here, seq_len, HEADS, head_dim), cosines, sines))
    value_low = low(value_raw).reshape(blocks_here, seq_len, HEADS, head_dim)
    scores = low_back(jnp.einsum('gthe,guhe->ghtu', query_low, key_low, precision=highest) * (1.0 / math.sqrt(head_dim)))
    positions = jnp.arange(seq_len, dtype=jnp.int32)
    causal = positions[None, :] <= positions[:, None]
    scores = jnp.where(causal, scores, -1e+30)
    row_peak = lax.optimization_barrier(jnp.max(scores, axis=-1, keepdims=True))
    exp_scores = jnp.exp(scores - row_peak)
    soft_weights = exp_scores / lax.optimization_barrier(jnp.sum(exp_scores, axis=-1, keepdims=True))
    attended = jnp.einsum('ghtu,guhe->gthe', low(soft_weights), value_low, precision=highest).reshape(blocks_here, seq_len, model_width)
    attended = low(low_back(attended))
    out_raw = low_back(project(attended, w_output))
    hidden = x_block + rms_norm(out_raw, attn_gain)
    hidden_low = low(hidden)
    gate_proj = low_back(project(hidden_low, w_gate))
    up_proj = low_back(project(hidden_low, w_up))
    act_low = low(jax.nn.silu(gate_proj) * up_proj)
    down_proj = low_back(jnp.einsum('gtf,fd->gtd', act_low, w_down, precision=highest))
    return valid_mask * (hidden + rms_norm(down_proj, mlp_gain))

def reference(tokens, lengths, dealing, w_query, w_key, w_value, w_output, query_gain, key_gain, attn_gain, w_gate, w_up, w_down, mlp_gain, cotangent):
    weights = tuple((weight_arg.astype(jnp.float32) for weight_arg in (w_query, w_key, w_value, w_output, query_gain, key_gain, attn_gain, w_gate, w_up, w_down, mlp_gain)))
    seq_len = tokens.shape[1]
    model_width = tokens.shape[2]
    dealt_tokens = jnp.take(tokens, dealing, axis=0).astype(jnp.float32)
    dealt_lengths = jnp.take(lengths, dealing)
    positions = jnp.arange(seq_len, dtype=jnp.int32)
    valid_all = (positions[None, :] < dealt_lengths[:, None]).astype(jnp.float32)[..., None]
    per_block = math.gcd(NSEQ, max(1, 4096 // SEQ_LEN))
    blocks = NSEQ // per_block
    scanned = (dealt_tokens.reshape(blocks, per_block, seq_len, model_width), valid_all.reshape(blocks, per_block, seq_len, 1), cotangent.astype(jnp.float32).reshape(blocks, per_block, seq_len, model_width))

    def one_block(totals_in, inputs):
        x_block, valid_mask, cot_block = inputs

        def forward(x_value, *weight_vals):
            return layer(x_value, valid_mask, *weight_vals)
        result, pullback = jax.vjp(forward, x_block, *weights)
        gradients = pullback(cot_block)
        summed = tuple((running + grad_one for running, grad_one in zip(totals_in, gradients[1:])))
        return (summed, (result.astype(jnp.bfloat16), gradients[0].astype(jnp.bfloat16)))
    initial = tuple((jnp.zeros_like(weight_one) for weight_one in weights))
    totals, (block_outs, dealt_grads) = lax.scan(one_block, initial, scanned)
    block_out = block_outs.reshape(NSEQ, seq_len, model_width)
    input_grad = jnp.zeros(tokens.shape, jnp.bfloat16).at[dealing].set(dealt_grads.reshape(NSEQ, seq_len, model_width))
    return (block_out, input_grad, totals[0], totals[1], totals[2], totals[3], totals[4], totals[5], totals[6], totals[7], totals[8], totals[9], totals[10])
```

```python
import math

import jax
import jax.numpy as jnp
from jax import lax
from jax.sharding import Mesh
from jax.sharding import PartitionSpec as P

HEADS = 16
PLANE = 8
BF = jnp.bfloat16
F32 = jnp.float32

norm_eps = 1e-06
rope_base = 500000.0

ALL = ("a", "y", "x", "c")
GROUP = ("y", "x", "c")
SWAP = [(0, 1), (1, 0)]


def swap(value, axis):
    return lax.ppermute(value, axis, SWAP)


def rotary_tables(length, head_dim):
    half_dim = head_dim // 2
    exponents = jnp.arange(half_dim, dtype=F32) * (2.0 / head_dim)
    frequency = jnp.power(F32(rope_base), -exponents)
    angles = jnp.arange(length, dtype=F32)[:, None] * frequency[None, :]
    return (jnp.cos(angles), jnp.sin(angles))


def rotate(values, cosines, sines):
    half_dim = values.shape[-1] // 2
    first_half = values[..., :half_dim]
    second_half = values[..., half_dim:]
    cos_rows = cosines[:, None, :]
    sin_rows = sines[:, None, :]
    return jnp.concatenate(
        [
            first_half * cos_rows - second_half * sin_rows,
            second_half * cos_rows + first_half * sin_rows,
        ],
        axis=-1,
    )


def group_gather(block):
    half = block.shape[0] // 2
    low, high = block[:half], block[half:]
    low_x = swap(low, "x")
    high_y = swap(high, "y")
    low_y, low_xy = swap(low, "y"), swap(low_x, "y")
    high_x, high_xy = swap(high, "x"), swap(high_y, "x")
    pieces = [
        (low, high),
        (low_x, high_x),
        (low_y, high_y),
        (low_xy, high_xy),
    ]
    out = []
    for first, second in pieces:
        out += [first, second, swap(first, "c"), swap(second, "c")]
    return jnp.concatenate(out, axis=0)


def group_scatter(partial):
    rows = partial.shape[0] // PLANE
    half = rows // 2
    low, high = [], []
    for place in range(4):
        base = partial[2 * place * rows : (2 * place + 1) * rows]
        away = swap(partial[(2 * place + 1) * rows : (2 * place + 2) * rows], "c")
        both = base.astype(F32) + away.astype(F32)
        low.append(both[:half])
        high.append(both[half:])
    low0 = low[0] + swap(low[2].astype(BF), "y").astype(F32)
    low1 = low[1] + swap(low[3].astype(BF), "y").astype(F32)
    low_sum = low0 + swap(low1.astype(BF), "x").astype(F32)
    high0 = high[0] + swap(high[1].astype(BF), "x").astype(F32)
    high1 = high[2] + swap(high[3].astype(BF), "x").astype(F32)
    high_sum = high0 + swap(high1.astype(BF), "y").astype(F32)
    return jnp.concatenate([low_sum, high_sum], axis=0)


def group_total(value):
    kinds, wide = value.shape
    split = value.reshape(kinds, 2, 2, 2, wide // PLANE)
    for axis, dim in (("c", 3), ("x", 2), ("y", 1)):
        split = split + jnp.flip(swap(split, axis), dim)
    return split.reshape(kinds, wide)


def per_device(
    tokens,
    lengths,
    dealing,
    w_query,
    w_key,
    w_value,
    w_output,
    query_gain,
    key_gain,
    attn_gain,
    w_gate,
    w_up,
    w_down,
    mlp_gain,
    cotangent,
):
    groups = lax.axis_size("a")
    total = groups * PLANE
    rank = lax.axis_index(ALL)
    place = lax.axis_index(GROUP)
    micro_count, seq_len, width = cotangent.shape
    rows = micro_count * seq_len
    wide = rows * PLANE
    shard = width // total
    head_dim = width // HEADS
    own_heads = HEADS // PLANE
    own_width = own_heads * head_dim
    spread = head_dim // shard
    head_axes = GROUP[3 - (spread.bit_length() - 1) :]
    fan = PLANE // spread
    lead, lane = place // spread, place % spread

    cosines, sines = rotary_tables(seq_len, head_dim)
    positions = jnp.arange(seq_len, dtype=jnp.int32)
    causal = (positions[None, :] <= positions[:, None])[None, None]
    qk_scale = 1.0 / math.sqrt(head_dim)

    def heads_out(weight):
        split = weight.reshape(shard, spread, own_heads, fan, head_dim)
        return split.transpose(3, 1, 0, 2, 4).reshape(PLANE, shard, own_width)

    outgoing = jnp.take(tokens, dealing, axis=0)
    arrived = lax.all_to_all(outgoing, ALL, split_axis=0, concat_axis=1, tiled=True)
    x_low = arrived.reshape(rows, width)

    qkv_out = jnp.concatenate([heads_out(w_query), heads_out(w_key), heads_out(w_value)], axis=2)
    qkv_in = lax.all_to_all(qkv_out, GROUP, split_axis=0, concat_axis=0, tiled=True)
    w_qkv = lax.all_gather(qkv_in, "a", axis=0, tiled=True).reshape(width, 3 * own_width)

    gains = jnp.stack([query_gain, key_gain, attn_gain, mlp_gain])
    gains = lax.all_to_all(
        jnp.broadcast_to(gains[None], (total, 4, shard)), ALL, split_axis=0, concat_axis=0, tiled=True
    )
    gains = gains.transpose(1, 0, 2).reshape(4, width).astype(F32)
    by_head = gains[:2].reshape(2, spread, own_heads, fan, head_dim)
    by_head = lax.dynamic_index_in_dim(by_head, lane, 1, keepdims=False)
    by_head = lax.dynamic_index_in_dim(by_head, lead, 2, keepdims=False)
    gain_query, gain_key = by_head[0].reshape(own_width), by_head[1].reshape(own_width)
    gain_attn, gain_mlp = gains[2], gains[3]

    out_all = lax.all_gather(w_output, "a", axis=0, tiled=False)
    w_out = lax.all_to_all(out_all, head_axes, split_axis=0, concat_axis=1, tiled=True)
    w_out = w_out.reshape(own_width, width)

    gate = lax.all_gather(w_gate.T, "a", axis=0, tiled=True)
    up = lax.all_gather(w_up.T, "a", axis=0, tiled=True)
    down = lax.all_gather(w_down, "a", axis=0, tiled=True)

    own_seqs = lax.dynamic_slice_in_dim(dealing, rank * micro_count, micro_count)
    own_lengths = jnp.take(lengths, own_seqs)
    valid_mask = (positions[None, :] < own_lengths[:, None]).astype(F32).reshape(rows, 1)

    x_wide = group_gather(x_low)
    qkv_raw = jnp.dot(x_wide, w_qkv, preferred_element_type=F32)
    query_raw = qkv_raw[:, :own_width]
    key_raw = qkv_raw[:, own_width : 2 * own_width]
    value_low = qkv_raw[:, 2 * own_width :].astype(BF)
    squares = group_total(
        jnp.stack([jnp.sum(query_raw * query_raw, axis=1), jnp.sum(key_raw * key_raw, axis=1)])
    )
    inverses = lax.rsqrt(squares * (1.0 / width) + norm_eps)
    query_inv, key_inv = inverses[0][:, None], inverses[1][:, None]
    head_shape = (wide // seq_len, seq_len, own_heads, head_dim)
    query_low = rotate((query_raw * query_inv * gain_query).reshape(head_shape), cosines, sines).astype(BF)
    key_low = rotate((key_raw * key_inv * gain_key).reshape(head_shape), cosines, sines).astype(BF)
    value_low = value_low.reshape(head_shape)
    scores = jnp.einsum("gthe,guhe->ghtu", query_low, key_low, preferred_element_type=F32) * qk_scale
    scores = jnp.where(causal, scores, -1e30)
    row_peak = jnp.max(scores, axis=-1, keepdims=True)
    exp_scores = jnp.exp(scores - row_peak)
    row_total = jnp.sum(exp_scores, axis=-1, keepdims=True)
    soft = exp_scores / row_total
    soft_low = soft.astype(BF)
    attended_low = (
        jnp.einsum("ghtu,guhe->gthe", soft_low, value_low, preferred_element_type=F32)
        .reshape(wide, own_width)
        .astype(BF)
    )
    out_raw = group_scatter(jnp.dot(attended_low, w_out, preferred_element_type=F32).astype(BF))
    out_inv = lax.rsqrt(jnp.mean(out_raw * out_raw, axis=-1, keepdims=True) + norm_eps)
    out_normed = out_raw * out_inv
    hidden = x_low.astype(F32) + out_normed * gain_attn

    hidden_wide = group_gather(hidden.astype(BF))
    contract_last = (((1,), (1,)), ((), ()))
    contract_rows = (((0,), (0,)), ((), ()))
    gate_proj = lax.dot_general(hidden_wide, gate, contract_last, preferred_element_type=F32)
    up_proj = lax.dot_general(hidden_wide, up, contract_last, preferred_element_type=F32)
    sigma_gate = jax.nn.sigmoid(gate_proj)
    act_value = gate_proj * sigma_gate
    act_low = (act_value * up_proj).astype(BF)
    down_raw = group_scatter(jnp.dot(act_low, down, preferred_element_type=F32).astype(BF))
    down_inv = lax.rsqrt(jnp.mean(down_raw * down_raw, axis=-1, keepdims=True) + norm_eps)
    down_normed = down_raw * down_inv
    block_out = (
        (valid_mask * (hidden + down_normed * gain_mlp)).astype(BF).reshape(micro_count, seq_len, width)
    )

    grad_out = valid_mask * cotangent.reshape(rows, width).astype(F32)
    grad_gain_mlp = jnp.sum(down_normed * grad_out, axis=0)
    scaled = grad_out * gain_mlp
    grad_down = down_inv * (scaled - down_normed * jnp.mean(scaled * down_normed, axis=-1, keepdims=True))
    grad_down_wide = group_gather(grad_down.astype(BF))

    grad_act = lax.dot_general(grad_down_wide, down, contract_last, preferred_element_type=F32)
    grad_gate_low = (grad_act * up_proj * sigma_gate * (1.0 + gate_proj * (1.0 - sigma_gate))).astype(BF)
    grad_up_low = (grad_act * act_value).astype(BF)
    grad_hidden = jnp.dot(grad_gate_low, gate, preferred_element_type=F32) + jnp.dot(
        grad_up_low, up, preferred_element_type=F32
    )
    grad_hidden = grad_out + group_scatter(grad_hidden.astype(BF))

    def owners(term):
        return lax.psum_scatter(term.astype(BF), "a", scatter_dimension=0, tiled=True).astype(F32)

    down_part = owners(
        lax.dot_general(act_low, grad_down_wide, contract_rows, preferred_element_type=F32)
    )
    gate_part = owners(
        lax.dot_general(grad_gate_low, hidden_wide, contract_rows, preferred_element_type=F32)
    ).T
    up_part = owners(
        lax.dot_general(grad_up_low, hidden_wide, contract_rows, preferred_element_type=F32)
    ).T

    grad_gain_attn = jnp.sum(out_normed * grad_hidden, axis=0)
    scaled = grad_hidden * gain_attn
    grad_out_raw = out_inv * (scaled - out_normed * jnp.mean(scaled * out_normed, axis=-1, keepdims=True))
    grad_out_wide = group_gather(grad_out_raw.astype(BF))

    output_term = lax.dot_general(attended_low, grad_out_wide, contract_rows, preferred_element_type=F32)
    output_term = lax.all_to_all(
        output_term.astype(BF).reshape(own_heads, head_dim, width),
        head_axes,
        split_axis=1,
        concat_axis=0,
        tiled=True,
    )
    output_part = owners(output_term.reshape(groups * shard, width))

    grad_att_low = (
        lax.dot_general(grad_out_wide, w_out, contract_last, preferred_element_type=F32)
        .astype(BF)
        .reshape(head_shape)
    )
    grad_soft = jnp.einsum("gthe,guhe->ghtu", grad_att_low, value_low, preferred_element_type=F32)
    row_delta = jnp.sum(soft * grad_soft, axis=-1, keepdims=True)
    grad_scores = (soft * (grad_soft - row_delta)).astype(BF)
    grad_q_rot = (
        jnp.einsum("ghtu,guhe->gthe", grad_scores, key_low, preferred_element_type=F32) * qk_scale
    )
    grad_k_rot = (
        jnp.einsum("ghtu,gthe->guhe", grad_scores, query_low, preferred_element_type=F32) * qk_scale
    )
    grad_value_low = (
        jnp.einsum("ghtu,gthe->guhe", soft_low, grad_att_low, preferred_element_type=F32)
        .reshape(wide, own_width)
        .astype(BF)
    )
    grad_q_norm = rotate(grad_q_rot, cosines, -sines).reshape(wide, own_width)
    grad_k_norm = rotate(grad_k_rot, cosines, -sines).reshape(wide, own_width)
    query_normed, key_normed = query_raw * query_inv, key_raw * key_inv
    grad_gain_q = jnp.sum(query_normed * grad_q_norm, axis=0)
    grad_gain_k = jnp.sum(key_normed * grad_k_norm, axis=0)
    scaled_q, scaled_k = grad_q_norm * gain_query, grad_k_norm * gain_key
    means = group_total(
        jnp.stack([jnp.sum(scaled_q * query_normed, axis=1), jnp.sum(scaled_k * key_normed, axis=1)])
    ) * (1.0 / width)
    grad_query = query_inv * (scaled_q - query_normed * means[0][:, None])
    grad_key = key_inv * (scaled_k - key_normed * means[1][:, None])
    grad_qkv = jnp.concatenate([grad_query.astype(BF), grad_key.astype(BF), grad_value_low], axis=1)

    grad_input = lax.dot_general(grad_qkv, w_qkv, contract_last, preferred_element_type=F32)
    grad_input = grad_hidden + group_scatter(grad_input.astype(BF))
    returned = lax.all_to_all(
        grad_input.astype(BF).reshape(micro_count, seq_len, width),
        ALL,
        split_axis=1,
        concat_axis=0,
        tiled=True,
    )
    input_grad = jnp.zeros_like(tokens).at[dealing].set(returned)

    qkv_term = lax.dot_general(x_wide, grad_qkv, contract_rows, preferred_element_type=F32)
    qkv_rows = lax.psum_scatter(qkv_term.astype(BF), "a", scatter_dimension=0, tiled=True)
    qkv_back = lax.all_to_all(
        qkv_rows.reshape(PLANE, shard, 3 * own_width), GROUP, split_axis=0, concat_axis=0, tiled=True
    )

    def heads_in(columns):
        split = columns.reshape(fan, spread, shard, own_heads, head_dim)
        return split.transpose(2, 1, 3, 0, 4).reshape(shard, width).astype(F32)

    query_part = heads_in(qkv_back[:, :, :own_width])
    key_part = heads_in(qkv_back[:, :, own_width : 2 * own_width])
    value_part = heads_in(qkv_back[:, :, 2 * own_width :])

    placed = jnp.zeros((2, spread, own_heads, fan, head_dim), F32)
    own = jnp.stack([grad_gain_q, grad_gain_k]).reshape(2, 1, own_heads, 1, head_dim)
    placed = lax.dynamic_update_slice(placed, own, (0, lane, 0, lead, 0)).reshape(2, width)
    gain_terms = jnp.concatenate([placed, jnp.stack([grad_gain_attn, grad_gain_mlp])])
    gain_terms = gain_terms.reshape(4, total, shard).transpose(1, 0, 2)
    gain_part = jnp.sum(
        lax.all_to_all(gain_terms, ALL, split_axis=0, concat_axis=0, tiled=True), axis=0
    )
    return (
        block_out,
        input_grad,
        query_part,
        key_part,
        value_part,
        output_part,
        gain_part[0],
        gain_part[1],
        gain_part[2],
        gate_part,
        up_part,
        down_part,
        gain_part[3],
    )


def solution(mesh):
    count = mesh.devices.size
    inner = Mesh(mesh.devices.reshape(count // PLANE, 2, 2, 2), ALL)
    first, second = P(ALL, None), P(None, ALL)
    vector = P(ALL)
    placed = (
        P(None, ALL, None),
        P(),
        P(),
        first,
        first,
        first,
        first,
        vector,
        vector,
        vector,
        second,
        second,
        first,
        vector,
        P(ALL, None, None),
    )
    return jax.shard_map(
        per_device,
        mesh=inner,
        in_specs=placed,
        out_specs=(
            P(ALL, None, None),
            P(None, ALL, None),
            first,
            first,
            first,
            first,
            vector,
            vector,
            vector,
            second,
            second,
            first,
            vector,
        ),
        check_vma=False,
    )
```

```python
import math

import jax
import jax.numpy as jnp
from jax import lax
from jax.sharding import Mesh
from jax.sharding import PartitionSpec as P

HEADS = 16
PLANE = 8
BF = jnp.bfloat16
F32 = jnp.float32

norm_eps = 1e-06
rope_base = 500000.0

ALL = ("a", "y", "x", "c")
GROUP = ("y", "x", "c")
SWAP = [(0, 1), (1, 0)]


def swap(value, axis):
    return lax.ppermute(value, axis, SWAP)


def rotary_tables(length, head_dim):
    half_dim = head_dim // 2
    exponents = jnp.arange(half_dim, dtype=F32) * (2.0 / head_dim)
    frequency = jnp.power(F32(rope_base), -exponents)
    angles = jnp.arange(length, dtype=F32)[:, None] * frequency[None, :]
    return (jnp.cos(angles), jnp.sin(angles))


def rotate(values, cosines, sines):
    half_dim = values.shape[-1] // 2
    first_half = values[..., :half_dim]
    second_half = values[..., half_dim:]
    cos_rows = cosines[:, None, :]
    sin_rows = sines[:, None, :]
    return jnp.concatenate(
        [
            first_half * cos_rows - second_half * sin_rows,
            second_half * cos_rows + first_half * sin_rows,
        ],
        axis=-1,
    )


def after(value, *earlier):
    return lax.optimization_barrier((value,) + earlier)[0]


def group_gather(block):
    half = block.shape[0] // 2
    low, high = block[:half], block[half:]
    low_x = swap(low, "x")
    high_y = swap(high, "y")
    low_y, low_xy = swap(low, "y"), swap(low_x, "y")
    high_x, high_xy = swap(high, "x"), swap(high_y, "x")
    pieces = [
        (low, high),
        (low_x, high_x),
        (low_y, high_y),
        (low_xy, high_xy),
    ]
    out = []
    for first, second in pieces:
        out += [first, second, swap(first, "c"), swap(second, "c")]
    return jnp.concatenate(out, axis=0)


def group_scatter(partial):
    rows = partial.shape[0] // PLANE
    half = rows // 2
    low, high = [], []
    for place in range(4):
        base = partial[2 * place * rows : (2 * place + 1) * rows]
        away = swap(partial[(2 * place + 1) * rows : (2 * place + 2) * rows], "c")
        both = base.astype(F32) + away.astype(F32)
        low.append(both[:half])
        high.append(both[half:])
    low0 = low[0] + swap(low[2].astype(BF), "y").astype(F32)
    low1 = low[1] + swap(low[3].astype(BF), "y").astype(F32)
    low_sum = low0 + swap(low1.astype(BF), "x").astype(F32)
    high0 = high[0] + swap(high[1].astype(BF), "x").astype(F32)
    high1 = high[2] + swap(high[3].astype(BF), "x").astype(F32)
    high_sum = high0 + swap(high1.astype(BF), "y").astype(F32)
    return jnp.concatenate([low_sum, high_sum], axis=0)


def group_total(value):
    kinds, wide = value.shape
    split = value.reshape(kinds, 2, 2, 2, wide // PLANE)
    for axis, dim in (("c", 3), ("x", 2), ("y", 1)):
        split = split + jnp.flip(swap(split, axis), dim)
    return split.reshape(kinds, wide)


def per_device(
    tokens,
    lengths,
    dealing,
    w_query,
    w_key,
    w_value,
    w_output,
    query_gain,
    key_gain,
    attn_gain,
    w_gate,
    w_up,
    w_down,
    mlp_gain,
    cotangent,
):
    groups = lax.axis_size("a")
    total = groups * PLANE
    rank = lax.axis_index(ALL)
    place = lax.axis_index(GROUP)
    micro_count, seq_len, width = cotangent.shape
    rows = micro_count * seq_len
    wide = rows * PLANE
    shard = width // total
    head_dim = width // HEADS
    own_heads = HEADS // PLANE
    own_width = own_heads * head_dim
    spread = head_dim // shard
    head_axes = GROUP[3 - (spread.bit_length() - 1) :]
    fan = PLANE // spread
    lead, lane = place // spread, place % spread

    cosines, sines = rotary_tables(seq_len, head_dim)
    positions = jnp.arange(seq_len, dtype=jnp.int32)
    causal = (positions[None, :] <= positions[:, None])[None, None]
    qk_scale = 1.0 / math.sqrt(head_dim)

    def heads_out(weight):
        split = weight.reshape(shard, spread, own_heads, fan, head_dim)
        return split.transpose(3, 1, 0, 2, 4).reshape(PLANE, shard, own_width)

    outgoing = jnp.take(tokens, dealing, axis=0)
    arrived = lax.all_to_all(outgoing, ALL, split_axis=0, concat_axis=1, tiled=True)
    x_low = arrived.reshape(rows, width)

    w_query, w_key, w_value, outgoing = lax.optimization_barrier((w_query, w_key, w_value, outgoing))
    qkv_out = jnp.concatenate([heads_out(w_query), heads_out(w_key), heads_out(w_value)], axis=2)
    qkv_in = lax.all_to_all(qkv_out, GROUP, split_axis=0, concat_axis=0, tiled=True)
    w_qkv = lax.all_gather(qkv_in, "a", axis=0, tiled=True).reshape(width, 3 * own_width)

    gains = jnp.stack([query_gain, key_gain, attn_gain, mlp_gain])
    gains = lax.all_to_all(
        jnp.broadcast_to(gains[None], (total, 4, shard)), ALL, split_axis=0, concat_axis=0, tiled=True
    )
    gains = gains.transpose(1, 0, 2).reshape(4, width).astype(F32)
    by_head = gains[:2].reshape(2, spread, own_heads, fan, head_dim)
    by_head = lax.dynamic_index_in_dim(by_head, lane, 1, keepdims=False)
    by_head = lax.dynamic_index_in_dim(by_head, lead, 2, keepdims=False)
    gain_query, gain_key = by_head[0].reshape(own_width), by_head[1].reshape(own_width)
    gain_attn, gain_mlp = gains[2], gains[3]

    out_all = lax.all_gather(w_output, "a", axis=0, tiled=False)
    w_out = lax.all_to_all(out_all, head_axes, split_axis=0, concat_axis=1, tiled=True)
    w_out = w_out.reshape(own_width, width)

    gate = lax.all_gather(after(w_gate.T, qkv_in), "a", axis=0, tiled=True)
    up = lax.all_gather(after(w_up.T, qkv_in), "a", axis=0, tiled=True)
    down = lax.all_gather(after(w_down, qkv_in), "a", axis=0, tiled=True)

    own_seqs = lax.dynamic_slice_in_dim(dealing, rank * micro_count, micro_count)
    own_lengths = jnp.take(lengths, own_seqs)
    valid_mask = (positions[None, :] < own_lengths[:, None]).astype(F32).reshape(rows, 1)

    x_wide = group_gather(x_low)
    qkv_raw = jnp.dot(x_wide, w_qkv, preferred_element_type=F32)
    query_raw = qkv_raw[:, :own_width]
    key_raw = qkv_raw[:, own_width : 2 * own_width]
    value_low = qkv_raw[:, 2 * own_width :].astype(BF)
    squares = group_total(
        jnp.stack([jnp.sum(query_raw * query_raw, axis=1), jnp.sum(key_raw * key_raw, axis=1)])
    )
    inverses = lax.rsqrt(squares * (1.0 / width) + norm_eps)
    query_inv, key_inv = inverses[0][:, None], inverses[1][:, None]
    head_shape = (wide // seq_len, seq_len, own_heads, head_dim)
    query_low = rotate((query_raw * query_inv * gain_query).reshape(head_shape), cosines, sines).astype(BF)
    key_low = rotate((key_raw * key_inv * gain_key).reshape(head_shape), cosines, sines).astype(BF)
    value_low = value_low.reshape(head_shape)
    scores = jnp.einsum("gthe,guhe->ghtu", query_low, key_low, preferred_element_type=F32) * qk_scale
    scores = jnp.where(causal, scores, -1e30)
    row_peak = jnp.max(scores, axis=-1, keepdims=True)
    exp_scores = jnp.exp(scores - row_peak)
    row_total = jnp.sum(exp_scores, axis=-1, keepdims=True)
    soft = exp_scores / row_total
    soft_low = soft.astype(BF)
    attended_low = (
        jnp.einsum("ghtu,guhe->gthe", soft_low, value_low, preferred_element_type=F32)
        .reshape(wide, own_width)
        .astype(BF)
    )
    out_raw = group_scatter(jnp.dot(attended_low, w_out, preferred_element_type=F32).astype(BF))
    out_inv = lax.rsqrt(jnp.mean(out_raw * out_raw, axis=-1, keepdims=True) + norm_eps)
    out_normed = out_raw * out_inv
    hidden = x_low.astype(F32) + out_normed * gain_attn

    hidden_wide = group_gather(hidden.astype(BF))
    contract_last = (((1,), (1,)), ((), ()))
    contract_rows = (((0,), (0,)), ((), ()))
    gate_proj = lax.dot_general(hidden_wide, gate, contract_last, preferred_element_type=F32)
    up_proj = lax.dot_general(hidden_wide, up, contract_last, preferred_element_type=F32)
    sigma_gate = jax.nn.sigmoid(gate_proj)
    act_value = gate_proj * sigma_gate
    act_low = (act_value * up_proj).astype(BF)
    down_raw = group_scatter(jnp.dot(act_low, down, preferred_element_type=F32).astype(BF))
    down_inv = lax.rsqrt(jnp.mean(down_raw * down_raw, axis=-1, keepdims=True) + norm_eps)
    down_normed = down_raw * down_inv
    block_out = (
        (valid_mask * (hidden + down_normed * gain_mlp)).astype(BF).reshape(micro_count, seq_len, width)
    )

    grad_out = valid_mask * cotangent.reshape(rows, width).astype(F32)
    grad_gain_mlp = jnp.sum(down_normed * grad_out, axis=0)
    scaled = grad_out * gain_mlp
    grad_down = down_inv * (scaled - down_normed * jnp.mean(scaled * down_normed, axis=-1, keepdims=True))
    grad_down_wide = group_gather(grad_down.astype(BF))

    down_term = lax.dot_general(
        act_low, grad_down_wide, contract_rows, preferred_element_type=F32
    ).astype(BF)
    grad_down_wide = after(grad_down_wide, down_term)
    grad_act = lax.dot_general(grad_down_wide, down, contract_last, preferred_element_type=F32)
    grad_gate_low = (grad_act * up_proj * sigma_gate * (1.0 + gate_proj * (1.0 - sigma_gate))).astype(BF)
    grad_up_low = (grad_act * act_value).astype(BF)
    grad_hidden = jnp.dot(grad_gate_low, gate, preferred_element_type=F32) + jnp.dot(
        grad_up_low, up, preferred_element_type=F32
    )
    grad_hidden = grad_out + group_scatter(grad_hidden.astype(BF))

    def owners(term):
        return lax.psum_scatter(term, "a", scatter_dimension=0, tiled=True)

    gate_term = lax.dot_general(
        grad_gate_low, hidden_wide, contract_rows, preferred_element_type=F32
    ).astype(BF)
    up_term = lax.dot_general(
        grad_up_low, hidden_wide, contract_rows, preferred_element_type=F32
    ).astype(BF)
    down_part = owners(down_term)
    gate_part = owners(after(gate_term, down_part))
    up_part = owners(after(up_term, gate_part))
    grad_hidden = after(grad_hidden, gate_term, up_term)

    grad_gain_attn = jnp.sum(out_normed * grad_hidden, axis=0)
    scaled = grad_hidden * gain_attn
    grad_out_raw = out_inv * (scaled - out_normed * jnp.mean(scaled * out_normed, axis=-1, keepdims=True))
    grad_out_wide = group_gather(grad_out_raw.astype(BF))

    output_term = lax.dot_general(attended_low, grad_out_wide, contract_rows, preferred_element_type=F32)
    output_term = lax.all_to_all(
        output_term.astype(BF).reshape(own_heads, head_dim, width),
        head_axes,
        split_axis=1,
        concat_axis=0,
        tiled=True,
    )
    output_part = owners(after(output_term.reshape(groups * shard, width), up_part))

    grad_att_low = (
        lax.dot_general(grad_out_wide, w_out, contract_last, preferred_element_type=F32)
        .astype(BF)
        .reshape(head_shape)
    )
    grad_soft = jnp.einsum("gthe,guhe->ghtu", grad_att_low, value_low, preferred_element_type=F32)
    row_delta = jnp.sum(soft * grad_soft, axis=-1, keepdims=True)
    grad_scores = (soft * (grad_soft - row_delta)).astype(BF)
    grad_q_rot = (
        jnp.einsum("ghtu,guhe->gthe", grad_scores, key_low, preferred_element_type=F32) * qk_scale
    )
    grad_k_rot = (
        jnp.einsum("ghtu,gthe->guhe", grad_scores, query_low, preferred_element_type=F32) * qk_scale
    )
    grad_value_low = (
        jnp.einsum("ghtu,gthe->guhe", soft_low, grad_att_low, preferred_element_type=F32)
        .reshape(wide, own_width)
        .astype(BF)
    )
    grad_q_norm = rotate(grad_q_rot, cosines, -sines).reshape(wide, own_width)
    grad_k_norm = rotate(grad_k_rot, cosines, -sines).reshape(wide, own_width)
    query_normed, key_normed = query_raw * query_inv, key_raw * key_inv
    grad_gain_q = jnp.sum(query_normed * grad_q_norm, axis=0)
    grad_gain_k = jnp.sum(key_normed * grad_k_norm, axis=0)
    scaled_q, scaled_k = grad_q_norm * gain_query, grad_k_norm * gain_key
    means = group_total(
        jnp.stack([jnp.sum(scaled_q * query_normed, axis=1), jnp.sum(scaled_k * key_normed, axis=1)])
    ) * (1.0 / width)
    grad_query = query_inv * (scaled_q - query_normed * means[0][:, None])
    grad_key = key_inv * (scaled_k - key_normed * means[1][:, None])
    grad_qkv = jnp.concatenate([grad_query.astype(BF), grad_key.astype(BF), grad_value_low], axis=1)

    grad_input = lax.dot_general(grad_qkv, w_qkv, contract_last, preferred_element_type=F32)
    grad_input = grad_hidden + group_scatter(grad_input.astype(BF))
    returned = lax.all_to_all(
        grad_input.astype(BF).reshape(micro_count, seq_len, width),
        ALL,
        split_axis=1,
        concat_axis=0,
        tiled=True,
    )
    input_grad = jnp.zeros_like(tokens).at[dealing].set(returned)

    qkv_term = lax.dot_general(x_wide, grad_qkv, contract_rows, preferred_element_type=F32)
    qkv_rows = owners(after(qkv_term.astype(BF), output_part))
    qkv_back = lax.all_to_all(
        qkv_rows.reshape(PLANE, shard, 3 * own_width), GROUP, split_axis=0, concat_axis=0, tiled=True
    )

    def heads_in(columns):
        split = columns.reshape(fan, spread, shard, own_heads, head_dim)
        return split.transpose(2, 1, 3, 0, 4).reshape(shard, width).astype(F32)

    query_part = heads_in(qkv_back[:, :, :own_width])
    key_part = heads_in(qkv_back[:, :, own_width : 2 * own_width])
    value_part = heads_in(qkv_back[:, :, 2 * own_width :])

    placed = jnp.zeros((2, spread, own_heads, fan, head_dim), F32)
    own = jnp.stack([grad_gain_q, grad_gain_k]).reshape(2, 1, own_heads, 1, head_dim)
    placed = lax.dynamic_update_slice(placed, own, (0, lane, 0, lead, 0)).reshape(2, width)
    gain_terms = jnp.concatenate([placed, jnp.stack([grad_gain_attn, grad_gain_mlp])])
    gain_terms = gain_terms.reshape(4, total, shard).transpose(1, 0, 2)
    gain_part = jnp.sum(
        lax.all_to_all(gain_terms, ALL, split_axis=0, concat_axis=0, tiled=True), axis=0
    )
    return (
        block_out,
        input_grad,
        query_part,
        key_part,
        value_part,
        output_part.astype(F32),
        gain_part[0],
        gain_part[1],
        gain_part[2],
        gate_part.astype(F32).T,
        up_part.astype(F32).T,
        down_part.astype(F32),
        gain_part[3],
    )


def solution(mesh):
    count = mesh.devices.size
    inner = Mesh(mesh.devices.reshape(count // PLANE, 2, 2, 2), ALL)
    first, second = P(ALL, None), P(None, ALL)
    vector = P(ALL)
    placed = (
        P(None, ALL, None),
        P(),
        P(),
        first,
        first,
        first,
        first,
        vector,
        vector,
        vector,
        second,
        second,
        first,
        vector,
        P(ALL, None, None),
    )
    return jax.shard_map(
        per_device,
        mesh=inner,
        in_specs=placed,
        out_specs=(
            P(ALL, None, None),
            P(None, ALL, None),
            first,
            first,
            first,
            first,
            vector,
            vector,
            vector,
            second,
            second,
            first,
            vector,
        ),
        check_vma=False,
    )
```

```python
import math

import jax
import jax.numpy as jnp
from jax import lax
from jax.experimental import pallas as pl
from jax.experimental.pallas import tpu as pltpu
from jax.sharding import Mesh
from jax.sharding import PartitionSpec as P

HEADS = 16
PLANE = 8
BF = jnp.bfloat16
F32 = jnp.float32

norm_eps = 1e-06
rope_base = 500000.0

ALL = ("z", "m", "y", "x", "c")
GROUP = ("y", "x", "c")
REST = ("z", "m")
LINE = 4
SWAP = [(0, 1), (1, 0)]


def swap(value, axis):
    return lax.ppermute(value, axis, SWAP)


def rotary_tables(length, head_dim):
    half_dim = head_dim // 2
    exponents = jnp.arange(half_dim, dtype=F32) * (2.0 / head_dim)
    frequency = jnp.power(F32(rope_base), -exponents)
    angles = jnp.arange(length, dtype=F32)[:, None] * frequency[None, :]
    return (jnp.cos(angles), jnp.sin(angles))


def wide_tables(length, head_dim):
    cosines, sines = rotary_tables(length, head_dim)
    return (
        jnp.concatenate([cosines, cosines], axis=1),
        jnp.concatenate([-sines, sines], axis=1),
    )


def by_rows(vector, columns):
    return jnp.broadcast_to(vector, (columns, vector.shape[1])).T


def row_sums(values):
    return jnp.sum(values.T, axis=0, keepdims=True)


def matmul(left, right, left_dim=1, right_dim=0):
    return lax.dot_general(left, right, (((left_dim,), (right_dim,)), ((), ())), preferred_element_type=F32)


def turn(values, cosines, sines):
    return values * cosines + pltpu.roll(values, values.shape[1] // 2, 1) * sines


def project_kernel(parts, x_ref, w_ref, raw_ref, squares_ref):
    raw = matmul(x_ref[...], w_ref[...])
    raw_ref[...] = raw
    width = raw.shape[1] // 3
    step = raw.shape[0] // parts
    for part in range(parts):
        rows = slice(part * step, (part + 1) * step)
        for kind in range(2):
            piece = raw[rows, kind * width : (kind + 1) * width]
            squares_ref[kind : kind + 1, rows] = row_sums(piece * piece)


def project(x_wide, weight, seq_len):
    wide, width = x_wide.shape
    out = weight.shape[1]
    block = 2 * seq_len
    return pl.pallas_call(
        lambda *refs: project_kernel(2, *refs),
        grid=(wide // block,),
        in_specs=[pl.BlockSpec((block, width), lambda i: (i, 0)), pl.BlockSpec((width, out), lambda i: (0, 0))],
        out_specs=[pl.BlockSpec((block, out), lambda i: (i, 0)), pl.BlockSpec((2, block), lambda i: (0, i))],
        out_shape=[jax.ShapeDtypeStruct((wide, out), F32), jax.ShapeDtypeStruct((2, wide), F32)],
        cost_estimate=pl.CostEstimate(
            flops=2 * wide * width * out, bytes_accessed=2 * wide * width + 2 * width * out + 4 * wide * out, transcendentals=0
        ),
        name="project",
    )(x_wide, weight)


def soften(scores, causal):
    scores = jnp.where(causal, scores, -1e30)
    exps = jnp.exp(scores - jnp.max(scores, axis=1, keepdims=True))
    return exps * (1.0 / jnp.sum(exps, axis=1, keepdims=True))


def causal_mask(length):
    rows = lax.broadcasted_iota(jnp.int32, (length, length), 0)
    return lax.broadcasted_iota(jnp.int32, (length, length), 1) <= rows


def heads_of(raw_ref, inverses, gain_ref, cosines, sines, rows, head, heads):
    dim = cosines.shape[1]
    out = []
    for kind in range(2):
        at = (kind * heads + head) * dim
        normed = raw_ref[rows, at : at + dim] * inverses[kind]
        gain = gain_ref[kind : kind + 1, head * dim : (head + 1) * dim]
        out += [normed, turn(normed * gain, cosines, sines).astype(BF), gain]
    at = (2 * heads + head) * dim
    return out + [raw_ref[rows, at : at + dim].astype(BF)]


def attend_kernel(heads, parts, scale, raw_ref, inv_ref, gain_ref, cos_ref, sin_ref, out_ref):
    cosines, sines = cos_ref[...], sin_ref[...]
    length, dim = cosines.shape
    causal = causal_mask(length)
    for part in range(parts):
        rows = slice(part * length, (part + 1) * length)
        inverses = [by_rows(inv_ref[kind : kind + 1, rows], dim) for kind in range(2)]
        for head in range(heads):
            _, query, _, _, key, _, value = heads_of(raw_ref, inverses, gain_ref, cosines, sines, rows, head, heads)
            soft = soften(matmul(query, key, 1, 1) * scale, causal)
            out_ref[rows, head * dim : (head + 1) * dim] = matmul(soft.astype(BF), value).astype(BF)


def attend_back_kernel(
    heads, parts, scale, raw_ref, inv_ref, gain_ref, cos_ref, sin_ref, grad_ref, scaled_ref, value_ref, dots_ref, gains_ref
):
    cosines, sines = cos_ref[...], sin_ref[...]
    length, dim = cosines.shape
    causal = causal_mask(length)

    @pl.when(pl.program_id(0) == 0)
    def _():
        gains_ref[...] = jnp.zeros_like(gains_ref)

    for part in range(parts):
        rows = slice(part * length, (part + 1) * length)
        inverses = [by_rows(inv_ref[kind : kind + 1, rows], dim) for kind in range(2)]
        dots = [0.0, 0.0]
        for head in range(heads):
            query_normed, query, query_gain, key_normed, key, key_gain, value = heads_of(
                raw_ref, inverses, gain_ref, cosines, sines, rows, head, heads
            )
            columns = slice(head * dim, (head + 1) * dim)
            soft = soften(matmul(query, key, 1, 1) * scale, causal)
            grad = grad_ref[rows, columns]
            grad_soft = matmul(grad, value, 1, 1)
            delta = jnp.sum(soft * grad_soft, axis=1, keepdims=True)
            grad_scores = (soft * (grad_soft - delta)).astype(BF)
            value_ref[rows, columns] = matmul(soft.astype(BF), grad, 0, 0).astype(BF)
            turned = (matmul(grad_scores, key) * scale, matmul(grad_scores, query, 0, 0) * scale)
            for kind, normed, gain in ((0, query_normed, query_gain), (1, key_normed, key_gain)):
                back = turn(turned[kind], cosines, -sines)
                gains_ref[kind : kind + 1, columns] += jnp.sum(normed * back, axis=0, keepdims=True)
                scaled = back * gain
                scaled_ref[rows, (kind * heads + head) * dim : (kind * heads + head + 1) * dim] = scaled
                dots[kind] = dots[kind] + scaled * normed
        for kind in range(2):
            dots_ref[kind : kind + 1, rows] = row_sums(dots[kind])


def finish_kernel(heads, parts, length, raw_ref, inv_ref, means_ref, scaled_ref, value_ref, out_ref):
    width = value_ref.shape[1]
    for part in range(parts):
        rows = slice(part * length, (part + 1) * length)
        for kind in range(2):
            columns = slice(kind * width, (kind + 1) * width)
            inverse = by_rows(inv_ref[kind : kind + 1, rows], width)
            mean = by_rows(means_ref[kind : kind + 1, rows], width)
            normed = raw_ref[rows, columns] * inverse
            out_ref[rows, columns] = (inverse * (scaled_ref[rows, columns] - normed * mean)).astype(BF)
        out_ref[rows, 2 * width :] = value_ref[rows, :]


def block_specs(block, heads, dim, length):
    own = heads * dim
    rows = lambda columns: pl.BlockSpec((block, columns), lambda i: (i, 0))
    lanes = pl.BlockSpec((2, block), lambda i: (0, i))
    fixed = lambda shape: pl.BlockSpec(shape, lambda i: (0, 0))
    return own, rows, lanes, [rows(3 * own), lanes, fixed((2, own)), fixed((length, dim)), fixed((length, dim))]


def attend(raw, inverses, gains, tables, heads):
    length, dim = tables[0].shape
    wide = raw.shape[0]
    block = 2 * length
    own, rows, _, specs = block_specs(block, heads, dim, length)
    return pl.pallas_call(
        lambda *refs: attend_kernel(heads, 2, 1.0 / math.sqrt(dim), *refs),
        grid=(wide // block,),
        in_specs=specs,
        out_specs=rows(own),
        out_shape=jax.ShapeDtypeStruct((wide, own), BF),
        cost_estimate=pl.CostEstimate(
            flops=4 * wide * length * own, bytes_accessed=14 * wide * own, transcendentals=wide * length * heads
        ),
        name="attend",
    )(raw, inverses, gains, *tables)


def attend_back(raw, inverses, gains, tables, heads, grad):
    length, dim = tables[0].shape
    wide = raw.shape[0]
    block = 2 * length
    own, rows, lanes, specs = block_specs(block, heads, dim, length)
    return pl.pallas_call(
        lambda *refs: attend_back_kernel(heads, 2, 1.0 / math.sqrt(dim), *refs),
        grid=(wide // block,),
        in_specs=specs + [rows(own)],
        out_specs=[rows(2 * own), rows(own), lanes, pl.BlockSpec((2, own), lambda i: (0, 0))],
        out_shape=[
            jax.ShapeDtypeStruct((wide, 2 * own), F32),
            jax.ShapeDtypeStruct((wide, own), BF),
            jax.ShapeDtypeStruct((2, wide), F32),
            jax.ShapeDtypeStruct((2, own), F32),
        ],
        cost_estimate=pl.CostEstimate(
            flops=10 * wide * length * own, bytes_accessed=26 * wide * own, transcendentals=wide * length * heads
        ),
        name="attend_back",
    )(raw, inverses, gains, *tables, grad)


def finish(raw, inverses, means, scaled, value, length, heads):
    wide, own = value.shape
    block = 2 * length
    rows = lambda columns: pl.BlockSpec((block, columns), lambda i: (i, 0))
    lanes = pl.BlockSpec((2, block), lambda i: (0, i))
    return pl.pallas_call(
        lambda *refs: finish_kernel(heads, 2, length, *refs),
        grid=(wide // block,),
        in_specs=[rows(3 * own), lanes, lanes, rows(2 * own), rows(own)],
        out_specs=rows(3 * own),
        out_shape=jax.ShapeDtypeStruct((wide, 3 * own), BF),
        cost_estimate=pl.CostEstimate(flops=8 * wide * own, bytes_accessed=28 * wide * own, transcendentals=0),
        name="finish",
    )(raw, inverses, means, scaled, value)


def after(value, *earlier):
    return lax.optimization_barrier((value,) + earlier)[0]


def group_gather(block, meanwhile=None):
    half = block.shape[0] // 2
    over_x, over_y = swap(block, "x"), swap(block, "y")
    near_x, near_y = over_x[:half], over_y[half:]
    done = None
    if meanwhile is not None:
        done = meanwhile(block)
        near_x, near_y, _ = lax.optimization_barrier((near_x, near_y, done))
    pieces = [block, over_x, over_y, swap(near_x, "y"), swap(near_y, "x")]
    return jnp.concatenate(pieces + [swap(piece, "c") for piece in pieces], axis=0), over_x, done


def group_scatter(partial, meanwhile=None):
    wide = partial.shape[0] // 2
    rows = wide // 4
    half = rows // 2

    def both(i):
        away = swap(partial[wide + i * rows : wide + (i + 1) * rows], "c")
        return partial[i * rows : (i + 1) * rows].astype(F32) + away.astype(F32)

    def move(value, axis):
        return swap(value.astype(BF), axis).astype(F32)

    far, over_x, over_y, own = both(3), both(1), both(2), both(0)
    far_low, far_high = far[:half].astype(BF), far[half:].astype(BF)
    far_x, far_y = swap(far_low, "x"), swap(far_high, "y")
    done = None
    if meanwhile is not None:
        done = meanwhile(far_low)
        far_x, far_y, _ = lax.optimization_barrier((far_x, far_y, done))
    over_y = jnp.concatenate([over_y[:half] + far_x.astype(F32), over_y[half:]])
    over_x = jnp.concatenate([over_x[:half], over_x[half:] + far_y.astype(F32)])
    return own + move(over_x, "x") + move(over_y, "y"), done


def ring(ahead):
    return [(i, (i + ahead) % LINE) for i in range(LINE)]


def line_gather(block, at):
    out = jnp.zeros((LINE,) + block.shape, block.dtype)
    out = lax.dynamic_update_index_in_dim(out, block, at, 0)
    for ahead in range(1, LINE):
        moved = lax.ppermute(block, "z", ring(ahead))
        out = lax.dynamic_update_index_in_dim(out, moved, (at - ahead) % LINE, 0)
    return out


def line_sum(blocks, at):
    total = lax.dynamic_index_in_dim(blocks, at, 0, keepdims=False).astype(F32)
    for ahead in range(1, LINE):
        block = lax.dynamic_index_in_dim(blocks, (at + ahead) % LINE, 0, keepdims=False)
        total = total + lax.ppermute(block, "z", ring(ahead)).astype(F32)
    return total


def group_total(value):
    kinds, wide = value.shape
    split = value.reshape(kinds, 2, 2, 2, wide // PLANE)
    for axis, dim in (("c", 1), ("x", 3), ("y", 2)):
        split = split + jnp.flip(swap(split, axis), dim)
    return split.reshape(kinds, wide)


def per_device(
    tokens,
    lengths,
    dealing,
    w_query,
    w_key,
    w_value,
    w_output,
    query_gain,
    key_gain,
    attn_gain,
    w_gate,
    w_up,
    w_down,
    mlp_gain,
    cotangent,
):
    groups = lax.axis_size(REST)
    total = groups * PLANE
    rank = lax.axis_index(ALL)
    place = lax.axis_index(GROUP)
    at = lax.axis_index("z")
    along = lax.axis_size("m")
    micro_count, seq_len, width = cotangent.shape
    rows = micro_count * seq_len
    wide = rows * PLANE
    shard = width // total
    head_dim = width // HEADS
    own_heads = HEADS // PLANE
    own_width = own_heads * head_dim
    spread = head_dim // shard
    head_axes = GROUP[3 - (spread.bit_length() - 1) :]
    fan = PLANE // spread
    lead, lane = place // spread, place % spread

    tables = wide_tables(seq_len, head_dim)
    positions = jnp.arange(seq_len, dtype=jnp.int32)

    def heads_out(weight):
        split = weight.reshape(shard, spread, own_heads, fan, head_dim)
        return split.transpose(3, 1, 0, 2, 4).reshape(PLANE, shard, own_width)

    outgoing = jnp.take(tokens, dealing, axis=0)
    arrived = lax.all_to_all(outgoing, ALL, split_axis=0, concat_axis=1, tiled=True)
    x_low = arrived.reshape(rows, width)

    w_query, w_key, w_value, outgoing = lax.optimization_barrier((w_query, w_key, w_value, outgoing))
    qkv_out = jnp.concatenate([heads_out(w_query), heads_out(w_key), heads_out(w_value)], axis=2)
    qkv_in = lax.all_to_all(qkv_out, GROUP, split_axis=0, concat_axis=0, tiled=True)

    gains = jnp.stack([query_gain, key_gain, attn_gain, mlp_gain])
    gains = lax.all_to_all(
        jnp.broadcast_to(gains[None], (total, 4, shard)), ALL, split_axis=0, concat_axis=0, tiled=True
    )
    gains = gains.transpose(1, 0, 2).reshape(4, width).astype(F32)
    by_head = gains[:2].reshape(2, spread, own_heads, fan, head_dim)
    by_head = lax.dynamic_index_in_dim(by_head, lane, 1, keepdims=False)
    by_head = lax.dynamic_index_in_dim(by_head, lead, 2, keepdims=False)
    gain_heads = by_head.reshape(2, own_width)
    gain_attn, gain_mlp = gains[2], gains[3]

    out_all = w_output
    if along > 1:
        out_all = lax.all_gather(out_all, "m", axis=0, tiled=True)
    out_all = line_gather(out_all, at).reshape(groups, shard, width)
    qkv_in = after(qkv_in, out_all)
    w_qkv = lax.all_gather(qkv_in, REST, axis=0, tiled=True).reshape(width, 3 * own_width)
    w_out = lax.all_to_all(out_all, head_axes, split_axis=0, concat_axis=1, tiled=True)
    w_out = w_out.reshape(own_width, width)

    gate = lax.all_gather(after(w_gate.T, qkv_in), REST, axis=0, tiled=True)
    up = lax.all_gather(after(w_up.T, qkv_in), REST, axis=0, tiled=True)
    down = lax.all_gather(after(w_down, qkv_in), REST, axis=0, tiled=True)

    own_seqs = lax.dynamic_slice_in_dim(dealing, rank * micro_count, micro_count)
    own_lengths = jnp.take(lengths, own_seqs)
    valid_mask = (positions[None, :] < own_lengths[:, None]).astype(F32).reshape(rows, 1)

    x_wide, _, _ = group_gather(x_low)
    qkv_raw, squares = project(x_wide, w_qkv, seq_len)
    inverses = lax.rsqrt(group_total(squares) * (1.0 / width) + norm_eps)
    attended_low = attend(qkv_raw, inverses, gain_heads, tables, own_heads)
    out_raw, _ = group_scatter(jnp.dot(attended_low, w_out, preferred_element_type=F32).astype(BF))
    out_inv = lax.rsqrt(jnp.mean(out_raw * out_raw, axis=-1, keepdims=True) + norm_eps)
    out_normed = out_raw * out_inv
    hidden = x_low.astype(F32) + out_normed * gain_attn

    hidden_wide, _, _ = group_gather(hidden.astype(BF))
    contract_last = (((1,), (1,)), ((), ()))
    contract_rows = (((0,), (0,)), ((), ()))
    gate_proj = lax.dot_general(hidden_wide, gate, contract_last, preferred_element_type=F32)
    up_proj = lax.dot_general(hidden_wide, up, contract_last, preferred_element_type=F32)
    sigma_gate = jax.nn.sigmoid(gate_proj)
    act_value = gate_proj * sigma_gate
    act_low = (act_value * up_proj).astype(BF)
    down_raw, _ = group_scatter(jnp.dot(act_low, down, preferred_element_type=F32).astype(BF))
    down_inv = lax.rsqrt(jnp.mean(down_raw * down_raw, axis=-1, keepdims=True) + norm_eps)
    down_normed = down_raw * down_inv
    block_out = (
        (valid_mask * (hidden + down_normed * gain_mlp)).astype(BF).reshape(micro_count, seq_len, width)
    )

    grad_out = valid_mask * cotangent.reshape(rows, width).astype(F32)
    grad_gain_mlp = jnp.sum(down_normed * grad_out, axis=0)
    scaled = grad_out * gain_mlp
    grad_down = down_inv * (scaled - down_normed * jnp.mean(scaled * down_normed, axis=-1, keepdims=True))
    grad_down_wide, _, _ = group_gather(grad_down.astype(BF))

    down_term = lax.dot_general(
        act_low, grad_down_wide, contract_rows, preferred_element_type=F32
    ).astype(BF)
    grad_act = lax.dot_general(grad_down_wide, down, contract_last, preferred_element_type=F32)
    grad_gate_low = (grad_act * up_proj * sigma_gate * (1.0 + gate_proj * (1.0 - sigma_gate))).astype(BF)
    grad_up_low = (grad_act * act_value).astype(BF)
    grad_gate_low = after(grad_gate_low, down_term)
    grad_hidden = jnp.dot(grad_gate_low, gate, preferred_element_type=F32) + jnp.dot(
        grad_up_low, up, preferred_element_type=F32
    )
    hidden_term = grad_hidden.astype(BF)

    def weight_term(left, right):
        return lambda token: lax.dot_general(
            after(left, token), right, contract_rows, preferred_element_type=F32
        ).astype(BF)

    moved, gate_term = group_scatter(hidden_term, weight_term(grad_gate_low, hidden_wide))
    grad_hidden = grad_out + moved

    def owners(term):
        return lax.psum_scatter(term, REST, scatter_dimension=0, tiled=True)

    down_part = owners(down_term)

    grad_gain_attn = jnp.sum(out_normed * grad_hidden, axis=0)
    scaled = grad_hidden * gain_attn
    grad_out_raw = out_inv * (scaled - out_normed * jnp.mean(scaled * out_normed, axis=-1, keepdims=True))
    grad_out_low = grad_out_raw.astype(BF)
    grad_out_wide, grad_out_near, up_term = group_gather(grad_out_low, weight_term(grad_up_low, hidden_wide))

    output_term = lax.dot_general(
        attended_low, grad_out_wide, contract_rows, preferred_element_type=F32
    ).astype(BF)
    grad_out_wide = after(grad_out_wide, output_term)
    output_term = lax.all_to_all(
        output_term.reshape(own_heads, head_dim, width),
        head_axes,
        split_axis=1,
        concat_axis=0,
        tiled=True,
    )

    grad_att = lax.dot_general(grad_out_wide, w_out, contract_last, preferred_element_type=F32).astype(BF)
    scaled, grad_value, dots, gain_term = attend_back(qkv_raw, inverses, gain_heads, tables, own_heads, grad_att)
    means = group_total(dots) * (1.0 / width)
    grad_qkv = finish(qkv_raw, inverses, means, scaled, grad_value, seq_len, own_heads)

    grad_input = lax.dot_general(grad_qkv, w_qkv, contract_last, preferred_element_type=F32)
    grad_input = after(grad_input.astype(BF), output_term)
    moved, qkv_term = group_scatter(grad_input, weight_term(x_wide, grad_qkv))
    grad_input = grad_hidden + moved
    output_part = line_sum(output_term.reshape(LINE, along * shard, width), at)
    if along > 1:
        output_part = lax.psum_scatter(output_part.astype(BF), "m", scatter_dimension=0, tiled=True)
    returned = lax.all_to_all(
        after(grad_input.astype(BF), output_part).reshape(micro_count, seq_len, width),
        ALL,
        split_axis=1,
        concat_axis=0,
        tiled=True,
    )
    input_grad = jnp.zeros_like(tokens).at[dealing].set(returned)

    gate_part = owners(after(gate_term, down_part, hidden_term))
    up_part = owners(after(up_term, gate_part, grad_out_near))
    qkv_rows = owners(after(qkv_term, up_part))
    qkv_back = lax.all_to_all(
        qkv_rows.reshape(PLANE, shard, 3 * own_width), GROUP, split_axis=0, concat_axis=0, tiled=True
    )

    def heads_in(columns):
        split = columns.reshape(fan, spread, shard, own_heads, head_dim)
        return split.transpose(2, 1, 3, 0, 4).reshape(shard, width).astype(F32)

    query_part = heads_in(qkv_back[:, :, :own_width])
    key_part = heads_in(qkv_back[:, :, own_width : 2 * own_width])
    value_part = heads_in(qkv_back[:, :, 2 * own_width :])

    placed = jnp.zeros((2, spread, own_heads, fan, head_dim), F32)
    own = gain_term.reshape(2, 1, own_heads, 1, head_dim)
    placed = lax.dynamic_update_slice(placed, own, (0, lane, 0, lead, 0)).reshape(2, width)
    gain_terms = jnp.concatenate([placed, jnp.stack([grad_gain_attn, grad_gain_mlp])])
    gain_terms = gain_terms.reshape(4, total, shard).transpose(1, 0, 2)
    gain_part = jnp.sum(
        lax.all_to_all(gain_terms, ALL, split_axis=0, concat_axis=0, tiled=True), axis=0
    )
    return (
        block_out,
        input_grad,
        query_part,
        key_part,
        value_part,
        output_part.astype(F32),
        gain_part[0],
        gain_part[1],
        gain_part[2],
        gate_part.astype(F32).T,
        up_part.astype(F32).T,
        down_part.astype(F32),
        gain_part[3],
    )


def solution(mesh):
    count = mesh.devices.size
    inner = Mesh(mesh.devices.reshape(LINE, count // (LINE * PLANE), 2, 2, 2), ALL)
    first, second = P(ALL, None), P(None, ALL)
    vector = P(ALL)
    placed = (
        P(None, ALL, None),
        P(),
        P(),
        first,
        first,
        first,
        first,
        vector,
        vector,
        vector,
        second,
        second,
        first,
        vector,
        P(ALL, None, None),
    )
    return jax.shard_map(
        per_device,
        mesh=inner,
        in_specs=placed,
        out_specs=(
            P(ALL, None, None),
            P(None, ALL, None),
            first,
            first,
            first,
            first,
            vector,
            vector,
            vector,
            second,
            second,
            first,
            vector,
        ),
        check_vma=False,
    )
```

```python
import math

import jax
import jax.numpy as jnp
from jax import lax
from jax.experimental import pallas as pl
from jax.experimental.pallas import tpu as pltpu
from jax.sharding import Mesh
from jax.sharding import PartitionSpec as P

HEADS = 16
PLANE = 8
BF = jnp.bfloat16
F32 = jnp.float32

norm_eps = 1e-06
rope_base = 500000.0

ALL = ("z", "m", "y", "x", "c")
GROUP = ("y", "x", "c")
REST = ("z", "m")
LINE = 4
SWAP = [(0, 1), (1, 0)]


def swap(value, axis):
    return lax.ppermute(value, axis, SWAP)


def rotary_tables(length, head_dim):
    half_dim = head_dim // 2
    exponents = jnp.arange(half_dim, dtype=F32) * (2.0 / head_dim)
    frequency = jnp.power(F32(rope_base), -exponents)
    angles = jnp.arange(length, dtype=F32)[:, None] * frequency[None, :]
    return (jnp.cos(angles), jnp.sin(angles))


def wide_tables(length, head_dim):
    cosines, sines = rotary_tables(length, head_dim)
    return (
        jnp.concatenate([cosines, cosines], axis=1),
        jnp.concatenate([-sines, sines], axis=1),
    )


def by_rows(vector, columns):
    return jnp.broadcast_to(vector, (columns, vector.shape[1])).T


def row_sums(values):
    return jnp.sum(values.T, axis=0, keepdims=True)


def matmul(left, right, left_dim=1, right_dim=0):
    return lax.dot_general(left, right, (((left_dim,), (right_dim,)), ((), ())), preferred_element_type=F32)


def turn(values, cosines, sines):
    return values * cosines + pltpu.roll(values, values.shape[1] // 2, 1) * sines


def project_kernel(parts, x_ref, w_ref, raw_ref, squares_ref):
    raw = matmul(x_ref[...], w_ref[...])
    raw_ref[...] = raw
    width = raw.shape[1] // 3
    step = raw.shape[0] // parts
    for part in range(parts):
        rows = slice(part * step, (part + 1) * step)
        for kind in range(2):
            piece = raw[rows, kind * width : (kind + 1) * width]
            squares_ref[kind : kind + 1, rows] = row_sums(piece * piece)


def project(x_wide, weight, seq_len):
    wide, width = x_wide.shape
    out = weight.shape[1]
    block = 2 * seq_len
    return pl.pallas_call(
        lambda *refs: project_kernel(2, *refs),
        grid=(wide // block,),
        in_specs=[pl.BlockSpec((block, width), lambda i: (i, 0)), pl.BlockSpec((width, out), lambda i: (0, 0))],
        out_specs=[pl.BlockSpec((block, out), lambda i: (i, 0)), pl.BlockSpec((2, block), lambda i: (0, i))],
        out_shape=[jax.ShapeDtypeStruct((wide, out), F32), jax.ShapeDtypeStruct((2, wide), F32)],
        cost_estimate=pl.CostEstimate(
            flops=2 * wide * width * out, bytes_accessed=2 * wide * width + 2 * width * out + 4 * wide * out, transcendentals=0
        ),
        name="project",
    )(x_wide, weight)


def soften(scores, causal):
    scores = jnp.where(causal, scores, -1e30)
    exps = jnp.exp(scores - jnp.max(scores, axis=1, keepdims=True))
    return exps * (1.0 / jnp.sum(exps, axis=1, keepdims=True))


def causal_mask(length):
    rows = lax.broadcasted_iota(jnp.int32, (length, length), 0)
    return lax.broadcasted_iota(jnp.int32, (length, length), 1) <= rows


def heads_of(raw_ref, inverses, gain_ref, cosines, sines, rows, head, heads):
    dim = cosines.shape[1]
    out = []
    for kind in range(2):
        at = (kind * heads + head) * dim
        normed = raw_ref[rows, at : at + dim] * inverses[kind]
        gain = gain_ref[kind : kind + 1, head * dim : (head + 1) * dim]
        out += [normed, turn(normed * gain, cosines, sines).astype(BF), gain]
    at = (2 * heads + head) * dim
    return out + [raw_ref[rows, at : at + dim].astype(BF)]


def attend_kernel(heads, parts, scale, raw_ref, inv_ref, gain_ref, cos_ref, sin_ref, out_ref):
    cosines, sines = cos_ref[...], sin_ref[...]
    length, dim = cosines.shape
    causal = causal_mask(length)
    for part in range(parts):
        rows = slice(part * length, (part + 1) * length)
        inverses = [by_rows(inv_ref[kind : kind + 1, rows], dim) for kind in range(2)]
        for head in range(heads):
            _, query, _, _, key, _, value = heads_of(raw_ref, inverses, gain_ref, cosines, sines, rows, head, heads)
            soft = soften(matmul(query, key, 1, 1) * scale, causal)
            out_ref[rows, head * dim : (head + 1) * dim] = matmul(soft.astype(BF), value).astype(BF)


def attend_back_kernel(
    heads, parts, scale, raw_ref, inv_ref, gain_ref, cos_ref, sin_ref, grad_ref, scaled_ref, value_ref, dots_ref, gains_ref
):
    cosines, sines = cos_ref[...], sin_ref[...]
    length, dim = cosines.shape
    causal = causal_mask(length)

    @pl.when(pl.program_id(0) == 0)
    def _():
        gains_ref[...] = jnp.zeros_like(gains_ref)

    for part in range(parts):
        rows = slice(part * length, (part + 1) * length)
        inverses = [by_rows(inv_ref[kind : kind + 1, rows], dim) for kind in range(2)]
        dots = [0.0, 0.0]
        for head in range(heads):
            query_normed, query, query_gain, key_normed, key, key_gain, value = heads_of(
                raw_ref, inverses, gain_ref, cosines, sines, rows, head, heads
            )
            columns = slice(head * dim, (head + 1) * dim)
            soft = soften(matmul(query, key, 1, 1) * scale, causal)
            grad = grad_ref[rows, columns]
            grad_soft = matmul(grad, value, 1, 1)
            delta = jnp.sum(soft * grad_soft, axis=1, keepdims=True)
            grad_scores = (soft * (grad_soft - delta)).astype(BF)
            value_ref[rows, columns] = matmul(soft.astype(BF), grad, 0, 0).astype(BF)
            turned = (matmul(grad_scores, key) * scale, matmul(grad_scores, query, 0, 0) * scale)
            for kind, normed, gain in ((0, query_normed, query_gain), (1, key_normed, key_gain)):
                back = turn(turned[kind], cosines, -sines)
                gains_ref[kind : kind + 1, columns] += jnp.sum(normed * back, axis=0, keepdims=True)
                scaled = back * gain
                scaled_ref[rows, (kind * heads + head) * dim : (kind * heads + head + 1) * dim] = scaled
                dots[kind] = dots[kind] + scaled * normed
        for kind in range(2):
            dots_ref[kind : kind + 1, rows] = row_sums(dots[kind])


def finish_kernel(heads, parts, length, raw_ref, inv_ref, means_ref, scaled_ref, value_ref, out_ref):
    width = value_ref.shape[1]
    for part in range(parts):
        rows = slice(part * length, (part + 1) * length)
        for kind in range(2):
            columns = slice(kind * width, (kind + 1) * width)
            inverse = by_rows(inv_ref[kind : kind + 1, rows], width)
            mean = by_rows(means_ref[kind : kind + 1, rows], width)
            normed = raw_ref[rows, columns] * inverse
            out_ref[rows, columns] = (inverse * (scaled_ref[rows, columns] - normed * mean)).astype(BF)
        out_ref[rows, 2 * width :] = value_ref[rows, :]


def block_specs(block, heads, dim, length):
    own = heads * dim
    rows = lambda columns: pl.BlockSpec((block, columns), lambda i: (i, 0))
    lanes = pl.BlockSpec((2, block), lambda i: (0, i))
    fixed = lambda shape: pl.BlockSpec(shape, lambda i: (0, 0))
    return own, rows, lanes, [rows(3 * own), lanes, fixed((2, own)), fixed((length, dim)), fixed((length, dim))]


def attend(raw, inverses, gains, tables, heads):
    length, dim = tables[0].shape
    wide = raw.shape[0]
    block = 2 * length
    own, rows, _, specs = block_specs(block, heads, dim, length)
    return pl.pallas_call(
        lambda *refs: attend_kernel(heads, 2, 1.0 / math.sqrt(dim), *refs),
        grid=(wide // block,),
        in_specs=specs,
        out_specs=rows(own),
        out_shape=jax.ShapeDtypeStruct((wide, own), BF),
        cost_estimate=pl.CostEstimate(
            flops=4 * wide * length * own, bytes_accessed=14 * wide * own, transcendentals=wide * length * heads
        ),
        name="attend",
    )(raw, inverses, gains, *tables)


def attend_back(raw, inverses, gains, tables, heads, grad):
    length, dim = tables[0].shape
    wide = raw.shape[0]
    block = 2 * length
    own, rows, lanes, specs = block_specs(block, heads, dim, length)
    return pl.pallas_call(
        lambda *refs: attend_back_kernel(heads, 2, 1.0 / math.sqrt(dim), *refs),
        grid=(wide // block,),
        in_specs=specs + [rows(own)],
        out_specs=[rows(2 * own), rows(own), lanes, pl.BlockSpec((2, own), lambda i: (0, 0))],
        out_shape=[
            jax.ShapeDtypeStruct((wide, 2 * own), F32),
            jax.ShapeDtypeStruct((wide, own), BF),
            jax.ShapeDtypeStruct((2, wide), F32),
            jax.ShapeDtypeStruct((2, own), F32),
        ],
        cost_estimate=pl.CostEstimate(
            flops=10 * wide * length * own, bytes_accessed=26 * wide * own, transcendentals=wide * length * heads
        ),
        name="attend_back",
    )(raw, inverses, gains, *tables, grad)


def finish(raw, inverses, means, scaled, value, length, heads):
    wide, own = value.shape
    block = 2 * length
    rows = lambda columns: pl.BlockSpec((block, columns), lambda i: (i, 0))
    lanes = pl.BlockSpec((2, block), lambda i: (0, i))
    return pl.pallas_call(
        lambda *refs: finish_kernel(heads, 2, length, *refs),
        grid=(wide // block,),
        in_specs=[rows(3 * own), lanes, lanes, rows(2 * own), rows(own)],
        out_specs=rows(3 * own),
        out_shape=jax.ShapeDtypeStruct((wide, 3 * own), BF),
        cost_estimate=pl.CostEstimate(flops=8 * wide * own, bytes_accessed=28 * wide * own, transcendentals=0),
        name="finish",
    )(raw, inverses, means, scaled, value)


def after(value, *earlier):
    return lax.optimization_barrier((value,) + earlier)[0]


def group_gather(block, meanwhile=None):
    half = block.shape[0] // 2
    over_x, over_y = swap(block, "x"), swap(block, "y")
    near_x, near_y = over_x[:half], over_y[half:]
    done = None
    if meanwhile is not None:
        done = meanwhile(block)
        near_x, near_y, _ = lax.optimization_barrier((near_x, near_y, done))
    pieces = [block, over_x, over_y, swap(near_x, "y"), swap(near_y, "x")]
    return jnp.concatenate(pieces + [swap(piece, "c") for piece in pieces], axis=0), over_x, done


def group_scatter(partial, meanwhile=None, until=()):
    wide = partial.shape[0] // 2
    rows = wide // 4
    half = rows // 2

    def both(i):
        away = swap(partial[wide + i * rows : wide + (i + 1) * rows], "c")
        return partial[i * rows : (i + 1) * rows].astype(F32) + away.astype(F32)

    def move(value, axis):
        return swap(value.astype(BF), axis).astype(F32)

    far, over_x, over_y, own = both(3), both(1), both(2), both(0)
    far_low, far_high = far[:half].astype(BF), far[half:].astype(BF)
    far_x, far_y = swap(far_low, "x"), swap(far_high, "y")
    done = None
    if meanwhile is not None:
        done = meanwhile(far_low)
        far_x, far_y = lax.optimization_barrier((far_x, far_y, done) + until)[:2]
    over_y = jnp.concatenate([over_y[:half] + far_x.astype(F32), over_y[half:]])
    over_x = jnp.concatenate([over_x[:half], over_x[half:] + far_y.astype(F32)])
    return own + move(over_x, "x") + move(over_y, "y"), done


def gated_kernel(groups, hidden_ref, weight_ref, raw_ref, act_ref):
    raw = matmul(hidden_ref[...], weight_ref[...], 1, 1)
    raw_ref[...] = raw
    step = raw.shape[1] // (2 * groups)
    for i in range(groups):
        gate = raw[:, 2 * i * step : (2 * i + 1) * step]
        up = raw[:, (2 * i + 1) * step : (2 * i + 2) * step]
        act_ref[:, i * step : (i + 1) * step] = (gate * jax.nn.sigmoid(gate) * up).astype(BF)


def gated(hidden, weight, groups):
    wide, width = hidden.shape
    units = weight.shape[0]
    block = 256
    rows = lambda columns: pl.BlockSpec((block, columns), lambda i: (i, 0))
    return pl.pallas_call(
        lambda *refs: gated_kernel(groups, *refs),
        grid=(wide // block,),
        in_specs=[rows(width), pl.BlockSpec((units, width), lambda i: (0, 0))],
        out_specs=[rows(units), rows(units // 2)],
        out_shape=[jax.ShapeDtypeStruct((wide, units), F32), jax.ShapeDtypeStruct((wide, units // 2), BF)],
        cost_estimate=pl.CostEstimate(
            flops=2 * wide * width * units,
            bytes_accessed=2 * wide * width + 2 * units * width + 5 * wide * units,
            transcendentals=wide * units // 2,
        ),
        name="gated",
    )(hidden, weight)


def gated_back_kernel(groups, grad_ref, down_ref, raw_ref, weight_ref, units_ref, hidden_ref):
    grad_act = matmul(grad_ref[...], down_ref[...], 1, 1)
    step = grad_act.shape[1] // groups
    for i in range(groups):
        gate = raw_ref[:, 2 * i * step : (2 * i + 1) * step]
        up = raw_ref[:, (2 * i + 1) * step : (2 * i + 2) * step]
        grad = grad_act[:, i * step : (i + 1) * step]
        sigma = jax.nn.sigmoid(gate)
        units_ref[:, 2 * i * step : (2 * i + 1) * step] = (
            grad * up * sigma * (1.0 + gate * (1.0 - sigma))
        ).astype(BF)
        units_ref[:, (2 * i + 1) * step : (2 * i + 2) * step] = (grad * (gate * sigma)).astype(BF)
    hidden_ref[...] = matmul(units_ref[...], weight_ref[...]).astype(BF)


def gated_back(grad, down, raw, weight, groups):
    wide, width = grad.shape
    units = weight.shape[0]
    block = 256
    rows = lambda columns: pl.BlockSpec((block, columns), lambda i: (i, 0))
    fixed = lambda count: pl.BlockSpec((count, width), lambda i: (0, 0))
    return pl.pallas_call(
        lambda *refs: gated_back_kernel(groups, *refs),
        grid=(wide // block,),
        in_specs=[rows(width), fixed(units // 2), rows(units), fixed(units)],
        out_specs=[rows(units), rows(width)],
        out_shape=[jax.ShapeDtypeStruct((wide, units), BF), jax.ShapeDtypeStruct((wide, width), BF)],
        cost_estimate=pl.CostEstimate(
            flops=3 * wide * width * units,
            bytes_accessed=4 * wide * width + 3 * units * width + 6 * wide * units,
            transcendentals=wide * units // 2,
        ),
        name="gated_back",
    )(grad, down, raw, weight)


def ring(ahead):
    return [(i, (i + ahead) % LINE) for i in range(LINE)]


def line_gather(block, at):
    out = jnp.zeros((LINE,) + block.shape, block.dtype)
    out = lax.dynamic_update_index_in_dim(out, block, at, 0)
    for ahead in range(1, LINE):
        moved = lax.ppermute(block, "z", ring(ahead))
        out = lax.dynamic_update_index_in_dim(out, moved, (at - ahead) % LINE, 0)
    return out


def group_total(value):
    kinds, wide = value.shape
    split = value.reshape(kinds, 2, 2, 2, wide // PLANE)
    for axis, dim in (("c", 1), ("x", 3), ("y", 2)):
        split = split + jnp.flip(swap(split, axis), dim)
    return split.reshape(kinds, wide)


def per_device(
    tokens,
    lengths,
    dealing,
    w_query,
    w_key,
    w_value,
    w_output,
    query_gain,
    key_gain,
    attn_gain,
    w_gate,
    w_up,
    w_down,
    mlp_gain,
    cotangent,
):
    groups = lax.axis_size(REST)
    total = groups * PLANE
    rank = lax.axis_index(ALL)
    place = lax.axis_index(GROUP)
    at = lax.axis_index("z")
    along = lax.axis_size("m")
    micro_count, seq_len, width = cotangent.shape
    rows = micro_count * seq_len
    wide = rows * PLANE
    shard = width // total
    head_dim = width // HEADS
    own_heads = HEADS // PLANE
    own_width = own_heads * head_dim
    spread = head_dim // shard
    head_axes = GROUP[3 - (spread.bit_length() - 1) :]
    fan = PLANE // spread
    lead, lane = place // spread, place % spread

    tables = wide_tables(seq_len, head_dim)
    positions = jnp.arange(seq_len, dtype=jnp.int32)

    def heads_out(weight):
        split = weight.reshape(shard, spread, own_heads, fan, head_dim)
        return split.transpose(3, 1, 0, 2, 4).reshape(PLANE, shard, own_width)

    outgoing = jnp.take(tokens, dealing, axis=0)
    arrived = lax.all_to_all(outgoing, ALL, split_axis=0, concat_axis=1, tiled=True)
    x_low = arrived.reshape(rows, width)

    w_query, w_key, w_value, outgoing = lax.optimization_barrier((w_query, w_key, w_value, outgoing))
    qkv_out = jnp.concatenate([heads_out(w_query), heads_out(w_key), heads_out(w_value)], axis=2)
    qkv_in = lax.all_to_all(qkv_out, GROUP, split_axis=0, concat_axis=0, tiled=True)

    gains = jnp.stack([query_gain, key_gain, attn_gain, mlp_gain])
    gains = lax.all_to_all(
        jnp.broadcast_to(gains[None], (total, 4, shard)), ALL, split_axis=0, concat_axis=0, tiled=True
    )
    gains = gains.transpose(1, 0, 2).reshape(4, width).astype(F32)
    by_head = gains[:2].reshape(2, spread, own_heads, fan, head_dim)
    by_head = lax.dynamic_index_in_dim(by_head, lane, 1, keepdims=False)
    by_head = lax.dynamic_index_in_dim(by_head, lead, 2, keepdims=False)
    gain_heads = by_head.reshape(2, own_width)
    gain_attn, gain_mlp = gains[2], gains[3]

    out_all = w_output
    if along > 1:
        out_all = lax.all_gather(out_all, "m", axis=0, tiled=True)
    out_all = line_gather(out_all, at).reshape(groups, shard, width)
    qkv_in = after(qkv_in, out_all)
    w_qkv = lax.all_gather(qkv_in, REST, axis=0, tiled=True).reshape(width, 3 * own_width)
    w_out = lax.all_to_all(out_all, head_axes, split_axis=0, concat_axis=1, tiled=True)
    w_out = w_out.reshape(own_width, width)

    units = w_gate.shape[1]
    gate_up = jnp.concatenate([w_gate.T, w_up.T])
    gate_up = lax.all_gather(after(gate_up, qkv_in), REST, axis=0, tiled=True)
    down = lax.all_gather(after(w_down, qkv_in), REST, axis=0, tiled=True)

    own_seqs = lax.dynamic_slice_in_dim(dealing, rank * micro_count, micro_count)
    own_lengths = jnp.take(lengths, own_seqs)
    valid_mask = (positions[None, :] < own_lengths[:, None]).astype(F32).reshape(rows, 1)

    x_wide, _, _ = group_gather(x_low)
    qkv_raw, squares = project(x_wide, w_qkv, seq_len)
    inverses = lax.rsqrt(group_total(squares) * (1.0 / width) + norm_eps)
    attended_low = attend(qkv_raw, inverses, gain_heads, tables, own_heads)
    out_raw, _ = group_scatter(jnp.dot(attended_low, w_out, preferred_element_type=F32).astype(BF))
    out_inv = lax.rsqrt(jnp.mean(out_raw * out_raw, axis=-1, keepdims=True) + norm_eps)
    out_normed = out_raw * out_inv
    hidden = x_low.astype(F32) + out_normed * gain_attn

    hidden_wide, _, _ = group_gather(hidden.astype(BF))
    contract_last = (((1,), (1,)), ((), ()))
    contract_rows = (((0,), (0,)), ((), ()))
    unit_raw, act_low = gated(hidden_wide, gate_up, groups)
    down_raw, _ = group_scatter(jnp.dot(act_low, down, preferred_element_type=F32).astype(BF))
    down_inv = lax.rsqrt(jnp.mean(down_raw * down_raw, axis=-1, keepdims=True) + norm_eps)
    down_normed = down_raw * down_inv
    block_out = (
        (valid_mask * (hidden + down_normed * gain_mlp)).astype(BF).reshape(micro_count, seq_len, width)
    )

    grad_out = valid_mask * cotangent.reshape(rows, width).astype(F32)
    grad_gain_mlp = jnp.sum(down_normed * grad_out, axis=0)
    scaled = grad_out * gain_mlp
    grad_down = down_inv * (scaled - down_normed * jnp.mean(scaled * down_normed, axis=-1, keepdims=True))
    grad_down_wide, _, _ = group_gather(grad_down.astype(BF))

    down_term = lax.dot_general(
        act_low, grad_down_wide, contract_rows, preferred_element_type=F32
    ).astype(BF)
    grad_units, hidden_term = gated_back(after(grad_down_wide, down_term), down, unit_raw, gate_up, groups)

    def weight_term(left, right):
        return lambda token: lax.dot_general(
            after(left, token), right, contract_rows, preferred_element_type=F32
        ).astype(BF)

    def owners(term):
        return lax.psum_scatter(term, REST, scatter_dimension=0, tiled=True)

    down_part = owners(down_term)
    moved, unit_term = group_scatter(hidden_term, weight_term(grad_units, hidden_wide), (down_part,))
    grad_hidden = grad_out + moved
    unit_part = owners(after(unit_term, down_part))

    grad_gain_attn = jnp.sum(out_normed * grad_hidden, axis=0)
    scaled = grad_hidden * gain_attn
    grad_out_raw = out_inv * (scaled - out_normed * jnp.mean(scaled * out_normed, axis=-1, keepdims=True))
    grad_out_low = grad_out_raw.astype(BF)
    grad_out_wide, _, _ = group_gather(grad_out_low)

    output_term = lax.dot_general(
        attended_low, grad_out_wide, contract_rows, preferred_element_type=F32
    ).astype(BF)
    grad_out_wide = after(grad_out_wide, output_term)
    output_term = lax.all_to_all(
        output_term.reshape(own_heads, head_dim, width),
        head_axes,
        split_axis=1,
        concat_axis=0,
        tiled=True,
    )

    grad_att = lax.dot_general(grad_out_wide, w_out, contract_last, preferred_element_type=F32).astype(BF)
    scaled, grad_value, dots, gain_term = attend_back(qkv_raw, inverses, gain_heads, tables, own_heads, grad_att)
    scaled = after(scaled, output_term)
    means = group_total(dots) * (1.0 / width)
    grad_qkv = finish(qkv_raw, inverses, means, scaled, grad_value, seq_len, own_heads)

    grad_input = lax.dot_general(grad_qkv, w_qkv, contract_last, preferred_element_type=F32)
    grad_input = after(grad_input.astype(BF), output_term)
    moved, qkv_term = group_scatter(grad_input, weight_term(x_wide, grad_qkv))
    grad_input = grad_hidden + moved
    returned = lax.all_to_all(
        grad_input.astype(BF).reshape(micro_count, seq_len, width),
        ALL,
        split_axis=1,
        concat_axis=0,
        tiled=True,
    )
    input_grad = jnp.zeros_like(tokens).at[dealing].set(returned)

    qkv_rows = owners(after(qkv_term, unit_part))
    output_part = owners(after(output_term.reshape(groups * shard, width), qkv_term))
    qkv_back = lax.all_to_all(
        qkv_rows.reshape(PLANE, shard, 3 * own_width), GROUP, split_axis=0, concat_axis=0, tiled=True
    )

    def heads_in(columns):
        split = columns.reshape(fan, spread, shard, own_heads, head_dim)
        return split.transpose(2, 1, 3, 0, 4).reshape(shard, width).astype(F32)

    query_part = heads_in(qkv_back[:, :, :own_width])
    key_part = heads_in(qkv_back[:, :, own_width : 2 * own_width])
    value_part = heads_in(qkv_back[:, :, 2 * own_width :])

    placed = jnp.zeros((2, spread, own_heads, fan, head_dim), F32)
    own = gain_term.reshape(2, 1, own_heads, 1, head_dim)
    placed = lax.dynamic_update_slice(placed, own, (0, lane, 0, lead, 0)).reshape(2, width)
    gain_terms = jnp.concatenate([placed, jnp.stack([grad_gain_attn, grad_gain_mlp])])
    gain_terms = gain_terms.reshape(4, total, shard).transpose(1, 0, 2)
    gain_part = jnp.sum(
        lax.all_to_all(gain_terms, ALL, split_axis=0, concat_axis=0, tiled=True), axis=0
    )
    return (
        block_out,
        input_grad,
        query_part,
        key_part,
        value_part,
        output_part.astype(F32),
        gain_part[0],
        gain_part[1],
        gain_part[2],
        unit_part[:units].astype(F32).T,
        unit_part[units:].astype(F32).T,
        down_part.astype(F32),
        gain_part[3],
    )


def solution(mesh):
    count = mesh.devices.size
    inner = Mesh(mesh.devices.reshape(LINE, count // (LINE * PLANE), 2, 2, 2), ALL)
    first, second = P(ALL, None), P(None, ALL)
    vector = P(ALL)
    placed = (
        P(None, ALL, None),
        P(),
        P(),
        first,
        first,
        first,
        first,
        vector,
        vector,
        vector,
        second,
        second,
        first,
        vector,
        P(ALL, None, None),
    )
    return jax.shard_map(
        per_device,
        mesh=inner,
        in_specs=placed,
        out_specs=(
            P(ALL, None, None),
            P(None, ALL, None),
            first,
            first,
            first,
            first,
            vector,
            vector,
            vector,
            second,
            second,
            first,
            vector,
        ),
        check_vma=False,
    )
```

```python
import math

import jax
import jax.numpy as jnp
from jax import lax
from jax.experimental import pallas as pl
from jax.experimental.pallas import tpu as pltpu
from jax.sharding import Mesh
from jax.sharding import PartitionSpec as P

HEADS = 16
PLANE = 8
BF = jnp.bfloat16
F32 = jnp.float32

norm_eps = 1e-06
rope_base = 500000.0

ALL = ("z", "m", "y", "x", "c")
GROUP = ("y", "x", "c")
REST = ("z", "m")
LINE = 4
SWAP = [(0, 1), (1, 0)]


def swap(value, axis):
    return lax.ppermute(value, axis, SWAP)


def rotary_tables(length, head_dim):
    half_dim = head_dim // 2
    exponents = jnp.arange(half_dim, dtype=F32) * (2.0 / head_dim)
    frequency = jnp.power(F32(rope_base), -exponents)
    angles = jnp.arange(length, dtype=F32)[:, None] * frequency[None, :]
    return (jnp.cos(angles), jnp.sin(angles))


def wide_tables(length, head_dim):
    cosines, sines = rotary_tables(length, head_dim)
    return (
        jnp.concatenate([cosines, cosines], axis=1),
        jnp.concatenate([-sines, sines], axis=1),
    )


def by_rows(vector, columns):
    return jnp.broadcast_to(vector, (columns, vector.shape[1])).T


def row_sums(values):
    return jnp.sum(values.T, axis=0, keepdims=True)


def matmul(left, right, left_dim=1, right_dim=0):
    return lax.dot_general(left, right, (((left_dim,), (right_dim,)), ((), ())), preferred_element_type=F32)


def turn(values, cosines, sines):
    return values * cosines + pltpu.roll(values, values.shape[1] // 2, 1) * sines


def project_kernel(parts, x_ref, w_ref, raw_ref, squares_ref):
    raw = matmul(x_ref[...], w_ref[...])
    raw_ref[...] = raw
    width = raw.shape[1] // 3
    step = raw.shape[0] // parts
    for part in range(parts):
        rows = slice(part * step, (part + 1) * step)
        for kind in range(2):
            piece = raw[rows, kind * width : (kind + 1) * width]
            squares_ref[kind : kind + 1, rows] = row_sums(piece * piece)


def project(x_wide, weight, seq_len):
    wide, width = x_wide.shape
    out = weight.shape[1]
    block = 2 * seq_len
    return pl.pallas_call(
        lambda *refs: project_kernel(2, *refs),
        grid=(wide // block,),
        in_specs=[pl.BlockSpec((block, width), lambda i: (i, 0)), pl.BlockSpec((width, out), lambda i: (0, 0))],
        out_specs=[pl.BlockSpec((block, out), lambda i: (i, 0)), pl.BlockSpec((2, block), lambda i: (0, i))],
        out_shape=[jax.ShapeDtypeStruct((wide, out), F32), jax.ShapeDtypeStruct((2, wide), F32)],
        cost_estimate=pl.CostEstimate(
            flops=2 * wide * width * out, bytes_accessed=2 * wide * width + 2 * width * out + 4 * wide * out, transcendentals=0
        ),
        name="project",
    )(x_wide, weight)


def soften(scores, causal):
    scores = jnp.where(causal, scores, -1e30)
    exps = jnp.exp(scores - jnp.max(scores, axis=1, keepdims=True))
    return exps * (1.0 / jnp.sum(exps, axis=1, keepdims=True))


def causal_mask(length):
    rows = lax.broadcasted_iota(jnp.int32, (length, length), 0)
    return lax.broadcasted_iota(jnp.int32, (length, length), 1) <= rows


def heads_of(raw_ref, inverses, gain_ref, cosines, sines, rows, head, heads):
    dim = cosines.shape[1]
    out = []
    for kind in range(2):
        at = (kind * heads + head) * dim
        normed = raw_ref[rows, at : at + dim] * inverses[kind]
        gain = gain_ref[kind : kind + 1, head * dim : (head + 1) * dim]
        out += [normed, turn(normed * gain, cosines, sines).astype(BF), gain]
    at = (2 * heads + head) * dim
    return out + [raw_ref[rows, at : at + dim].astype(BF)]


def attend_kernel(heads, parts, scale, raw_ref, inv_ref, gain_ref, cos_ref, sin_ref, out_ref):
    cosines, sines = cos_ref[...], sin_ref[...]
    length, dim = cosines.shape
    causal = causal_mask(length)
    for part in range(parts):
        rows = slice(part * length, (part + 1) * length)
        inverses = [by_rows(inv_ref[kind : kind + 1, rows], dim) for kind in range(2)]
        for head in range(heads):
            _, query, _, _, key, _, value = heads_of(raw_ref, inverses, gain_ref, cosines, sines, rows, head, heads)
            soft = soften(matmul(query, key, 1, 1) * scale, causal)
            out_ref[rows, head * dim : (head + 1) * dim] = matmul(soft.astype(BF), value).astype(BF)


def attend_back_kernel(
    heads, parts, scale, raw_ref, inv_ref, gain_ref, cos_ref, sin_ref, grad_ref, scaled_ref, value_ref, dots_ref, gains_ref
):
    cosines, sines = cos_ref[...], sin_ref[...]
    length, dim = cosines.shape
    causal = causal_mask(length)

    @pl.when(pl.program_id(0) == 0)
    def _():
        gains_ref[...] = jnp.zeros_like(gains_ref)

    for part in range(parts):
        rows = slice(part * length, (part + 1) * length)
        inverses = [by_rows(inv_ref[kind : kind + 1, rows], dim) for kind in range(2)]
        dots = [0.0, 0.0]
        for head in range(heads):
            query_normed, query, query_gain, key_normed, key, key_gain, value = heads_of(
                raw_ref, inverses, gain_ref, cosines, sines, rows, head, heads
            )
            columns = slice(head * dim, (head + 1) * dim)
            soft = soften(matmul(query, key, 1, 1) * scale, causal)
            grad = grad_ref[rows, columns]
            grad_soft = matmul(grad, value, 1, 1)
            delta = jnp.sum(soft * grad_soft, axis=1, keepdims=True)
            grad_scores = (soft * (grad_soft - delta)).astype(BF)
            value_ref[rows, columns] = matmul(soft.astype(BF), grad, 0, 0).astype(BF)
            turned = (matmul(grad_scores, key) * scale, matmul(grad_scores, query, 0, 0) * scale)
            for kind, normed, gain in ((0, query_normed, query_gain), (1, key_normed, key_gain)):
                back = turn(turned[kind], cosines, -sines)
                gains_ref[kind : kind + 1, columns] += jnp.sum(normed * back, axis=0, keepdims=True)
                scaled = back * gain
                scaled_ref[rows, (kind * heads + head) * dim : (kind * heads + head + 1) * dim] = scaled
                dots[kind] = dots[kind] + scaled * normed
        for kind in range(2):
            dots_ref[kind : kind + 1, rows] = row_sums(dots[kind])


def finish_kernel(heads, parts, length, raw_ref, inv_ref, means_ref, scaled_ref, value_ref, weight_ref, out_ref, input_ref):
    width = value_ref.shape[1]
    for part in range(parts):
        rows = slice(part * length, (part + 1) * length)
        for kind in range(2):
            columns = slice(kind * width, (kind + 1) * width)
            inverse = by_rows(inv_ref[kind : kind + 1, rows], width)
            mean = by_rows(means_ref[kind : kind + 1, rows], width)
            normed = raw_ref[rows, columns] * inverse
            out_ref[rows, columns] = (inverse * (scaled_ref[rows, columns] - normed * mean)).astype(BF)
        out_ref[rows, 2 * width :] = value_ref[rows, :]
    input_ref[...] = matmul(out_ref[...], weight_ref[...], 1, 1).astype(BF)


def block_specs(block, heads, dim, length):
    own = heads * dim
    rows = lambda columns: pl.BlockSpec((block, columns), lambda i: (i, 0))
    lanes = pl.BlockSpec((2, block), lambda i: (0, i))
    fixed = lambda shape: pl.BlockSpec(shape, lambda i: (0, 0))
    return own, rows, lanes, [rows(3 * own), lanes, fixed((2, own)), fixed((length, dim)), fixed((length, dim))]


def attend(raw, inverses, gains, tables, heads):
    length, dim = tables[0].shape
    wide = raw.shape[0]
    block = 2 * length
    own, rows, _, specs = block_specs(block, heads, dim, length)
    return pl.pallas_call(
        lambda *refs: attend_kernel(heads, 2, 1.0 / math.sqrt(dim), *refs),
        grid=(wide // block,),
        in_specs=specs,
        out_specs=rows(own),
        out_shape=jax.ShapeDtypeStruct((wide, own), BF),
        cost_estimate=pl.CostEstimate(
            flops=4 * wide * length * own, bytes_accessed=14 * wide * own, transcendentals=wide * length * heads
        ),
        name="attend",
    )(raw, inverses, gains, *tables)


def attend_back(raw, inverses, gains, tables, heads, grad):
    length, dim = tables[0].shape
    wide = raw.shape[0]
    block = 2 * length
    own, rows, lanes, specs = block_specs(block, heads, dim, length)
    return pl.pallas_call(
        lambda *refs: attend_back_kernel(heads, 2, 1.0 / math.sqrt(dim), *refs),
        grid=(wide // block,),
        in_specs=specs + [rows(own)],
        out_specs=[rows(2 * own), rows(own), lanes, pl.BlockSpec((2, own), lambda i: (0, 0))],
        out_shape=[
            jax.ShapeDtypeStruct((wide, 2 * own), F32),
            jax.ShapeDtypeStruct((wide, own), BF),
            jax.ShapeDtypeStruct((2, wide), F32),
            jax.ShapeDtypeStruct((2, own), F32),
        ],
        cost_estimate=pl.CostEstimate(
            flops=10 * wide * length * own, bytes_accessed=26 * wide * own, transcendentals=wide * length * heads
        ),
        name="attend_back",
    )(raw, inverses, gains, *tables, grad)


def finish(raw, inverses, means, scaled, value, length, heads, weight):
    wide, own = value.shape
    block = 2 * length
    rows = lambda columns: pl.BlockSpec((block, columns), lambda i: (i, 0))
    lanes = pl.BlockSpec((2, block), lambda i: (0, i))
    return pl.pallas_call(
        lambda *refs: finish_kernel(heads, 2, length, *refs),
        grid=(wide // block,),
        in_specs=[rows(3 * own), lanes, lanes, rows(2 * own), rows(own), pl.BlockSpec(weight.shape, lambda i: (0, 0))],
        out_specs=[rows(3 * own), rows(weight.shape[0])],
        out_shape=[jax.ShapeDtypeStruct((wide, 3 * own), BF), jax.ShapeDtypeStruct((wide, weight.shape[0]), BF)],
        cost_estimate=pl.CostEstimate(
            flops=2 * wide * weight.size, bytes_accessed=28 * wide * own + 2 * wide * weight.shape[0], transcendentals=0
        ),
        name="finish",
    )(raw, inverses, means, scaled, value, weight)


def after(value, *earlier):
    return lax.optimization_barrier((value,) + earlier)[0]


def group_gather(block, meanwhile=None):
    half = block.shape[0] // 2
    over_x, over_y = swap(block, "x"), swap(block, "y")
    near_x, near_y = over_x[:half], over_y[half:]
    done = None
    if meanwhile is not None:
        done = meanwhile(block)
        near_x, near_y, _ = lax.optimization_barrier((near_x, near_y, done))
    pieces = [block, over_x, over_y, swap(near_x, "y"), swap(near_y, "x")]
    return jnp.concatenate(pieces + [swap(piece, "c") for piece in pieces], axis=0), over_x, done


def group_scatter(partial, meanwhile=None):
    wide = partial.shape[0] // 2
    rows = wide // 4
    half = rows // 2

    def both(i):
        away = swap(partial[wide + i * rows : wide + (i + 1) * rows], "c")
        return partial[i * rows : (i + 1) * rows].astype(F32) + away.astype(F32)

    def move(value, axis):
        return swap(value.astype(BF), axis).astype(F32)

    far, over_x, over_y, own = both(3), both(1), both(2), both(0)
    far_low, far_high = far[:half].astype(BF), far[half:].astype(BF)
    far_x, far_y = swap(far_low, "x"), swap(far_high, "y")
    done = None
    if meanwhile is not None:
        done = meanwhile(far_low)
        far_x, far_y, done = lax.optimization_barrier((far_x, far_y, done))
    over_y = jnp.concatenate([over_y[:half] + far_x.astype(F32), over_y[half:]])
    over_x = jnp.concatenate([over_x[:half], over_x[half:] + far_y.astype(F32)])
    return own + move(over_x, "x") + move(over_y, "y"), done


def gated_kernel(groups, hidden_ref, weight_ref, raw_ref, act_ref):
    raw = matmul(hidden_ref[...], weight_ref[...], 1, 1)
    raw_ref[...] = raw
    step = raw.shape[1] // (2 * groups)
    for i in range(groups):
        gate = raw[:, 2 * i * step : (2 * i + 1) * step]
        up = raw[:, (2 * i + 1) * step : (2 * i + 2) * step]
        act_ref[:, i * step : (i + 1) * step] = (gate * jax.nn.sigmoid(gate) * up).astype(BF)


def gated(hidden, weight, groups):
    wide, width = hidden.shape
    units = weight.shape[0]
    block = 256
    rows = lambda columns: pl.BlockSpec((block, columns), lambda i: (i, 0))
    return pl.pallas_call(
        lambda *refs: gated_kernel(groups, *refs),
        grid=(wide // block,),
        in_specs=[rows(width), pl.BlockSpec((units, width), lambda i: (0, 0))],
        out_specs=[rows(units), rows(units // 2)],
        out_shape=[jax.ShapeDtypeStruct((wide, units), F32), jax.ShapeDtypeStruct((wide, units // 2), BF)],
        cost_estimate=pl.CostEstimate(
            flops=2 * wide * width * units,
            bytes_accessed=2 * wide * width + 2 * units * width + 5 * wide * units,
            transcendentals=wide * units // 2,
        ),
        name="gated",
    )(hidden, weight)


def gated_back_kernel(groups, grad_ref, down_ref, raw_ref, weight_ref, units_ref, hidden_ref):
    grad_act = matmul(grad_ref[...], down_ref[...], 1, 1)
    step = grad_act.shape[1] // groups
    for i in range(groups):
        gate = raw_ref[:, 2 * i * step : (2 * i + 1) * step]
        up = raw_ref[:, (2 * i + 1) * step : (2 * i + 2) * step]
        grad = grad_act[:, i * step : (i + 1) * step]
        sigma = jax.nn.sigmoid(gate)
        units_ref[:, 2 * i * step : (2 * i + 1) * step] = (
            grad * up * sigma * (1.0 + gate * (1.0 - sigma))
        ).astype(BF)
        units_ref[:, (2 * i + 1) * step : (2 * i + 2) * step] = (grad * (gate * sigma)).astype(BF)
    hidden_ref[...] = matmul(units_ref[...], weight_ref[...]).astype(BF)


def gated_back(grad, down, raw, weight, groups):
    wide, width = grad.shape
    units = weight.shape[0]
    block = 256
    rows = lambda columns: pl.BlockSpec((block, columns), lambda i: (i, 0))
    fixed = lambda count: pl.BlockSpec((count, width), lambda i: (0, 0))
    return pl.pallas_call(
        lambda *refs: gated_back_kernel(groups, *refs),
        grid=(wide // block,),
        in_specs=[rows(width), fixed(units // 2), rows(units), fixed(units)],
        out_specs=[rows(units), rows(width)],
        out_shape=[jax.ShapeDtypeStruct((wide, units), BF), jax.ShapeDtypeStruct((wide, width), BF)],
        cost_estimate=pl.CostEstimate(
            flops=3 * wide * width * units,
            bytes_accessed=4 * wide * width + 3 * units * width + 6 * wide * units,
            transcendentals=wide * units // 2,
        ),
        name="gated_back",
    )(grad, down, raw, weight)


def ring(ahead):
    return [(i, (i + ahead) % LINE) for i in range(LINE)]


def line_gather(block, at):
    out = jnp.zeros((LINE,) + block.shape, block.dtype)
    out = lax.dynamic_update_index_in_dim(out, block, at, 0)
    for ahead in range(1, LINE):
        moved = lax.ppermute(block, "z", ring(ahead))
        out = lax.dynamic_update_index_in_dim(out, moved, (at - ahead) % LINE, 0)
    return out


def group_exchange(blocks, place):
    out = jnp.zeros_like(blocks)
    out = lax.dynamic_update_index_in_dim(out, lax.dynamic_index_in_dim(blocks, place, 0), place, 0)
    for apart in range(1, PLANE):
        block = lax.dynamic_index_in_dim(blocks, place ^ apart, 0)
        moved = lax.ppermute(block, GROUP, [(i, i ^ apart) for i in range(PLANE)])
        out = lax.dynamic_update_index_in_dim(out, moved, place ^ apart, 0)
    return out


def group_total(value):
    kinds, wide = value.shape
    split = value.reshape(kinds, 2, 2, 2, wide // PLANE)
    for axis, dim in (("c", 1), ("x", 3), ("y", 2)):
        split = split + jnp.flip(swap(split, axis), dim)
    return split.reshape(kinds, wide)


def per_device(
    tokens,
    lengths,
    dealing,
    w_query,
    w_key,
    w_value,
    w_output,
    query_gain,
    key_gain,
    attn_gain,
    w_gate,
    w_up,
    w_down,
    mlp_gain,
    cotangent,
):
    groups = lax.axis_size(REST)
    total = groups * PLANE
    rank = lax.axis_index(ALL)
    place = lax.axis_index(GROUP)
    at = lax.axis_index("z")
    along = lax.axis_size("m")
    micro_count, seq_len, width = cotangent.shape
    rows = micro_count * seq_len
    wide = rows * PLANE
    shard = width // total
    head_dim = width // HEADS
    own_heads = HEADS // PLANE
    own_width = own_heads * head_dim
    spread = head_dim // shard
    head_axes = GROUP[3 - (spread.bit_length() - 1) :]
    fan = PLANE // spread
    lead, lane = place // spread, place % spread

    tables = wide_tables(seq_len, head_dim)
    positions = jnp.arange(seq_len, dtype=jnp.int32)

    def heads_out(weight):
        split = weight.reshape(shard, spread, own_heads, fan, head_dim)
        return split.transpose(3, 1, 0, 2, 4).reshape(PLANE, shard, own_width)

    outgoing = jnp.take(tokens, dealing, axis=0)
    arrived = lax.all_to_all(outgoing, ALL, split_axis=0, concat_axis=1, tiled=True)
    x_low = arrived.reshape(rows, width)

    w_query, w_key, w_value, outgoing = lax.optimization_barrier((w_query, w_key, w_value, outgoing))
    qkv_out = jnp.concatenate([heads_out(w_query), heads_out(w_key), heads_out(w_value)], axis=2)
    qkv_in = lax.all_to_all(qkv_out, GROUP, split_axis=0, concat_axis=0, tiled=True)

    gains = jnp.stack([query_gain, key_gain, attn_gain, mlp_gain])
    gains = lax.all_to_all(
        jnp.broadcast_to(gains[None], (total, 4, shard)), ALL, split_axis=0, concat_axis=0, tiled=True
    )
    gains = gains.transpose(1, 0, 2).reshape(4, width).astype(F32)
    by_head = gains[:2].reshape(2, spread, own_heads, fan, head_dim)
    by_head = lax.dynamic_index_in_dim(by_head, lane, 1, keepdims=False)
    by_head = lax.dynamic_index_in_dim(by_head, lead, 2, keepdims=False)
    gain_heads = by_head.reshape(2, own_width)
    gain_attn, gain_mlp = gains[2], gains[3]

    out_all = w_output
    if along > 1:
        out_all = lax.all_gather(out_all, "m", axis=0, tiled=True)
    out_all = line_gather(out_all, at).reshape(groups, shard, width)
    qkv_in = after(qkv_in, out_all)
    w_qkv = lax.all_gather(qkv_in, REST, axis=0, tiled=True).reshape(width, 3 * own_width)
    w_out = lax.all_to_all(out_all, head_axes, split_axis=0, concat_axis=1, tiled=True)
    w_out = w_out.reshape(own_width, width)

    units = w_gate.shape[1]
    gate_up = jnp.concatenate([w_gate.T, w_up.T])
    gate_up = lax.all_gather(after(gate_up, qkv_in), REST, axis=0, tiled=True)
    down = lax.all_gather(after(w_down, qkv_in), REST, axis=0, tiled=True)

    own_seqs = lax.dynamic_slice_in_dim(dealing, rank * micro_count, micro_count)
    own_lengths = jnp.take(lengths, own_seqs)
    valid_mask = (positions[None, :] < own_lengths[:, None]).astype(F32).reshape(rows, 1)

    x_wide, _, _ = group_gather(x_low)
    qkv_raw, squares = project(x_wide, w_qkv, seq_len)
    inverses = lax.rsqrt(group_total(squares) * (1.0 / width) + norm_eps)
    attended_low = attend(qkv_raw, inverses, gain_heads, tables, own_heads)
    out_raw, _ = group_scatter(jnp.dot(attended_low, w_out, preferred_element_type=F32).astype(BF))
    out_inv = lax.rsqrt(jnp.mean(out_raw * out_raw, axis=-1, keepdims=True) + norm_eps)
    out_normed = out_raw * out_inv
    hidden = x_low.astype(F32) + out_normed * gain_attn

    hidden_wide, _, _ = group_gather(hidden.astype(BF))
    contract_last = (((1,), (1,)), ((), ()))
    contract_rows = (((0,), (0,)), ((), ()))
    unit_raw, act_low = gated(hidden_wide, gate_up, groups)
    down_raw, _ = group_scatter(jnp.dot(act_low, down, preferred_element_type=F32).astype(BF))
    down_inv = lax.rsqrt(jnp.mean(down_raw * down_raw, axis=-1, keepdims=True) + norm_eps)
    down_normed = down_raw * down_inv
    block_out = (
        (valid_mask * (hidden + down_normed * gain_mlp)).astype(BF).reshape(micro_count, seq_len, width)
    )

    grad_out = valid_mask * cotangent.reshape(rows, width).astype(F32)
    grad_gain_mlp = jnp.sum(down_normed * grad_out, axis=0)
    scaled = grad_out * gain_mlp
    grad_down = down_inv * (scaled - down_normed * jnp.mean(scaled * down_normed, axis=-1, keepdims=True))
    grad_down_wide, _, _ = group_gather(grad_down.astype(BF))

    down_term = lax.dot_general(
        act_low, grad_down_wide, contract_rows, preferred_element_type=F32
    ).astype(BF)
    grad_units, hidden_term = gated_back(after(grad_down_wide, down_term), down, unit_raw, gate_up, groups)

    def weight_term(left, right):
        return lambda token: lax.dot_general(
            after(left, *(token if isinstance(token, tuple) else (token,))), right, contract_rows, preferred_element_type=F32
        ).astype(BF)

    def owners(term):
        return lax.psum_scatter(term, REST, scatter_dimension=0, tiled=True)

    down_part = owners(down_term)
    moved, unit_term = group_scatter(hidden_term, weight_term(grad_units, hidden_wide))
    grad_hidden = grad_out + moved
    unit_part = owners(after(unit_term, down_part))

    grad_gain_attn = jnp.sum(out_normed * grad_hidden, axis=0)
    scaled = grad_hidden * gain_attn
    grad_out_raw = out_inv * (scaled - out_normed * jnp.mean(scaled * out_normed, axis=-1, keepdims=True))
    grad_out_low = grad_out_raw.astype(BF)
    grad_out_wide, _, _ = group_gather(grad_out_low)

    output_term = lax.dot_general(
        attended_low, grad_out_wide, contract_rows, preferred_element_type=F32
    ).astype(BF)
    grad_out_wide = after(grad_out_wide, output_term)
    output_term = lax.all_to_all(
        output_term.reshape(own_heads, head_dim, width),
        head_axes,
        split_axis=1,
        concat_axis=0,
        tiled=True,
    )

    grad_att = lax.dot_general(grad_out_wide, w_out, contract_last, preferred_element_type=F32).astype(BF)
    scaled, grad_value, dots, gain_term = attend_back(qkv_raw, inverses, gain_heads, tables, own_heads, grad_att)
    scaled = after(scaled, output_term)
    means = group_total(dots) * (1.0 / width)
    grad_qkv, grad_input = finish(qkv_raw, inverses, means, scaled, grad_value, seq_len, own_heads, w_qkv)

    qkv_term = weight_term(x_wide, grad_qkv)((output_term,))
    moved, _ = group_scatter(after(grad_input, qkv_term))
    grad_input = grad_hidden + moved
    returned = lax.all_to_all(
        grad_input.astype(BF).reshape(micro_count, seq_len, width),
        ALL,
        split_axis=1,
        concat_axis=0,
        tiled=True,
    )
    input_grad = jnp.zeros_like(tokens).at[dealing].set(returned)

    qkv_rows = owners(after(qkv_term, unit_part))
    qkv_back = group_exchange(qkv_rows.reshape(PLANE, shard, 3 * own_width), place)

    output_part = owners(after(output_term.reshape(groups * shard, width), qkv_back))

    def heads_in(columns):
        split = columns.reshape(fan, spread, shard, own_heads, head_dim)
        return split.transpose(2, 1, 3, 0, 4).reshape(shard, width).astype(F32)

    query_part = heads_in(qkv_back[:, :, :own_width])
    key_part = heads_in(qkv_back[:, :, own_width : 2 * own_width])
    value_part = heads_in(qkv_back[:, :, 2 * own_width :])

    placed = jnp.zeros((2, spread, own_heads, fan, head_dim), F32)
    own = gain_term.reshape(2, 1, own_heads, 1, head_dim)
    placed = lax.dynamic_update_slice(placed, own, (0, lane, 0, lead, 0)).reshape(2, width)
    gain_terms = jnp.concatenate([placed, jnp.stack([grad_gain_attn, grad_gain_mlp])])
    gain_terms = gain_terms.reshape(4, total, shard).transpose(1, 0, 2)
    gain_part = jnp.sum(
        lax.all_to_all(gain_terms, ALL, split_axis=0, concat_axis=0, tiled=True), axis=0
    )
    return (
        block_out,
        input_grad,
        query_part,
        key_part,
        value_part,
        output_part.astype(F32),
        gain_part[0],
        gain_part[1],
        gain_part[2],
        unit_part[:units].astype(F32).T,
        unit_part[units:].astype(F32).T,
        down_part.astype(F32),
        gain_part[3],
    )


def solution(mesh):
    count = mesh.devices.size
    inner = Mesh(mesh.devices.reshape(LINE, count // (LINE * PLANE), 2, 2, 2), ALL)
    first, second = P(ALL, None), P(None, ALL)
    vector = P(ALL)
    placed = (
        P(None, ALL, None),
        P(),
        P(),
        first,
        first,
        first,
        first,
        vector,
        vector,
        vector,
        second,
        second,
        first,
        vector,
        P(ALL, None, None),
    )
    return jax.shard_map(
        per_device,
        mesh=inner,
        in_specs=placed,
        out_specs=(
            P(ALL, None, None),
            P(None, ALL, None),
            first,
            first,
            first,
            first,
            vector,
            vector,
            vector,
            second,
            second,
            first,
            vector,
        ),
        check_vma=False,
    )
```

```python
import math

import jax
import jax.numpy as jnp
from jax import lax
from jax.experimental import pallas as pl
from jax.experimental.pallas import tpu as pltpu
from jax.sharding import Mesh
from jax.sharding import PartitionSpec as P

HEADS = 16
PLANE = 8
BF = jnp.bfloat16
F32 = jnp.float32

norm_eps = 1e-06
rope_base = 500000.0

ALL = ("z", "m", "y", "x", "c")
GROUP = ("y", "x", "c")
REST = ("z", "m")
LINE = 4
SWAP = [(0, 1), (1, 0)]


def swap(value, axis):
    return lax.ppermute(value, axis, SWAP)


def rotary_tables(length, head_dim):
    half_dim = head_dim // 2
    exponents = jnp.arange(half_dim, dtype=F32) * (2.0 / head_dim)
    frequency = jnp.power(F32(rope_base), -exponents)
    angles = jnp.arange(length, dtype=F32)[:, None] * frequency[None, :]
    return (jnp.cos(angles), jnp.sin(angles))


def wide_tables(length, head_dim):
    cosines, sines = rotary_tables(length, head_dim)
    return (
        jnp.concatenate([cosines, cosines], axis=1),
        jnp.concatenate([-sines, sines], axis=1),
    )


def by_rows(vector, columns):
    return jnp.broadcast_to(vector, (columns, vector.shape[1])).T


def row_sums(values):
    return jnp.sum(values.T, axis=0, keepdims=True)


def matmul(left, right, left_dim=1, right_dim=0):
    return lax.dot_general(left, right, (((left_dim,), (right_dim,)), ((), ())), preferred_element_type=F32)


def turn(values, cosines, sines):
    return values * cosines + pltpu.roll(values, values.shape[1] // 2, 1) * sines


def project_kernel(parts, x_ref, w_ref, raw_ref, squares_ref):
    raw = matmul(x_ref[...], w_ref[...])
    raw_ref[...] = raw
    width = raw.shape[1] // 3
    step = raw.shape[0] // parts
    for part in range(parts):
        rows = slice(part * step, (part + 1) * step)
        for kind in range(2):
            piece = raw[rows, kind * width : (kind + 1) * width]
            squares_ref[kind : kind + 1, rows] = row_sums(piece * piece)


def project(x_wide, weight, seq_len):
    wide, width = x_wide.shape
    out = weight.shape[1]
    block = 2 * seq_len
    return pl.pallas_call(
        lambda *refs: project_kernel(2, *refs),
        grid=(wide // block,),
        in_specs=[pl.BlockSpec((block, width), lambda i: (i, 0)), pl.BlockSpec((width, out), lambda i: (0, 0))],
        out_specs=[pl.BlockSpec((block, out), lambda i: (i, 0)), pl.BlockSpec((2, block), lambda i: (0, i))],
        out_shape=[jax.ShapeDtypeStruct((wide, out), F32), jax.ShapeDtypeStruct((2, wide), F32)],
        cost_estimate=pl.CostEstimate(
            flops=2 * wide * width * out, bytes_accessed=2 * wide * width + 2 * width * out + 4 * wide * out, transcendentals=0
        ),
        name="project",
    )(x_wide, weight)


def soften(scores, causal):
    scores = jnp.where(causal, scores, -1e30)
    exps = jnp.exp(scores - jnp.max(scores, axis=1, keepdims=True))
    return exps * (1.0 / jnp.sum(exps, axis=1, keepdims=True))


def causal_mask(length):
    rows = lax.broadcasted_iota(jnp.int32, (length, length), 0)
    return lax.broadcasted_iota(jnp.int32, (length, length), 1) <= rows


def heads_of(raw_ref, inverses, gain_ref, cosines, sines, rows, head, heads):
    dim = cosines.shape[1]
    out = []
    for kind in range(2):
        at = (kind * heads + head) * dim
        normed = raw_ref[rows, at : at + dim] * inverses[kind]
        gain = gain_ref[kind : kind + 1, head * dim : (head + 1) * dim]
        out += [normed, turn(normed * gain, cosines, sines).astype(BF), gain]
    at = (2 * heads + head) * dim
    return out + [raw_ref[rows, at : at + dim].astype(BF)]


def attend_kernel(heads, parts, scale, raw_ref, inv_ref, gain_ref, cos_ref, sin_ref, out_ref):
    cosines, sines = cos_ref[...], sin_ref[...]
    length, dim = cosines.shape
    causal = causal_mask(length)
    for part in range(parts):
        rows = slice(part * length, (part + 1) * length)
        inverses = [by_rows(inv_ref[kind : kind + 1, rows], dim) for kind in range(2)]
        for head in range(heads):
            _, query, _, _, key, _, value = heads_of(raw_ref, inverses, gain_ref, cosines, sines, rows, head, heads)
            soft = soften(matmul(query, key, 1, 1) * scale, causal)
            out_ref[rows, head * dim : (head + 1) * dim] = matmul(soft.astype(BF), value).astype(BF)


def attend_back_kernel(
    heads, parts, scale, raw_ref, inv_ref, gain_ref, cos_ref, sin_ref, grad_ref, scaled_ref, value_ref, dots_ref, gains_ref
):
    cosines, sines = cos_ref[...], sin_ref[...]
    length, dim = cosines.shape
    causal = causal_mask(length)

    @pl.when(pl.program_id(0) == 0)
    def _():
        gains_ref[...] = jnp.zeros_like(gains_ref)

    for part in range(parts):
        rows = slice(part * length, (part + 1) * length)
        inverses = [by_rows(inv_ref[kind : kind + 1, rows], dim) for kind in range(2)]
        dots = [0.0, 0.0]
        for head in range(heads):
            query_normed, query, query_gain, key_normed, key, key_gain, value = heads_of(
                raw_ref, inverses, gain_ref, cosines, sines, rows, head, heads
            )
            columns = slice(head * dim, (head + 1) * dim)
            soft = soften(matmul(query, key, 1, 1) * scale, causal)
            grad = grad_ref[rows, columns]
            grad_soft = matmul(grad, value, 1, 1)
            delta = jnp.sum(soft * grad_soft, axis=1, keepdims=True)
            grad_scores = (soft * (grad_soft - delta)).astype(BF)
            value_ref[rows, columns] = matmul(soft.astype(BF), grad, 0, 0).astype(BF)
            turned = (matmul(grad_scores, key) * scale, matmul(grad_scores, query, 0, 0) * scale)
            for kind, normed, gain in ((0, query_normed, query_gain), (1, key_normed, key_gain)):
                back = turn(turned[kind], cosines, -sines)
                gains_ref[kind : kind + 1, columns] += jnp.sum(normed * back, axis=0, keepdims=True)
                scaled = back * gain
                scaled_ref[rows, (kind * heads + head) * dim : (kind * heads + head + 1) * dim] = scaled
                dots[kind] = dots[kind] + scaled * normed
        for kind in range(2):
            dots_ref[kind : kind + 1, rows] = row_sums(dots[kind])


def finish_kernel(heads, parts, length, raw_ref, inv_ref, means_ref, scaled_ref, value_ref, weight_ref, out_ref, input_ref):
    width = value_ref.shape[1]
    for part in range(parts):
        rows = slice(part * length, (part + 1) * length)
        for kind in range(2):
            columns = slice(kind * width, (kind + 1) * width)
            inverse = by_rows(inv_ref[kind : kind + 1, rows], width)
            mean = by_rows(means_ref[kind : kind + 1, rows], width)
            normed = raw_ref[rows, columns] * inverse
            out_ref[rows, columns] = (inverse * (scaled_ref[rows, columns] - normed * mean)).astype(BF)
        out_ref[rows, 2 * width :] = value_ref[rows, :]
    input_ref[...] = matmul(out_ref[...], weight_ref[...], 1, 1).astype(BF)


def block_specs(block, heads, dim, length):
    own = heads * dim
    rows = lambda columns: pl.BlockSpec((block, columns), lambda i: (i, 0))
    lanes = pl.BlockSpec((2, block), lambda i: (0, i))
    fixed = lambda shape: pl.BlockSpec(shape, lambda i: (0, 0))
    return own, rows, lanes, [rows(3 * own), lanes, fixed((2, own)), fixed((length, dim)), fixed((length, dim))]


def attend(raw, inverses, gains, tables, heads):
    length, dim = tables[0].shape
    wide = raw.shape[0]
    block = 2 * length
    own, rows, _, specs = block_specs(block, heads, dim, length)
    return pl.pallas_call(
        lambda *refs: attend_kernel(heads, 2, 1.0 / math.sqrt(dim), *refs),
        grid=(wide // block,),
        in_specs=specs,
        out_specs=rows(own),
        out_shape=jax.ShapeDtypeStruct((wide, own), BF),
        cost_estimate=pl.CostEstimate(
            flops=4 * wide * length * own, bytes_accessed=14 * wide * own, transcendentals=wide * length * heads
        ),
        name="attend",
    )(raw, inverses, gains, *tables)


def attend_back(raw, inverses, gains, tables, heads, grad):
    length, dim = tables[0].shape
    wide = raw.shape[0]
    block = 2 * length
    own, rows, lanes, specs = block_specs(block, heads, dim, length)
    return pl.pallas_call(
        lambda *refs: attend_back_kernel(heads, 2, 1.0 / math.sqrt(dim), *refs),
        grid=(wide // block,),
        in_specs=specs + [rows(own)],
        out_specs=[rows(2 * own), rows(own), lanes, pl.BlockSpec((2, own), lambda i: (0, 0))],
        out_shape=[
            jax.ShapeDtypeStruct((wide, 2 * own), F32),
            jax.ShapeDtypeStruct((wide, own), BF),
            jax.ShapeDtypeStruct((2, wide), F32),
            jax.ShapeDtypeStruct((2, own), F32),
        ],
        cost_estimate=pl.CostEstimate(
            flops=10 * wide * length * own, bytes_accessed=26 * wide * own, transcendentals=wide * length * heads
        ),
        name="attend_back",
    )(raw, inverses, gains, *tables, grad)


def finish(raw, inverses, means, scaled, value, length, heads, weight):
    wide, own = value.shape
    block = 2 * length
    rows = lambda columns: pl.BlockSpec((block, columns), lambda i: (i, 0))
    lanes = pl.BlockSpec((2, block), lambda i: (0, i))
    return pl.pallas_call(
        lambda *refs: finish_kernel(heads, 2, length, *refs),
        grid=(wide // block,),
        in_specs=[rows(3 * own), lanes, lanes, rows(2 * own), rows(own), pl.BlockSpec(weight.shape, lambda i: (0, 0))],
        out_specs=[rows(3 * own), rows(weight.shape[0])],
        out_shape=[jax.ShapeDtypeStruct((wide, 3 * own), BF), jax.ShapeDtypeStruct((wide, weight.shape[0]), BF)],
        cost_estimate=pl.CostEstimate(
            flops=2 * wide * weight.size, bytes_accessed=28 * wide * own + 2 * wide * weight.shape[0], transcendentals=0
        ),
        name="finish",
    )(raw, inverses, means, scaled, value, weight)


def after(value, *earlier):
    return lax.optimization_barrier((value,) + earlier)[0]


def group_gather(block, meanwhile=None):
    half = block.shape[0] // 2
    over_x, over_y = swap(block, "x"), swap(block, "y")
    near_x, near_y = over_x[:half], over_y[half:]
    done = None
    if meanwhile is not None:
        done = meanwhile(block)
        near_x, near_y, _ = lax.optimization_barrier((near_x, near_y, done))
    pieces = [block, over_x, over_y, swap(near_x, "y"), swap(near_y, "x")]
    return jnp.concatenate(pieces + [swap(piece, "c") for piece in pieces], axis=0), over_x, done


def group_scatter(partial, meanwhile=None):
    wide = partial.shape[0] // 2
    rows = wide // 4
    half = rows // 2

    def both(i):
        away = swap(partial[wide + i * rows : wide + (i + 1) * rows], "c")
        return partial[i * rows : (i + 1) * rows].astype(F32) + away.astype(F32)

    def move(value, axis):
        return swap(value.astype(BF), axis).astype(F32)

    far, over_x, over_y, own = both(3), both(1), both(2), both(0)
    far_low, far_high = far[:half].astype(BF), far[half:].astype(BF)
    far_x, far_y = swap(far_low, "x"), swap(far_high, "y")
    done = None
    if meanwhile is not None:
        done = meanwhile(far_low)
        far_x, far_y, done = lax.optimization_barrier((far_x, far_y, done))
    over_y = jnp.concatenate([over_y[:half] + far_x.astype(F32), over_y[half:]])
    over_x = jnp.concatenate([over_x[:half], over_x[half:] + far_y.astype(F32)])
    return own + move(over_x, "x") + move(over_y, "y"), done


def gated_kernel(groups, hidden_ref, weight_ref, raw_ref, act_ref):
    raw = matmul(hidden_ref[...], weight_ref[...], 1, 1)
    raw_ref[...] = raw
    step = raw.shape[1] // (2 * groups)
    for i in range(groups):
        gate = raw[:, 2 * i * step : (2 * i + 1) * step]
        up = raw[:, (2 * i + 1) * step : (2 * i + 2) * step]
        act_ref[:, i * step : (i + 1) * step] = (gate * jax.nn.sigmoid(gate) * up).astype(BF)


def gated(hidden, weight, groups):
    wide, width = hidden.shape
    units = weight.shape[0]
    block = 256
    rows = lambda columns: pl.BlockSpec((block, columns), lambda i: (i, 0))
    return pl.pallas_call(
        lambda *refs: gated_kernel(groups, *refs),
        grid=(wide // block,),
        in_specs=[rows(width), pl.BlockSpec((units, width), lambda i: (0, 0))],
        out_specs=[rows(units), rows(units // 2)],
        out_shape=[jax.ShapeDtypeStruct((wide, units), F32), jax.ShapeDtypeStruct((wide, units // 2), BF)],
        cost_estimate=pl.CostEstimate(
            flops=2 * wide * width * units,
            bytes_accessed=2 * wide * width + 2 * units * width + 5 * wide * units,
            transcendentals=wide * units // 2,
        ),
        name="gated",
    )(hidden, weight)


def gated_back_kernel(groups, grad_ref, first_ref, second_ref, raw_ref, weight_ref, units_ref, hidden_ref):
    split = first_ref.shape[1]
    grad_act = matmul(grad_ref[:, :split], first_ref[...], 1, 1) + matmul(grad_ref[:, split:], second_ref[...], 1, 1)
    step = grad_act.shape[1] // groups
    for i in range(groups):
        gate = raw_ref[:, 2 * i * step : (2 * i + 1) * step]
        up = raw_ref[:, (2 * i + 1) * step : (2 * i + 2) * step]
        grad = grad_act[:, i * step : (i + 1) * step]
        sigma = jax.nn.sigmoid(gate)
        units_ref[:, 2 * i * step : (2 * i + 1) * step] = (
            grad * up * sigma * (1.0 + gate * (1.0 - sigma))
        ).astype(BF)
        units_ref[:, (2 * i + 1) * step : (2 * i + 2) * step] = (grad * (gate * sigma)).astype(BF)
    hidden_ref[...] = matmul(units_ref[...], weight_ref[...]).astype(BF)


def gated_back(grad, downs, raw, weight, groups):
    wide, width = grad.shape
    units = weight.shape[0]
    block = 256
    rows = lambda columns: pl.BlockSpec((block, columns), lambda i: (i, 0))
    fixed = lambda array: pl.BlockSpec(array.shape, lambda i: (0, 0))
    return pl.pallas_call(
        lambda *refs: gated_back_kernel(groups, *refs),
        grid=(wide // block,),
        in_specs=[rows(width), fixed(downs[0]), fixed(downs[1]), rows(units), fixed(weight)],
        out_specs=[rows(units), rows(width)],
        out_shape=[jax.ShapeDtypeStruct((wide, units), BF), jax.ShapeDtypeStruct((wide, width), BF)],
        cost_estimate=pl.CostEstimate(
            flops=3 * wide * width * units,
            bytes_accessed=4 * wide * width + 3 * units * width + 6 * wide * units,
            transcendentals=wide * units // 2,
        ),
        name="gated_back",
    )(grad, *downs, raw, weight)


def ring(ahead):
    return [(i, (i + ahead) % LINE) for i in range(LINE)]


def line_gather(block, at):
    out = jnp.zeros((LINE,) + block.shape, block.dtype)
    out = lax.dynamic_update_index_in_dim(out, block, at, 0)
    for ahead in range(1, LINE):
        moved = lax.ppermute(block, "z", ring(ahead))
        out = lax.dynamic_update_index_in_dim(out, moved, (at - ahead) % LINE, 0)
    return out


def group_exchange(blocks, place):
    out = jnp.zeros_like(blocks)
    out = lax.dynamic_update_index_in_dim(out, lax.dynamic_index_in_dim(blocks, place, 0), place, 0)
    for apart in range(1, PLANE):
        block = lax.dynamic_index_in_dim(blocks, place ^ apart, 0)
        moved = lax.ppermute(block, GROUP, [(i, i ^ apart) for i in range(PLANE)])
        out = lax.dynamic_update_index_in_dim(out, moved, place ^ apart, 0)
    return out


def group_total(value):
    kinds, wide = value.shape
    split = value.reshape(kinds, 2, 2, 2, wide // PLANE)
    for axis, dim in (("c", 1), ("x", 3), ("y", 2)):
        split = split + jnp.flip(swap(split, axis), dim)
    return split.reshape(kinds, wide)


def per_device(
    tokens,
    lengths,
    dealing,
    w_query,
    w_key,
    w_value,
    w_output,
    query_gain,
    key_gain,
    attn_gain,
    w_gate,
    w_up,
    w_down,
    mlp_gain,
    cotangent,
):
    groups = lax.axis_size(REST)
    total = groups * PLANE
    rank = lax.axis_index(ALL)
    place = lax.axis_index(GROUP)
    at = lax.axis_index("z")
    along = lax.axis_size("m")
    micro_count, seq_len, width = cotangent.shape
    rows = micro_count * seq_len
    wide = rows * PLANE
    shard = width // total
    head_dim = width // HEADS
    own_heads = HEADS // PLANE
    own_width = own_heads * head_dim
    spread = head_dim // shard
    head_axes = GROUP[3 - (spread.bit_length() - 1) :]
    fan = PLANE // spread
    lead, lane = place // spread, place % spread

    tables = wide_tables(seq_len, head_dim)
    positions = jnp.arange(seq_len, dtype=jnp.int32)

    def heads_out(weight):
        split = weight.reshape(shard, spread, own_heads, fan, head_dim)
        return split.transpose(3, 1, 0, 2, 4).reshape(PLANE, shard, own_width)

    outgoing = jnp.take(tokens, dealing, axis=0)
    arrived = lax.all_to_all(outgoing, ALL, split_axis=0, concat_axis=1, tiled=True)
    x_low = arrived.reshape(rows, width)

    w_query, w_key, w_value, outgoing = lax.optimization_barrier((w_query, w_key, w_value, outgoing))
    qkv_out = jnp.concatenate([heads_out(w_query), heads_out(w_key), heads_out(w_value)], axis=2)
    qkv_in = lax.all_to_all(qkv_out, GROUP, split_axis=0, concat_axis=0, tiled=True)

    gains = jnp.stack([query_gain, key_gain, attn_gain, mlp_gain])
    gains = lax.all_to_all(
        jnp.broadcast_to(gains[None], (total, 4, shard)), ALL, split_axis=0, concat_axis=0, tiled=True
    )
    gains = gains.transpose(1, 0, 2).reshape(4, width).astype(F32)
    by_head = gains[:2].reshape(2, spread, own_heads, fan, head_dim)
    by_head = lax.dynamic_index_in_dim(by_head, lane, 1, keepdims=False)
    by_head = lax.dynamic_index_in_dim(by_head, lead, 2, keepdims=False)
    gain_heads = by_head.reshape(2, own_width)
    gain_attn, gain_mlp = gains[2], gains[3]

    out_all = w_output
    if along > 1:
        out_all = lax.all_gather(out_all, "m", axis=0, tiled=True)
    out_all = line_gather(out_all, at).reshape(groups, shard, width)
    qkv_in = after(qkv_in, out_all)
    w_qkv = lax.all_gather(qkv_in, REST, axis=0, tiled=True).reshape(width, 3 * own_width)
    w_out = lax.all_to_all(out_all, head_axes, split_axis=0, concat_axis=1, tiled=True)
    w_out = w_out.reshape(own_width, width)

    units = w_gate.shape[1]
    gate_up = jnp.concatenate([w_gate.T, w_up.T])
    gate_up = lax.all_gather(after(gate_up, qkv_in), REST, axis=0, tiled=True)
    split = width // 2
    downs = [
        lax.all_gather(after(part, qkv_in), REST, axis=0, tiled=True)
        for part in (w_down[:, :split], w_down[:, split:])
    ]

    own_seqs = lax.dynamic_slice_in_dim(dealing, rank * micro_count, micro_count)
    own_lengths = jnp.take(lengths, own_seqs)
    valid_mask = (positions[None, :] < own_lengths[:, None]).astype(F32).reshape(rows, 1)

    x_wide, _, _ = group_gather(x_low)
    qkv_raw, squares = project(x_wide, w_qkv, seq_len)
    inverses = lax.rsqrt(group_total(squares) * (1.0 / width) + norm_eps)
    attended_low = attend(qkv_raw, inverses, gain_heads, tables, own_heads)
    out_raw, _ = group_scatter(jnp.dot(attended_low, w_out, preferred_element_type=F32).astype(BF))
    out_inv = lax.rsqrt(jnp.mean(out_raw * out_raw, axis=-1, keepdims=True) + norm_eps)
    out_normed = out_raw * out_inv
    hidden = x_low.astype(F32) + out_normed * gain_attn

    hidden_wide, _, _ = group_gather(hidden.astype(BF))
    contract_last = (((1,), (1,)), ((), ()))
    contract_rows = (((0,), (0,)), ((), ()))
    unit_raw, act_low = gated(hidden_wide, gate_up, groups)
    down_raws = []
    for part in downs:
        rows_in = after(act_low, *down_raws)
        down_raws.append(group_scatter(jnp.dot(rows_in, part, preferred_element_type=F32).astype(BF))[0])
    down_raw = jnp.concatenate(down_raws, axis=1)
    down_inv = lax.rsqrt(jnp.mean(down_raw * down_raw, axis=-1, keepdims=True) + norm_eps)
    down_normed = down_raw * down_inv
    block_out = (
        (valid_mask * (hidden + down_normed * gain_mlp)).astype(BF).reshape(micro_count, seq_len, width)
    )

    grad_out = valid_mask * cotangent.reshape(rows, width).astype(F32)
    grad_gain_mlp = jnp.sum(down_normed * grad_out, axis=0)
    scaled = grad_out * gain_mlp
    grad_down = down_inv * (scaled - down_normed * jnp.mean(scaled * down_normed, axis=-1, keepdims=True))
    grad_down_wide, _, _ = group_gather(grad_down.astype(BF))

    down_term = lax.dot_general(
        act_low, grad_down_wide, contract_rows, preferred_element_type=F32
    ).astype(BF)
    grad_units, hidden_term = gated_back(after(grad_down_wide, down_term), downs, unit_raw, gate_up, groups)

    def weight_term(left, right):
        return lambda token: lax.dot_general(
            after(left, *(token if isinstance(token, tuple) else (token,))), right, contract_rows, preferred_element_type=F32
        ).astype(BF)

    def owners(term):
        return lax.psum_scatter(term, REST, scatter_dimension=0, tiled=True)

    down_part = owners(down_term)
    moved, unit_term = group_scatter(hidden_term, weight_term(grad_units, hidden_wide))
    grad_hidden = grad_out + moved
    unit_part = owners(after(unit_term, down_part))

    grad_gain_attn = jnp.sum(out_normed * grad_hidden, axis=0)
    scaled = grad_hidden * gain_attn
    grad_out_raw = out_inv * (scaled - out_normed * jnp.mean(scaled * out_normed, axis=-1, keepdims=True))
    grad_out_low = grad_out_raw.astype(BF)
    grad_out_wide, _, _ = group_gather(grad_out_low)

    output_term = lax.dot_general(
        attended_low, grad_out_wide, contract_rows, preferred_element_type=F32
    ).astype(BF)
    grad_out_wide = after(grad_out_wide, output_term)
    output_term = lax.all_to_all(
        output_term.reshape(own_heads, head_dim, width),
        head_axes,
        split_axis=1,
        concat_axis=0,
        tiled=True,
    )

    grad_att = lax.dot_general(grad_out_wide, w_out, contract_last, preferred_element_type=F32).astype(BF)
    scaled, grad_value, dots, gain_term = attend_back(qkv_raw, inverses, gain_heads, tables, own_heads, grad_att)
    scaled = after(scaled, output_term)
    means = group_total(dots) * (1.0 / width)
    grad_qkv, grad_input = finish(qkv_raw, inverses, means, scaled, grad_value, seq_len, own_heads, w_qkv)

    qkv_term = weight_term(x_wide, grad_qkv)((output_term,))
    moved, _ = group_scatter(after(grad_input, qkv_term))
    grad_input = grad_hidden + moved
    returned = lax.all_to_all(
        grad_input.astype(BF).reshape(micro_count, seq_len, width),
        ALL,
        split_axis=1,
        concat_axis=0,
        tiled=True,
    )
    input_grad = jnp.zeros_like(tokens).at[dealing].set(returned)

    qkv_rows = owners(after(qkv_term, unit_part))
    qkv_back = group_exchange(qkv_rows.reshape(PLANE, shard, 3 * own_width), place)

    output_part = owners(after(output_term.reshape(groups * shard, width), qkv_back))

    def heads_in(columns):
        split = columns.reshape(fan, spread, shard, own_heads, head_dim)
        return split.transpose(2, 1, 3, 0, 4).reshape(shard, width).astype(F32)

    query_part = heads_in(qkv_back[:, :, :own_width])
    key_part = heads_in(qkv_back[:, :, own_width : 2 * own_width])
    value_part = heads_in(qkv_back[:, :, 2 * own_width :])

    placed = jnp.zeros((2, spread, own_heads, fan, head_dim), F32)
    own = gain_term.reshape(2, 1, own_heads, 1, head_dim)
    placed = lax.dynamic_update_slice(placed, own, (0, lane, 0, lead, 0)).reshape(2, width)
    gain_terms = jnp.concatenate([placed, jnp.stack([grad_gain_attn, grad_gain_mlp])])
    gain_terms = gain_terms.reshape(4, total, shard).transpose(1, 0, 2)
    gain_part = jnp.sum(
        lax.all_to_all(gain_terms, ALL, split_axis=0, concat_axis=0, tiled=True), axis=0
    )
    return (
        block_out,
        input_grad,
        query_part,
        key_part,
        value_part,
        output_part.astype(F32),
        gain_part[0],
        gain_part[1],
        gain_part[2],
        unit_part[:units].astype(F32).T,
        unit_part[units:].astype(F32).T,
        down_part.astype(F32),
        gain_part[3],
    )


def solution(mesh):
    count = mesh.devices.size
    inner = Mesh(mesh.devices.reshape(LINE, count // (LINE * PLANE), 2, 2, 2), ALL)
    first, second = P(ALL, None), P(None, ALL)
    vector = P(ALL)
    placed = (
        P(None, ALL, None),
        P(),
        P(),
        first,
        first,
        first,
        first,
        vector,
        vector,
        vector,
        second,
        second,
        first,
        vector,
        P(ALL, None, None),
    )
    return jax.shard_map(
        per_device,
        mesh=inner,
        in_specs=placed,
        out_specs=(
            P(ALL, None, None),
            P(None, ALL, None),
            first,
            first,
            first,
            first,
            vector,
            vector,
            vector,
            second,
            second,
            first,
            vector,
        ),
        check_vma=False,
    )
```

```python
import math

import jax
import jax.numpy as jnp
from jax import lax
from jax.experimental import pallas as pl
from jax.experimental.pallas import tpu as pltpu
from jax.sharding import Mesh
from jax.sharding import PartitionSpec as P

HEADS = 16
PLANE = 8
BF = jnp.bfloat16
F32 = jnp.float32

norm_eps = 1e-06
rope_base = 500000.0

ALL = ("z", "m", "y", "x", "c")
GROUP = ("y", "x", "c")
REST = ("z", "m")
LINE = 4
SWAP = [(0, 1), (1, 0)]


def swap(value, axis):
    return lax.ppermute(value, axis, SWAP)


def rotary_tables(length, head_dim):
    half_dim = head_dim // 2
    exponents = jnp.arange(half_dim, dtype=F32) * (2.0 / head_dim)
    frequency = jnp.power(F32(rope_base), -exponents)
    angles = jnp.arange(length, dtype=F32)[:, None] * frequency[None, :]
    return (jnp.cos(angles), jnp.sin(angles))


def wide_tables(length, head_dim):
    cosines, sines = rotary_tables(length, head_dim)
    return (
        jnp.concatenate([cosines, cosines], axis=1),
        jnp.concatenate([-sines, sines], axis=1),
    )


def by_rows(vector, columns):
    return jnp.broadcast_to(vector, (columns, vector.shape[1])).T


def row_sums(values):
    return jnp.sum(values.T, axis=0, keepdims=True)


def matmul(left, right, left_dim=1, right_dim=0):
    return lax.dot_general(left, right, (((left_dim,), (right_dim,)), ((), ())), preferred_element_type=F32)


def turn(values, cosines, sines):
    return values * cosines + pltpu.roll(values, values.shape[1] // 2, 1) * sines


def project_kernel(parts, x_ref, w_ref, raw_ref, squares_ref):
    raw = matmul(x_ref[...], w_ref[...])
    raw_ref[...] = raw
    width = raw.shape[1] // 3
    step = raw.shape[0] // parts
    for part in range(parts):
        rows = slice(part * step, (part + 1) * step)
        for kind in range(2):
            piece = raw[rows, kind * width : (kind + 1) * width]
            squares_ref[kind : kind + 1, rows] = row_sums(piece * piece)


def project(x_wide, weight, seq_len):
    wide, width = x_wide.shape
    out = weight.shape[1]
    block = 2 * seq_len
    return pl.pallas_call(
        lambda *refs: project_kernel(2, *refs),
        grid=(wide // block,),
        in_specs=[pl.BlockSpec((block, width), lambda i: (i, 0)), pl.BlockSpec((width, out), lambda i: (0, 0))],
        out_specs=[pl.BlockSpec((block, out), lambda i: (i, 0)), pl.BlockSpec((2, block), lambda i: (0, i))],
        out_shape=[jax.ShapeDtypeStruct((wide, out), F32), jax.ShapeDtypeStruct((2, wide), F32)],
        cost_estimate=pl.CostEstimate(
            flops=2 * wide * width * out, bytes_accessed=2 * wide * width + 2 * width * out + 4 * wide * out, transcendentals=0
        ),
        name="project",
    )(x_wide, weight)


def soften(scores, causal):
    scores = jnp.where(causal, scores, -1e30)
    exps = jnp.exp(scores - jnp.max(scores, axis=1, keepdims=True))
    return exps * (1.0 / jnp.sum(exps, axis=1, keepdims=True))


def causal_mask(length):
    rows = lax.broadcasted_iota(jnp.int32, (length, length), 0)
    return lax.broadcasted_iota(jnp.int32, (length, length), 1) <= rows


def heads_of(raw_ref, inverses, gain_ref, cosines, sines, rows, head, heads):
    dim = cosines.shape[1]
    out = []
    for kind in range(2):
        at = (kind * heads + head) * dim
        normed = raw_ref[rows, at : at + dim] * inverses[kind]
        gain = gain_ref[kind : kind + 1, head * dim : (head + 1) * dim]
        out += [normed, turn(normed * gain, cosines, sines).astype(BF), gain]
    at = (2 * heads + head) * dim
    return out + [raw_ref[rows, at : at + dim].astype(BF)]


def attend_kernel(heads, parts, scale, raw_ref, inv_ref, gain_ref, cos_ref, sin_ref, out_ref):
    cosines, sines = cos_ref[...], sin_ref[...]
    length, dim = cosines.shape
    causal = causal_mask(length)
    for part in range(parts):
        rows = slice(part * length, (part + 1) * length)
        inverses = [by_rows(inv_ref[kind : kind + 1, rows], dim) for kind in range(2)]
        for head in range(heads):
            _, query, _, _, key, _, value = heads_of(raw_ref, inverses, gain_ref, cosines, sines, rows, head, heads)
            soft = soften(matmul(query, key, 1, 1) * scale, causal)
            out_ref[rows, head * dim : (head + 1) * dim] = matmul(soft.astype(BF), value).astype(BF)


def attend_back_kernel(
    heads, parts, scale, raw_ref, inv_ref, gain_ref, cos_ref, sin_ref, grad_ref, scaled_ref, value_ref, dots_ref, gains_ref
):
    cosines, sines = cos_ref[...], sin_ref[...]
    length, dim = cosines.shape
    causal = causal_mask(length)

    @pl.when(pl.program_id(0) == 0)
    def _():
        gains_ref[...] = jnp.zeros_like(gains_ref)

    for part in range(parts):
        rows = slice(part * length, (part + 1) * length)
        inverses = [by_rows(inv_ref[kind : kind + 1, rows], dim) for kind in range(2)]
        dots = [0.0, 0.0]
        for head in range(heads):
            query_normed, query, query_gain, key_normed, key, key_gain, value = heads_of(
                raw_ref, inverses, gain_ref, cosines, sines, rows, head, heads
            )
            columns = slice(head * dim, (head + 1) * dim)
            soft = soften(matmul(query, key, 1, 1) * scale, causal)
            grad = grad_ref[rows, columns]
            grad_soft = matmul(grad, value, 1, 1)
            delta = jnp.sum(soft * grad_soft, axis=1, keepdims=True)
            grad_scores = (soft * (grad_soft - delta)).astype(BF)
            value_ref[rows, columns] = matmul(soft.astype(BF), grad, 0, 0).astype(BF)
            turned = (matmul(grad_scores, key) * scale, matmul(grad_scores, query, 0, 0) * scale)
            for kind, normed, gain in ((0, query_normed, query_gain), (1, key_normed, key_gain)):
                back = turn(turned[kind], cosines, -sines)
                gains_ref[kind : kind + 1, columns] += jnp.sum(normed * back, axis=0, keepdims=True)
                scaled = back * gain
                scaled_ref[rows, (kind * heads + head) * dim : (kind * heads + head + 1) * dim] = scaled
                dots[kind] = dots[kind] + scaled * normed
        for kind in range(2):
            dots_ref[kind : kind + 1, rows] = row_sums(dots[kind])


def finish_kernel(heads, parts, length, raw_ref, inv_ref, means_ref, scaled_ref, value_ref, weight_ref, out_ref, input_ref):
    width = value_ref.shape[1]
    for part in range(parts):
        rows = slice(part * length, (part + 1) * length)
        for kind in range(2):
            columns = slice(kind * width, (kind + 1) * width)
            inverse = by_rows(inv_ref[kind : kind + 1, rows], width)
            mean = by_rows(means_ref[kind : kind + 1, rows], width)
            normed = raw_ref[rows, columns] * inverse
            out_ref[rows, columns] = (inverse * (scaled_ref[rows, columns] - normed * mean)).astype(BF)
        out_ref[rows, 2 * width :] = value_ref[rows, :]
    input_ref[...] = matmul(out_ref[...], weight_ref[...], 1, 1).astype(BF)


def block_specs(block, heads, dim, length):
    own = heads * dim
    rows = lambda columns: pl.BlockSpec((block, columns), lambda i: (i, 0))
    lanes = pl.BlockSpec((2, block), lambda i: (0, i))
    fixed = lambda shape: pl.BlockSpec(shape, lambda i: (0, 0))
    return own, rows, lanes, [rows(3 * own), lanes, fixed((2, own)), fixed((length, dim)), fixed((length, dim))]


def attend(raw, inverses, gains, tables, heads):
    length, dim = tables[0].shape
    wide = raw.shape[0]
    block = 2 * length
    own, rows, _, specs = block_specs(block, heads, dim, length)
    return pl.pallas_call(
        lambda *refs: attend_kernel(heads, 2, 1.0 / math.sqrt(dim), *refs),
        grid=(wide // block,),
        in_specs=specs,
        out_specs=rows(own),
        out_shape=jax.ShapeDtypeStruct((wide, own), BF),
        cost_estimate=pl.CostEstimate(
            flops=4 * wide * length * own, bytes_accessed=14 * wide * own, transcendentals=wide * length * heads
        ),
        name="attend",
    )(raw, inverses, gains, *tables)


def attend_back(raw, inverses, gains, tables, heads, grad):
    length, dim = tables[0].shape
    wide = raw.shape[0]
    block = 2 * length
    own, rows, lanes, specs = block_specs(block, heads, dim, length)
    return pl.pallas_call(
        lambda *refs: attend_back_kernel(heads, 2, 1.0 / math.sqrt(dim), *refs),
        grid=(wide // block,),
        in_specs=specs + [rows(own)],
        out_specs=[rows(2 * own), rows(own), lanes, pl.BlockSpec((2, own), lambda i: (0, 0))],
        out_shape=[
            jax.ShapeDtypeStruct((wide, 2 * own), F32),
            jax.ShapeDtypeStruct((wide, own), BF),
            jax.ShapeDtypeStruct((2, wide), F32),
            jax.ShapeDtypeStruct((2, own), F32),
        ],
        cost_estimate=pl.CostEstimate(
            flops=10 * wide * length * own, bytes_accessed=26 * wide * own, transcendentals=wide * length * heads
        ),
        name="attend_back",
    )(raw, inverses, gains, *tables, grad)


def finish(raw, inverses, means, scaled, value, length, heads, weight):
    wide, own = value.shape
    block = 2 * length
    rows = lambda columns: pl.BlockSpec((block, columns), lambda i: (i, 0))
    lanes = pl.BlockSpec((2, block), lambda i: (0, i))
    return pl.pallas_call(
        lambda *refs: finish_kernel(heads, 2, length, *refs),
        grid=(wide // block,),
        in_specs=[rows(3 * own), lanes, lanes, rows(2 * own), rows(own), pl.BlockSpec(weight.shape, lambda i: (0, 0))],
        out_specs=[rows(3 * own), rows(weight.shape[0])],
        out_shape=[jax.ShapeDtypeStruct((wide, 3 * own), BF), jax.ShapeDtypeStruct((wide, weight.shape[0]), BF)],
        cost_estimate=pl.CostEstimate(
            flops=2 * wide * weight.size, bytes_accessed=28 * wide * own + 2 * wide * weight.shape[0], transcendentals=0
        ),
        name="finish",
    )(raw, inverses, means, scaled, value, weight)


def after(value, *earlier):
    return lax.optimization_barrier((value,) + earlier)[0]


def group_gather(block, meanwhile=None):
    half = block.shape[0] // 2
    over_x, over_y = swap(block, "x"), swap(block, "y")
    near_x, near_y = over_x[:half], over_y[half:]
    done = None
    if meanwhile is not None:
        done = meanwhile(block)
        near_x, near_y, _ = lax.optimization_barrier((near_x, near_y, done))
    pieces = [block, over_x, over_y, swap(near_x, "y"), swap(near_y, "x")]
    return jnp.concatenate(pieces + [swap(piece, "c") for piece in pieces], axis=0), over_x, done


def group_scatter(partial, meanwhile=None):
    wide = partial.shape[0] // 2
    rows = wide // 4
    half = rows // 2

    def both(i):
        away = swap(partial[wide + i * rows : wide + (i + 1) * rows], "c")
        return partial[i * rows : (i + 1) * rows].astype(F32) + away.astype(F32)

    def move(value, axis):
        return swap(value.astype(BF), axis).astype(F32)

    far, over_x, over_y, own = both(3), both(1), both(2), both(0)
    far_low, far_high = far[:half].astype(BF), far[half:].astype(BF)
    far_x, far_y = swap(far_low, "x"), swap(far_high, "y")
    done = None
    if meanwhile is not None:
        done = meanwhile(far_low)
        far_x, far_y, done = lax.optimization_barrier((far_x, far_y, done))
    over_y = jnp.concatenate([over_y[:half] + far_x.astype(F32), over_y[half:]])
    over_x = jnp.concatenate([over_x[:half], over_x[half:] + far_y.astype(F32)])
    return own + move(over_x, "x") + move(over_y, "y"), done


def gated_kernel(groups, hidden_ref, weight_ref, raw_ref, act_ref):
    raw = matmul(hidden_ref[...], weight_ref[...], 1, 1)
    raw_ref[...] = raw
    step = raw.shape[1] // (2 * groups)
    for i in range(groups):
        gate = raw[:, 2 * i * step : (2 * i + 1) * step]
        up = raw[:, (2 * i + 1) * step : (2 * i + 2) * step]
        act_ref[:, i * step : (i + 1) * step] = (gate * jax.nn.sigmoid(gate) * up).astype(BF)


def gated(hidden, weight, groups):
    wide, width = hidden.shape
    units = weight.shape[0]
    block = 256
    rows = lambda columns: pl.BlockSpec((block, columns), lambda i: (i, 0))
    return pl.pallas_call(
        lambda *refs: gated_kernel(groups, *refs),
        grid=(wide // block,),
        in_specs=[rows(width), pl.BlockSpec((units, width), lambda i: (0, 0))],
        out_specs=[rows(units), rows(units // 2)],
        out_shape=[jax.ShapeDtypeStruct((wide, units), F32), jax.ShapeDtypeStruct((wide, units // 2), BF)],
        cost_estimate=pl.CostEstimate(
            flops=2 * wide * width * units,
            bytes_accessed=2 * wide * width + 2 * units * width + 5 * wide * units,
            transcendentals=wide * units // 2,
        ),
        name="gated",
    )(hidden, weight)


def gated_back_kernel(groups, grad_ref, first_ref, second_ref, raw_ref, weight_ref, units_ref, hidden_ref):
    split = first_ref.shape[1]
    grad_act = matmul(grad_ref[:, :split], first_ref[...], 1, 1) + matmul(grad_ref[:, split:], second_ref[...], 1, 1)
    step = grad_act.shape[1] // groups
    for i in range(groups):
        gate = raw_ref[:, 2 * i * step : (2 * i + 1) * step]
        up = raw_ref[:, (2 * i + 1) * step : (2 * i + 2) * step]
        grad = grad_act[:, i * step : (i + 1) * step]
        sigma = jax.nn.sigmoid(gate)
        units_ref[:, 2 * i * step : (2 * i + 1) * step] = (
            grad * up * sigma * (1.0 + gate * (1.0 - sigma))
        ).astype(BF)
        units_ref[:, (2 * i + 1) * step : (2 * i + 2) * step] = (grad * (gate * sigma)).astype(BF)
    hidden_ref[...] = matmul(units_ref[...], weight_ref[...]).astype(BF)


def gated_back(grad, downs, raw, weight, groups):
    wide, width = grad.shape
    units = weight.shape[0]
    block = 256
    rows = lambda columns: pl.BlockSpec((block, columns), lambda i: (i, 0))
    fixed = lambda array: pl.BlockSpec(array.shape, lambda i: (0, 0))
    return pl.pallas_call(
        lambda *refs: gated_back_kernel(groups, *refs),
        grid=(wide // block,),
        in_specs=[rows(width), fixed(downs[0]), fixed(downs[1]), rows(units), fixed(weight)],
        out_specs=[rows(units), rows(width)],
        out_shape=[jax.ShapeDtypeStruct((wide, units), BF), jax.ShapeDtypeStruct((wide, width), BF)],
        cost_estimate=pl.CostEstimate(
            flops=3 * wide * width * units,
            bytes_accessed=4 * wide * width + 3 * units * width + 6 * wide * units,
            transcendentals=wide * units // 2,
        ),
        name="gated_back",
    )(grad, *downs, raw, weight)


def ring(ahead):
    return [(i, (i + ahead) % LINE) for i in range(LINE)]


def line_gather(block, at):
    out = jnp.zeros((LINE,) + block.shape, block.dtype)
    out = lax.dynamic_update_index_in_dim(out, block, at, 0)
    for ahead in range(1, LINE):
        moved = lax.ppermute(block, "z", ring(ahead))
        out = lax.dynamic_update_index_in_dim(out, moved, (at - ahead) % LINE, 0)
    return out


def group_exchange(blocks, place):
    out = jnp.zeros_like(blocks)
    out = lax.dynamic_update_index_in_dim(out, lax.dynamic_index_in_dim(blocks, place, 0), place, 0)
    for apart in range(1, PLANE):
        block = lax.dynamic_index_in_dim(blocks, place ^ apart, 0)
        moved = lax.ppermute(block, GROUP, [(i, i ^ apart) for i in range(PLANE)])
        if apart == 1:
            token = moved
        out = lax.dynamic_update_index_in_dim(out, moved, place ^ apart, 0)
    return out, token


def group_total(value):
    kinds, wide = value.shape
    split = value.reshape(kinds, 2, 2, 2, wide // PLANE)
    for axis, dim in (("c", 1), ("x", 3), ("y", 2)):
        split = split + jnp.flip(swap(split, axis), dim)
    return split.reshape(kinds, wide)


def per_device(
    tokens,
    lengths,
    dealing,
    w_query,
    w_key,
    w_value,
    w_output,
    query_gain,
    key_gain,
    attn_gain,
    w_gate,
    w_up,
    w_down,
    mlp_gain,
    cotangent,
):
    groups = lax.axis_size(REST)
    total = groups * PLANE
    rank = lax.axis_index(ALL)
    place = lax.axis_index(GROUP)
    at = lax.axis_index("z")
    along = lax.axis_size("m")
    micro_count, seq_len, width = cotangent.shape
    rows = micro_count * seq_len
    wide = rows * PLANE
    shard = width // total
    head_dim = width // HEADS
    own_heads = HEADS // PLANE
    own_width = own_heads * head_dim
    spread = head_dim // shard
    head_axes = GROUP[3 - (spread.bit_length() - 1) :]
    fan = PLANE // spread
    lead, lane = place // spread, place % spread

    tables = wide_tables(seq_len, head_dim)
    positions = jnp.arange(seq_len, dtype=jnp.int32)

    def heads_out(weight):
        split = weight.reshape(shard, spread, own_heads, fan, head_dim)
        return split.transpose(3, 1, 0, 2, 4).reshape(PLANE, shard, own_width)

    outgoing = jnp.take(tokens, dealing, axis=0)
    arrived = lax.all_to_all(outgoing, ALL, split_axis=0, concat_axis=1, tiled=True)
    x_low = arrived.reshape(rows, width)

    w_query, w_key, w_value, outgoing = lax.optimization_barrier((w_query, w_key, w_value, outgoing))
    qkv_out = jnp.concatenate([heads_out(w_query), heads_out(w_key), heads_out(w_value)], axis=2)
    qkv_in = lax.all_to_all(qkv_out, GROUP, split_axis=0, concat_axis=0, tiled=True)

    gains = jnp.stack([query_gain, key_gain, attn_gain, mlp_gain])
    gains = lax.all_to_all(
        jnp.broadcast_to(gains[None], (total, 4, shard)), ALL, split_axis=0, concat_axis=0, tiled=True
    )
    gains = gains.transpose(1, 0, 2).reshape(4, width).astype(F32)
    by_head = gains[:2].reshape(2, spread, own_heads, fan, head_dim)
    by_head = lax.dynamic_index_in_dim(by_head, lane, 1, keepdims=False)
    by_head = lax.dynamic_index_in_dim(by_head, lead, 2, keepdims=False)
    gain_heads = by_head.reshape(2, own_width)
    gain_attn, gain_mlp = gains[2], gains[3]

    out_all = w_output
    if along > 1:
        out_all = lax.all_gather(out_all, "m", axis=0, tiled=True)
    out_all = line_gather(out_all, at).reshape(groups, shard, width)
    qkv_in = after(qkv_in, out_all)
    w_qkv = lax.all_gather(qkv_in, REST, axis=0, tiled=True).reshape(width, 3 * own_width)
    w_out = lax.all_to_all(out_all, head_axes, split_axis=0, concat_axis=1, tiled=True)
    w_out = w_out.reshape(own_width, width)

    units = w_gate.shape[1]
    gate_up = jnp.concatenate([w_gate.T, w_up.T])
    gate_up = lax.all_gather(after(gate_up, qkv_in), REST, axis=0, tiled=True)
    split = width // 2
    downs = [
        lax.all_gather(after(part, qkv_in), REST, axis=0, tiled=True)
        for part in (w_down[:, :split], w_down[:, split:])
    ]

    own_seqs = lax.dynamic_slice_in_dim(dealing, rank * micro_count, micro_count)
    own_lengths = jnp.take(lengths, own_seqs)
    valid_mask = (positions[None, :] < own_lengths[:, None]).astype(F32).reshape(rows, 1)

    x_wide, _, _ = group_gather(x_low)
    qkv_raw, squares = project(x_wide, w_qkv, seq_len)
    inverses = lax.rsqrt(group_total(squares) * (1.0 / width) + norm_eps)
    attended_low = attend(qkv_raw, inverses, gain_heads, tables, own_heads)
    out_raw, _ = group_scatter(jnp.dot(attended_low, w_out, preferred_element_type=F32).astype(BF))
    out_inv = lax.rsqrt(jnp.mean(out_raw * out_raw, axis=-1, keepdims=True) + norm_eps)
    out_normed = out_raw * out_inv
    hidden = x_low.astype(F32) + out_normed * gain_attn

    hidden_wide, _, _ = group_gather(hidden.astype(BF))
    contract_last = (((1,), (1,)), ((), ()))
    contract_rows = (((0,), (0,)), ((), ()))
    unit_raw, act_low = gated(hidden_wide, gate_up, groups)
    down_raws = []
    for part in downs:
        rows_in = after(act_low, *down_raws)
        down_raws.append(group_scatter(jnp.dot(rows_in, part, preferred_element_type=F32).astype(BF))[0])
    down_raw = jnp.concatenate(down_raws, axis=1)
    down_inv = lax.rsqrt(jnp.mean(down_raw * down_raw, axis=-1, keepdims=True) + norm_eps)
    down_normed = down_raw * down_inv
    block_out = (
        (valid_mask * (hidden + down_normed * gain_mlp)).astype(BF).reshape(micro_count, seq_len, width)
    )

    grad_out = valid_mask * cotangent.reshape(rows, width).astype(F32)
    grad_gain_mlp = jnp.sum(down_normed * grad_out, axis=0)
    scaled = grad_out * gain_mlp
    grad_down = down_inv * (scaled - down_normed * jnp.mean(scaled * down_normed, axis=-1, keepdims=True))
    grad_down_wide, _, _ = group_gather(grad_down.astype(BF))

    down_term = lax.dot_general(
        act_low, grad_down_wide, contract_rows, preferred_element_type=F32
    ).astype(BF)
    grad_units, hidden_term = gated_back(after(grad_down_wide, down_term), downs, unit_raw, gate_up, groups)

    def weight_term(left, right):
        return lambda token: lax.dot_general(
            after(left, *(token if isinstance(token, tuple) else (token,))), right, contract_rows, preferred_element_type=F32
        ).astype(BF)

    def owners(term):
        return lax.psum_scatter(term, REST, scatter_dimension=0, tiled=True)

    down_part = owners(down_term)
    moved, unit_term = group_scatter(hidden_term, weight_term(grad_units, hidden_wide))
    grad_hidden = grad_out + moved
    unit_part = owners(after(unit_term, down_part))

    grad_gain_attn = jnp.sum(out_normed * grad_hidden, axis=0)
    scaled = grad_hidden * gain_attn
    grad_out_raw = out_inv * (scaled - out_normed * jnp.mean(scaled * out_normed, axis=-1, keepdims=True))
    grad_out_low = grad_out_raw.astype(BF)
    grad_out_wide, _, _ = group_gather(grad_out_low)

    output_term = lax.dot_general(
        attended_low, grad_out_wide, contract_rows, preferred_element_type=F32
    ).astype(BF)
    grad_out_wide = after(grad_out_wide, output_term)
    output_term = lax.all_to_all(
        output_term.reshape(own_heads, head_dim, width),
        head_axes,
        split_axis=1,
        concat_axis=0,
        tiled=True,
    )

    grad_att = lax.dot_general(grad_out_wide, w_out, contract_last, preferred_element_type=F32).astype(BF)
    scaled, grad_value, dots, gain_term = attend_back(qkv_raw, inverses, gain_heads, tables, own_heads, grad_att)
    scaled = after(scaled, output_term)
    means = group_total(dots) * (1.0 / width)
    grad_qkv, grad_input = finish(qkv_raw, inverses, means, scaled, grad_value, seq_len, own_heads, w_qkv)

    qkv_term = weight_term(x_wide, grad_qkv)((output_term,))
    moved, _ = group_scatter(after(grad_input, qkv_term))
    grad_input = grad_hidden + moved

    qkv_rows = owners(after(qkv_term, unit_part))
    qkv_back, sent = group_exchange(qkv_rows.reshape(PLANE, shard, 3 * own_width), place)
    returned = lax.all_to_all(
        after(grad_input.astype(BF), sent).reshape(micro_count, seq_len, width),
        ALL,
        split_axis=1,
        concat_axis=0,
        tiled=True,
    )
    input_grad = jnp.zeros_like(tokens).at[dealing].set(returned)

    output_part = owners(after(output_term.reshape(groups * shard, width), qkv_rows))

    def heads_in(columns):
        split = columns.reshape(fan, spread, shard, own_heads, head_dim)
        return split.transpose(2, 1, 3, 0, 4).reshape(shard, width).astype(F32)

    query_part = heads_in(qkv_back[:, :, :own_width])
    key_part = heads_in(qkv_back[:, :, own_width : 2 * own_width])
    value_part = heads_in(qkv_back[:, :, 2 * own_width :])

    placed = jnp.zeros((2, spread, own_heads, fan, head_dim), F32)
    own = gain_term.reshape(2, 1, own_heads, 1, head_dim)
    placed = lax.dynamic_update_slice(placed, own, (0, lane, 0, lead, 0)).reshape(2, width)
    gain_terms = jnp.concatenate([placed, jnp.stack([grad_gain_attn, grad_gain_mlp])])
    gain_terms = gain_terms.reshape(4, total, shard).transpose(1, 0, 2)
    gain_part = jnp.sum(
        lax.all_to_all(gain_terms, ALL, split_axis=0, concat_axis=0, tiled=True), axis=0
    )
    return (
        block_out,
        input_grad,
        query_part,
        key_part,
        value_part,
        output_part.astype(F32),
        gain_part[0],
        gain_part[1],
        gain_part[2],
        unit_part[:units].astype(F32).T,
        unit_part[units:].astype(F32).T,
        down_part.astype(F32),
        gain_part[3],
    )


def solution(mesh):
    count = mesh.devices.size
    inner = Mesh(mesh.devices.reshape(LINE, count // (LINE * PLANE), 2, 2, 2), ALL)
    first, second = P(ALL, None), P(None, ALL)
    vector = P(ALL)
    placed = (
        P(None, ALL, None),
        P(),
        P(),
        first,
        first,
        first,
        first,
        vector,
        vector,
        vector,
        second,
        second,
        first,
        vector,
        P(ALL, None, None),
    )
    return jax.shard_map(
        per_device,
        mesh=inner,
        in_specs=placed,
        out_specs=(
            P(ALL, None, None),
            P(None, ALL, None),
            first,
            first,
            first,
            first,
            vector,
            vector,
            vector,
            second,
            second,
            first,
            vector,
        ),
        check_vma=False,
    )
```

```python
import math

import jax
import jax.numpy as jnp
from jax import lax
from jax.experimental import pallas as pl
from jax.experimental.pallas import tpu as pltpu
from jax.sharding import Mesh
from jax.sharding import PartitionSpec as P

HEADS = 16
PLANE = 8
BF = jnp.bfloat16
F32 = jnp.float32

norm_eps = 1e-06
rope_base = 500000.0

ALL = ("z", "m", "y", "x", "c")
GROUP = ("y", "x", "c")
REST = ("z", "m")
LINE = 4
SWAP = [(0, 1), (1, 0)]


def swap(value, axis):
    return lax.ppermute(value, axis, SWAP)


def rotary_tables(length, head_dim):
    half_dim = head_dim // 2
    exponents = jnp.arange(half_dim, dtype=F32) * (2.0 / head_dim)
    frequency = jnp.power(F32(rope_base), -exponents)
    angles = jnp.arange(length, dtype=F32)[:, None] * frequency[None, :]
    return (jnp.cos(angles), jnp.sin(angles))


def wide_tables(length, head_dim):
    cosines, sines = rotary_tables(length, head_dim)
    return (
        jnp.concatenate([cosines, cosines], axis=1),
        jnp.concatenate([-sines, sines], axis=1),
    )


def by_rows(vector, columns):
    return jnp.broadcast_to(vector, (columns, vector.shape[1])).T


def row_sums(values):
    return jnp.sum(values.T, axis=0, keepdims=True)


def matmul(left, right, left_dim=1, right_dim=0):
    return lax.dot_general(left, right, (((left_dim,), (right_dim,)), ((), ())), preferred_element_type=F32)


def turn(values, cosines, sines):
    return values * cosines + pltpu.roll(values, values.shape[1] // 2, 1) * sines


def project_kernel(parts, x_ref, w_ref, raw_ref, squares_ref):
    raw = matmul(x_ref[...], w_ref[...])
    raw_ref[...] = raw
    width = raw.shape[1] // 3
    step = raw.shape[0] // parts
    for part in range(parts):
        rows = slice(part * step, (part + 1) * step)
        for kind in range(2):
            piece = raw[rows, kind * width : (kind + 1) * width]
            squares_ref[kind : kind + 1, rows] = row_sums(piece * piece)


def project(x_wide, weight, seq_len):
    wide, width = x_wide.shape
    out = weight.shape[1]
    block = 2 * seq_len
    return pl.pallas_call(
        lambda *refs: project_kernel(2, *refs),
        grid=(wide // block,),
        in_specs=[pl.BlockSpec((block, width), lambda i: (i, 0)), pl.BlockSpec((width, out), lambda i: (0, 0))],
        out_specs=[pl.BlockSpec((block, out), lambda i: (i, 0)), pl.BlockSpec((2, block), lambda i: (0, i))],
        out_shape=[jax.ShapeDtypeStruct((wide, out), F32), jax.ShapeDtypeStruct((2, wide), F32)],
        cost_estimate=pl.CostEstimate(
            flops=2 * wide * width * out, bytes_accessed=2 * wide * width + 2 * width * out + 4 * wide * out, transcendentals=0
        ),
        name="project",
    )(x_wide, weight)


def soften(scores, causal):
    scores = jnp.where(causal, scores, -1e30)
    exps = jnp.exp(scores - jnp.max(scores, axis=1, keepdims=True))
    return exps * (1.0 / jnp.sum(exps, axis=1, keepdims=True))


def causal_mask(length):
    rows = lax.broadcasted_iota(jnp.int32, (length, length), 0)
    return lax.broadcasted_iota(jnp.int32, (length, length), 1) <= rows


def heads_of(raw_ref, inverses, gain_ref, cosines, sines, rows, head, heads):
    dim = cosines.shape[1]
    out = []
    for kind in range(2):
        at = (kind * heads + head) * dim
        normed = raw_ref[rows, at : at + dim] * inverses[kind]
        gain = gain_ref[kind : kind + 1, head * dim : (head + 1) * dim]
        out += [normed, turn(normed * gain, cosines, sines).astype(BF), gain]
    at = (2 * heads + head) * dim
    return out + [raw_ref[rows, at : at + dim].astype(BF)]


def attend_kernel(heads, parts, scale, raw_ref, inv_ref, gain_ref, cos_ref, sin_ref, out_ref):
    cosines, sines = cos_ref[...], sin_ref[...]
    length, dim = cosines.shape
    causal = causal_mask(length)
    for part in range(parts):
        rows = slice(part * length, (part + 1) * length)
        inverses = [by_rows(inv_ref[kind : kind + 1, rows], dim) for kind in range(2)]
        for head in range(heads):
            _, query, _, _, key, _, value = heads_of(raw_ref, inverses, gain_ref, cosines, sines, rows, head, heads)
            soft = soften(matmul(query, key, 1, 1) * scale, causal)
            out_ref[rows, head * dim : (head + 1) * dim] = matmul(soft.astype(BF), value).astype(BF)


def attend_back_kernel(
    heads, parts, scale, raw_ref, inv_ref, gain_ref, cos_ref, sin_ref, grad_ref, scaled_ref, value_ref, dots_ref, gains_ref
):
    cosines, sines = cos_ref[...], sin_ref[...]
    length, dim = cosines.shape
    causal = causal_mask(length)

    @pl.when(pl.program_id(0) == 0)
    def _():
        gains_ref[...] = jnp.zeros_like(gains_ref)

    for part in range(parts):
        rows = slice(part * length, (part + 1) * length)
        inverses = [by_rows(inv_ref[kind : kind + 1, rows], dim) for kind in range(2)]
        dots = [0.0, 0.0]
        for head in range(heads):
            query_normed, query, query_gain, key_normed, key, key_gain, value = heads_of(
                raw_ref, inverses, gain_ref, cosines, sines, rows, head, heads
            )
            columns = slice(head * dim, (head + 1) * dim)
            soft = soften(matmul(query, key, 1, 1) * scale, causal)
            grad = grad_ref[rows, columns]
            grad_soft = matmul(grad, value, 1, 1)
            delta = jnp.sum(soft * grad_soft, axis=1, keepdims=True)
            grad_scores = (soft * (grad_soft - delta)).astype(BF)
            value_ref[rows, columns] = matmul(soft.astype(BF), grad, 0, 0).astype(BF)
            turned = (matmul(grad_scores, key) * scale, matmul(grad_scores, query, 0, 0) * scale)
            for kind, normed, gain in ((0, query_normed, query_gain), (1, key_normed, key_gain)):
                back = turn(turned[kind], cosines, -sines)
                gains_ref[kind : kind + 1, columns] += jnp.sum(normed * back, axis=0, keepdims=True)
                scaled = back * gain
                scaled_ref[rows, (kind * heads + head) * dim : (kind * heads + head + 1) * dim] = scaled
                dots[kind] = dots[kind] + scaled * normed
        for kind in range(2):
            dots_ref[kind : kind + 1, rows] = row_sums(dots[kind])


def finish_kernel(heads, parts, length, raw_ref, inv_ref, means_ref, scaled_ref, value_ref, weight_ref, out_ref, input_ref):
    width = value_ref.shape[1]
    for part in range(parts):
        rows = slice(part * length, (part + 1) * length)
        for kind in range(2):
            columns = slice(kind * width, (kind + 1) * width)
            inverse = by_rows(inv_ref[kind : kind + 1, rows], width)
            mean = by_rows(means_ref[kind : kind + 1, rows], width)
            normed = raw_ref[rows, columns] * inverse
            out_ref[rows, columns] = (inverse * (scaled_ref[rows, columns] - normed * mean)).astype(BF)
        out_ref[rows, 2 * width :] = value_ref[rows, :]
    input_ref[...] = matmul(out_ref[...], weight_ref[...], 1, 1).astype(BF)


def block_specs(block, heads, dim, length):
    own = heads * dim
    rows = lambda columns: pl.BlockSpec((block, columns), lambda i: (i, 0))
    lanes = pl.BlockSpec((2, block), lambda i: (0, i))
    fixed = lambda shape: pl.BlockSpec(shape, lambda i: (0, 0))
    return own, rows, lanes, [rows(3 * own), lanes, fixed((2, own)), fixed((length, dim)), fixed((length, dim))]


def attend(raw, inverses, gains, tables, heads):
    length, dim = tables[0].shape
    wide = raw.shape[0]
    block = 2 * length
    own, rows, _, specs = block_specs(block, heads, dim, length)
    return pl.pallas_call(
        lambda *refs: attend_kernel(heads, 2, 1.0 / math.sqrt(dim), *refs),
        grid=(wide // block,),
        in_specs=specs,
        out_specs=rows(own),
        out_shape=jax.ShapeDtypeStruct((wide, own), BF),
        cost_estimate=pl.CostEstimate(
            flops=4 * wide * length * own, bytes_accessed=14 * wide * own, transcendentals=wide * length * heads
        ),
        name="attend",
    )(raw, inverses, gains, *tables)


def attend_back(raw, inverses, gains, tables, heads, grad):
    length, dim = tables[0].shape
    wide = raw.shape[0]
    block = 2 * length
    own, rows, lanes, specs = block_specs(block, heads, dim, length)
    return pl.pallas_call(
        lambda *refs: attend_back_kernel(heads, 2, 1.0 / math.sqrt(dim), *refs),
        grid=(wide // block,),
        in_specs=specs + [rows(own)],
        out_specs=[rows(2 * own), rows(own), lanes, pl.BlockSpec((2, own), lambda i: (0, 0))],
        out_shape=[
            jax.ShapeDtypeStruct((wide, 2 * own), F32),
            jax.ShapeDtypeStruct((wide, own), BF),
            jax.ShapeDtypeStruct((2, wide), F32),
            jax.ShapeDtypeStruct((2, own), F32),
        ],
        cost_estimate=pl.CostEstimate(
            flops=10 * wide * length * own, bytes_accessed=26 * wide * own, transcendentals=wide * length * heads
        ),
        name="attend_back",
    )(raw, inverses, gains, *tables, grad)


def finish(raw, inverses, means, scaled, value, length, heads, weight):
    wide, own = value.shape
    block = 2 * length
    rows = lambda columns: pl.BlockSpec((block, columns), lambda i: (i, 0))
    lanes = pl.BlockSpec((2, block), lambda i: (0, i))
    return pl.pallas_call(
        lambda *refs: finish_kernel(heads, 2, length, *refs),
        grid=(wide // block,),
        in_specs=[rows(3 * own), lanes, lanes, rows(2 * own), rows(own), pl.BlockSpec(weight.shape, lambda i: (0, 0))],
        out_specs=[rows(3 * own), rows(weight.shape[0])],
        out_shape=[jax.ShapeDtypeStruct((wide, 3 * own), BF), jax.ShapeDtypeStruct((wide, weight.shape[0]), BF)],
        cost_estimate=pl.CostEstimate(
            flops=2 * wide * weight.size, bytes_accessed=28 * wide * own + 2 * wide * weight.shape[0], transcendentals=0
        ),
        name="finish",
    )(raw, inverses, means, scaled, value, weight)


def after(value, *earlier):
    return lax.optimization_barrier((value,) + earlier)[0]


def group_gather(block, meanwhile=None):
    half = block.shape[0] // 2
    over_x, over_y = swap(block, "x"), swap(block, "y")
    near_x, near_y = over_x[:half], over_y[half:]
    done = None
    if meanwhile is not None:
        done = meanwhile(block)
        near_x, near_y, _ = lax.optimization_barrier((near_x, near_y, done))
    pieces = [block, over_x, over_y, swap(near_x, "y"), swap(near_y, "x")]
    return jnp.concatenate(pieces + [swap(piece, "c") for piece in pieces], axis=0), over_x, done


def group_scatter(partial, meanwhile=None):
    wide = partial.shape[0] // 2
    rows = wide // 4
    half = rows // 2

    def both(i):
        away = swap(partial[wide + i * rows : wide + (i + 1) * rows], "c")
        return partial[i * rows : (i + 1) * rows].astype(F32) + away.astype(F32)

    def move(value, axis):
        return swap(value.astype(BF), axis).astype(F32)

    far, over_x, over_y, own = both(3), both(1), both(2), both(0)
    far_low, far_high = far[:half].astype(BF), far[half:].astype(BF)
    far_x, far_y = swap(far_low, "x"), swap(far_high, "y")
    done = None
    if meanwhile is not None:
        done = meanwhile(far_low)
        far_x, far_y, done = lax.optimization_barrier((far_x, far_y, done))
    over_y = jnp.concatenate([over_y[:half] + far_x.astype(F32), over_y[half:]])
    over_x = jnp.concatenate([over_x[:half], over_x[half:] + far_y.astype(F32)])
    return own + move(over_x, "x") + move(over_y, "y"), done


def gated_kernel(groups, hidden_ref, weight_ref, raw_ref, act_ref):
    raw = matmul(hidden_ref[...], weight_ref[...], 1, 1)
    raw_ref[...] = raw
    step = raw.shape[1] // (2 * groups)
    for i in range(groups):
        gate = raw[:, 2 * i * step : (2 * i + 1) * step]
        up = raw[:, (2 * i + 1) * step : (2 * i + 2) * step]
        act_ref[:, i * step : (i + 1) * step] = (gate * jax.nn.sigmoid(gate) * up).astype(BF)


def gated(hidden, weight, groups):
    wide, width = hidden.shape
    units = weight.shape[0]
    block = 256
    rows = lambda columns: pl.BlockSpec((block, columns), lambda i: (i, 0))
    return pl.pallas_call(
        lambda *refs: gated_kernel(groups, *refs),
        grid=(wide // block,),
        in_specs=[rows(width), pl.BlockSpec((units, width), lambda i: (0, 0))],
        out_specs=[rows(units), rows(units // 2)],
        out_shape=[jax.ShapeDtypeStruct((wide, units), F32), jax.ShapeDtypeStruct((wide, units // 2), BF)],
        cost_estimate=pl.CostEstimate(
            flops=2 * wide * width * units,
            bytes_accessed=2 * wide * width + 2 * units * width + 5 * wide * units,
            transcendentals=wide * units // 2,
        ),
        name="gated",
    )(hidden, weight)


def gated_back_kernel(groups, grad_ref, first_ref, second_ref, raw_ref, weight_ref, units_ref, hidden_ref):
    split = first_ref.shape[1]
    grad_act = matmul(grad_ref[:, :split], first_ref[...], 1, 1) + matmul(grad_ref[:, split:], second_ref[...], 1, 1)
    step = grad_act.shape[1] // groups
    for i in range(groups):
        gate = raw_ref[:, 2 * i * step : (2 * i + 1) * step]
        up = raw_ref[:, (2 * i + 1) * step : (2 * i + 2) * step]
        grad = grad_act[:, i * step : (i + 1) * step]
        sigma = jax.nn.sigmoid(gate)
        units_ref[:, 2 * i * step : (2 * i + 1) * step] = (
            grad * up * sigma * (1.0 + gate * (1.0 - sigma))
        ).astype(BF)
        units_ref[:, (2 * i + 1) * step : (2 * i + 2) * step] = (grad * (gate * sigma)).astype(BF)
    hidden_ref[...] = matmul(units_ref[...], weight_ref[...]).astype(BF)


def gated_back(grad, downs, raw, weight, groups):
    wide, width = grad.shape
    units = weight.shape[0]
    block = 256
    rows = lambda columns: pl.BlockSpec((block, columns), lambda i: (i, 0))
    fixed = lambda array: pl.BlockSpec(array.shape, lambda i: (0, 0))
    return pl.pallas_call(
        lambda *refs: gated_back_kernel(groups, *refs),
        grid=(wide // block,),
        in_specs=[rows(width), fixed(downs[0]), fixed(downs[1]), rows(units), fixed(weight)],
        out_specs=[rows(units), rows(width)],
        out_shape=[jax.ShapeDtypeStruct((wide, units), BF), jax.ShapeDtypeStruct((wide, width), BF)],
        cost_estimate=pl.CostEstimate(
            flops=3 * wide * width * units,
            bytes_accessed=4 * wide * width + 3 * units * width + 6 * wide * units,
            transcendentals=wide * units // 2,
        ),
        name="gated_back",
    )(grad, *downs, raw, weight)


def ring(ahead):
    return [(i, (i + ahead) % LINE) for i in range(LINE)]


def line_gather(block, at):
    out = jnp.zeros((LINE,) + block.shape, block.dtype)
    out = lax.dynamic_update_index_in_dim(out, block, at, 0)
    for ahead in range(1, LINE):
        moved = lax.ppermute(block, "z", ring(ahead))
        out = lax.dynamic_update_index_in_dim(out, moved, (at - ahead) % LINE, 0)
    return out


def group_exchange(blocks, place):
    out = jnp.zeros_like(blocks)
    out = lax.dynamic_update_index_in_dim(out, lax.dynamic_index_in_dim(blocks, place, 0), place, 0)
    for apart in range(1, PLANE):
        block = lax.dynamic_index_in_dim(blocks, place ^ apart, 0)
        moved = lax.ppermute(block, GROUP, [(i, i ^ apart) for i in range(PLANE)])
        if apart == 1:
            token = moved
        out = lax.dynamic_update_index_in_dim(out, moved, place ^ apart, 0)
    return out, token


def group_total(value):
    kinds, wide = value.shape
    split = value.reshape(kinds, 2, 2, 2, wide // PLANE)
    for axis, dim in (("c", 1), ("x", 3), ("y", 2)):
        split = split + jnp.flip(swap(split, axis), dim)
    return split.reshape(kinds, wide)


def per_device(
    tokens,
    lengths,
    dealing,
    w_query,
    w_key,
    w_value,
    w_output,
    query_gain,
    key_gain,
    attn_gain,
    w_gate,
    w_up,
    w_down,
    mlp_gain,
    cotangent,
):
    groups = lax.axis_size(REST)
    total = groups * PLANE
    rank = lax.axis_index(ALL)
    place = lax.axis_index(GROUP)
    at = lax.axis_index("z")
    along = lax.axis_size("m")
    micro_count, seq_len, width = cotangent.shape
    rows = micro_count * seq_len
    wide = rows * PLANE
    shard = width // total
    head_dim = width // HEADS
    own_heads = HEADS // PLANE
    own_width = own_heads * head_dim
    spread = head_dim // shard
    head_axes = GROUP[3 - (spread.bit_length() - 1) :]
    fan = PLANE // spread
    lead, lane = place // spread, place % spread

    tables = wide_tables(seq_len, head_dim)
    positions = jnp.arange(seq_len, dtype=jnp.int32)

    def heads_out(weight):
        split = weight.reshape(shard, spread, own_heads, fan, head_dim)
        return split.transpose(3, 1, 0, 2, 4).reshape(PLANE, shard, own_width)

    outgoing = jnp.take(tokens, dealing, axis=0)
    arrived = lax.all_to_all(outgoing, ALL, split_axis=0, concat_axis=1, tiled=True)
    x_low = arrived.reshape(rows, width)

    w_query, w_key, w_value, outgoing = lax.optimization_barrier((w_query, w_key, w_value, outgoing))
    qkv_out = jnp.concatenate([heads_out(w_query), heads_out(w_key), heads_out(w_value)], axis=2)
    qkv_in = lax.all_to_all(qkv_out, GROUP, split_axis=0, concat_axis=0, tiled=True)

    gains = jnp.stack([query_gain, key_gain, attn_gain, mlp_gain])
    gains = lax.all_to_all(
        jnp.broadcast_to(gains[None], (total, 4, shard)), ALL, split_axis=0, concat_axis=0, tiled=True
    )
    gains = gains.transpose(1, 0, 2).reshape(4, width).astype(F32)
    by_head = gains[:2].reshape(2, spread, own_heads, fan, head_dim)
    by_head = lax.dynamic_index_in_dim(by_head, lane, 1, keepdims=False)
    by_head = lax.dynamic_index_in_dim(by_head, lead, 2, keepdims=False)
    gain_heads = by_head.reshape(2, own_width)
    gain_attn, gain_mlp = gains[2], gains[3]

    out_all = w_output
    if along > 1:
        out_all = lax.all_gather(out_all, "m", axis=0, tiled=True)
    out_all = line_gather(out_all, at).reshape(groups, shard, width)
    qkv_in = after(qkv_in, out_all)
    w_qkv = lax.all_gather(qkv_in, REST, axis=0, tiled=True).reshape(width, 3 * own_width)
    w_out = lax.all_to_all(out_all, head_axes, split_axis=0, concat_axis=1, tiled=True)
    w_out = w_out.reshape(own_width, width)

    units = w_gate.shape[1]
    gate_up = jnp.concatenate([w_gate.T, w_up.T])
    gate_up = lax.all_gather(after(gate_up, qkv_in), REST, axis=0, tiled=True)
    split = width // 2
    downs = [
        lax.all_gather(after(part, qkv_in), REST, axis=0, tiled=True)
        for part in (w_down[:, :split], w_down[:, split:])
    ]

    own_seqs = lax.dynamic_slice_in_dim(dealing, rank * micro_count, micro_count)
    own_lengths = jnp.take(lengths, own_seqs)
    valid_mask = (positions[None, :] < own_lengths[:, None]).astype(F32).reshape(rows, 1)

    x_wide, _, _ = group_gather(x_low)
    qkv_raw, squares = project(x_wide, w_qkv, seq_len)
    inverses = lax.rsqrt(group_total(squares) * (1.0 / width) + norm_eps)
    attended_low = attend(qkv_raw, inverses, gain_heads, tables, own_heads)
    out_raw, _ = group_scatter(jnp.dot(attended_low, w_out, preferred_element_type=F32).astype(BF))
    out_inv = lax.rsqrt(jnp.mean(out_raw * out_raw, axis=-1, keepdims=True) + norm_eps)
    out_normed = out_raw * out_inv
    hidden = x_low.astype(F32) + out_normed * gain_attn

    hidden_wide, _, _ = group_gather(hidden.astype(BF))
    contract_last = (((1,), (1,)), ((), ()))
    contract_rows = (((0,), (0,)), ((), ()))
    unit_raw, act_low = gated(hidden_wide, gate_up, groups)
    down_raws = []
    for part in downs:
        rows_in = after(act_low, *down_raws)
        down_raws.append(group_scatter(jnp.dot(rows_in, part, preferred_element_type=F32).astype(BF))[0])
    down_raw = jnp.concatenate(down_raws, axis=1)
    down_inv = lax.rsqrt(jnp.mean(down_raw * down_raw, axis=-1, keepdims=True) + norm_eps)
    down_normed = down_raw * down_inv
    block_out = (
        (valid_mask * (hidden + down_normed * gain_mlp)).astype(BF).reshape(micro_count, seq_len, width)
    )

    grad_out = valid_mask * cotangent.reshape(rows, width).astype(F32)
    grad_gain_mlp = jnp.sum(down_normed * grad_out, axis=0)
    scaled = grad_out * gain_mlp
    grad_down = down_inv * (scaled - down_normed * jnp.mean(scaled * down_normed, axis=-1, keepdims=True))
    grad_down_wide, _, _ = group_gather(grad_down.astype(BF))

    down_term = lax.dot_general(
        act_low, grad_down_wide, contract_rows, preferred_element_type=F32
    ).astype(BF)
    grad_units, hidden_term = gated_back(after(grad_down_wide, down_term), downs, unit_raw, gate_up, groups)

    def weight_term(left, right):
        return lambda token: lax.dot_general(
            after(left, *(token if isinstance(token, tuple) else (token,))), right, contract_rows, preferred_element_type=F32
        ).astype(BF)

    def owners(term):
        return lax.psum_scatter(term, REST, scatter_dimension=0, tiled=True)

    down_part = owners(down_term)
    moved, unit_term = group_scatter(hidden_term, weight_term(grad_units, hidden_wide))
    grad_hidden = grad_out + moved
    unit_part = owners(after(unit_term, down_part))

    grad_gain_attn = jnp.sum(out_normed * grad_hidden, axis=0)
    scaled = grad_hidden * gain_attn
    grad_out_raw = out_inv * (scaled - out_normed * jnp.mean(scaled * out_normed, axis=-1, keepdims=True))
    grad_out_low = grad_out_raw.astype(BF)
    grad_out_wide, _, _ = group_gather(grad_out_low)

    output_term = lax.dot_general(
        attended_low, grad_out_wide, contract_rows, preferred_element_type=F32
    ).astype(BF)
    grad_out_wide = after(grad_out_wide, output_term)
    output_term = lax.all_to_all(
        output_term.reshape(own_heads, head_dim, width),
        head_axes,
        split_axis=1,
        concat_axis=0,
        tiled=True,
    )

    grad_att = lax.dot_general(grad_out_wide, w_out, contract_last, preferred_element_type=F32).astype(BF)
    scaled, grad_value, dots, gain_term = attend_back(qkv_raw, inverses, gain_heads, tables, own_heads, grad_att)
    scaled = after(scaled, output_term)
    placed = jnp.zeros((2, spread, own_heads, fan, head_dim), F32)
    own = gain_term.reshape(2, 1, own_heads, 1, head_dim)
    placed = lax.dynamic_update_slice(placed, own, (0, lane, 0, lead, 0)).reshape(2, width)
    gain_terms = jnp.concatenate([placed, jnp.stack([grad_gain_attn, grad_gain_mlp])])
    gain_terms = gain_terms.reshape(4, total, shard).transpose(1, 0, 2)
    gain_part = jnp.sum(
        lax.all_to_all(gain_terms, ALL, split_axis=0, concat_axis=0, tiled=True), axis=0
    )
    means = group_total(dots) * (1.0 / width)
    grad_qkv, grad_input = finish(qkv_raw, inverses, means, scaled, grad_value, seq_len, own_heads, w_qkv)

    qkv_term = weight_term(x_wide, grad_qkv)((output_term,))
    moved, _ = group_scatter(after(grad_input, qkv_term, gain_part))
    grad_input = grad_hidden + moved

    qkv_rows = owners(after(qkv_term, unit_part))
    qkv_back, sent = group_exchange(qkv_rows.reshape(PLANE, shard, 3 * own_width), place)
    returned = lax.all_to_all(
        after(grad_input.astype(BF), sent).reshape(micro_count, seq_len, width),
        ALL,
        split_axis=1,
        concat_axis=0,
        tiled=True,
    )
    input_grad = jnp.zeros_like(tokens).at[dealing].set(returned)

    output_part = owners(after(output_term.reshape(groups * shard, width), qkv_rows))

    def heads_in(columns):
        split = columns.reshape(fan, spread, shard, own_heads, head_dim)
        return split.transpose(2, 1, 3, 0, 4).reshape(shard, width).astype(F32)

    query_part = heads_in(qkv_back[:, :, :own_width])
    key_part = heads_in(qkv_back[:, :, own_width : 2 * own_width])
    value_part = heads_in(qkv_back[:, :, 2 * own_width :])

    return (
        block_out,
        input_grad,
        query_part,
        key_part,
        value_part,
        output_part.astype(F32),
        gain_part[0],
        gain_part[1],
        gain_part[2],
        unit_part[:units].astype(F32).T,
        unit_part[units:].astype(F32).T,
        down_part.astype(F32),
        gain_part[3],
    )


def solution(mesh):
    count = mesh.devices.size
    inner = Mesh(mesh.devices.reshape(LINE, count // (LINE * PLANE), 2, 2, 2), ALL)
    first, second = P(ALL, None), P(None, ALL)
    vector = P(ALL)
    placed = (
        P(None, ALL, None),
        P(),
        P(),
        first,
        first,
        first,
        first,
        vector,
        vector,
        vector,
        second,
        second,
        first,
        vector,
        P(ALL, None, None),
    )
    return jax.shard_map(
        per_device,
        mesh=inner,
        in_specs=placed,
        out_specs=(
            P(ALL, None, None),
            P(None, ALL, None),
            first,
            first,
            first,
            first,
            vector,
            vector,
            vector,
            second,
            second,
            first,
            vector,
        ),
        check_vma=False,
    )
```
